256 devices in a mesh: tile: 32 (over z_hi, x, core), energy: 8 (over z_lo, y).
Axes of the slice: x: 4, y: 4, z: 8 (z_hi: 4, z_lo: 2; z = z_hi * 2 + z_lo), core: 2. Of those that a mesh axis runs over, the one named last changes fastest.
Arguments:
- object_tiles: float32 [8, 2, 8192, 256], P('energy', None, 'tile'), may hold values from -4 to 4
- probe_field: float32 [8, 2, 128, 128], P('energy'), may hold values from -4 to 4
- intensity: bfloat16 [8, 32, 8, 128, 128], P('energy', 'tile'), may hold values from 0.019897461 to 2
- row_offsets: int32 [32, 8], P('tile'), may hold values from -64 to 192, as said below
- col_offsets: int32 [32, 8], P('tile'), may hold values from 0 to 128
- tile_counts: int32 [32], P('tile'), may hold values from 3 to 8
- material_spectra: float32 [8, 3], replicated, may hold values from 0.2 to 2
Outputs:
- material_maps: float32 [3, 8192, 256], P(None, 'tile')
- model_object: float32 [8, 2, 8192, 256], P('energy', None, 'tile')
The draws below stay inside these ranges and needn't reach their ends.
Inputs may be any that keep to these rules, and one draw needn't show every extreme that they name: `row_offsets`: in every tile one of slots 0 and 1 starts at -64 and the other at 192.
All inputs are finite; a program needn't handle non-finite values.
Results may differ from the reference program's by a relative error of at most 0.0003.
Values sent between devices are 32-bit elements; how exact they have to be, the bound alone decides.
A program may use at most 64 MiB of HBM per device.

```python
import math
import jax
import jax.numpy as jnp
from jax import lax

TILE = 256
PROBE = 128
P_DEV = 8
SWEEPS = 1
MATERIALS = 3
NN_ITERS = 8
BORDER = 64
TILES = 32
ENERGIES = 8
HEIGHT = 8192


def draw_row_offsets(key, part):
    key_rows = jax.random.fold_in(key, 11)
    key_flip = jax.random.fold_in(key, 12)
    lowest = 0 - BORDER
    highest = TILE - PROBE + BORDER
    rows = jax.random.randint(key_rows, (TILES, P_DEV), lowest, highest + 1, dtype=jnp.int32)
    flips = jax.random.randint(key_flip, (TILES,), 0, 2, dtype=jnp.int32)
    first = jnp.where(flips == 0, lowest, highest).astype(jnp.int32)
    second = jnp.where(flips == 0, highest, lowest).astype(jnp.int32)
    rows = rows.at[:, 0].set(first)
    rows = rows.at[:, 1].set(second)
    return rows


def with_ends(drawn, key, low, high):
    longest = drawn.shape.index(max(drawn.shape))
    spots = []
    for shift in (0, 1):
        where = [jax.random.randint(jax.random.fold_in(key, axis), (), 0, length) for axis, length in enumerate(drawn.shape)]
        where[longest] = (where[longest] + shift) % drawn.shape[longest]
        spots.append(tuple(where))
    return drawn.at[spots[0]].set(low).at[spots[1]].set(high)


def block_scale(stream_key, shape, split, smallest, top_value):
    def one(position, blocks):
        heights = jax.random.uniform(jax.random.fold_in(jax.random.fold_in(stream_key, 6), position), (blocks,), jnp.float32, smallest / len(split), top_value / len(split))
        return jnp.repeat(jnp.exp(heights), shape[position] // blocks).reshape((-1,) + (1,) * (len(shape) - position - 1))

    gain = one(*split[0])
    for cut in split[1:]:
        gain = gain * one(*cut)
    return gain


def bell_draw(stream_key, dims, scale, most, split=(), kind=jnp.bfloat16):
    values = jax.random.normal(stream_key, dims, jnp.float32) * scale
    if len(split) > 0:
        values = block_scale(stream_key, dims, split, -0.22, 0.18) * values
    return jnp.clip(values, min=-most, max=most).astype(kind)


def setup_inputs(seed: int = 0) -> dict:
    key_of = jax.random.split(jax.random.key(seed), 8)
    object_tiles = bell_draw(key_of[0], (ENERGIES, 2, HEIGHT, TILE), 0.7, 4.0, ((0, 8), (2, 32)), jnp.float32)
    probe_field = bell_draw(key_of[1], (ENERGIES, 2, PROBE, PROBE), 0.7, 4.0, ((0, 8),), jnp.float32)
    intensity = jnp.clip(jnp.exp(math.log(2.0) - 4.61031033 * jax.random.uniform(key_of[2], (ENERGIES, TILES, P_DEV, PROBE, PROBE), jnp.float32) ** block_scale(key_of[2], (ENERGIES, TILES, P_DEV, PROBE, PROBE), ((0, 8), (1, 32)), -0.2, 0.2)), 0.019897461, 2.0).astype(jnp.bfloat16)
    row_offsets = draw_row_offsets(jax.random.fold_in(key_of[7], 71), 0)
    col_offsets = with_ends(jax.random.randint(key_of[4], (TILES, P_DEV), 0, TILE - PROBE + 1), jax.random.fold_in(key_of[4], 1), 0, TILE - PROBE).astype(jnp.int32)
    tile_counts = with_ends(jax.random.randint(key_of[5], (TILES,), max(2, P_DEV // 4 + 1), P_DEV + 1), jax.random.fold_in(key_of[5], 1), max(2, P_DEV // 4 + 1), P_DEV).astype(jnp.int32)
    material_spectra = jnp.clip(jnp.exp(jax.random.uniform(key_of[6], (ENERGIES, MATERIALS), jnp.float32, math.log(0.2), math.log(2.0))), 0.2, 2.0)
    return {"object_tiles": object_tiles, "probe_field": probe_field, "intensity": intensity, "row_offsets": row_offsets, "col_offsets": col_offsets, "tile_counts": tile_counts, "material_spectra": material_spectra}


SMOOTH = 0.01
DAMPING = 0.5

def unmix_maps(attenuation, spectra):
    step_size = 1.0 / jnp.sum(spectra * spectra)
    materials = jnp.zeros((spectra.shape[1],) + attenuation.shape[1:], attenuation.dtype)
    for iteration in range(NN_ITERS):
        predicted = lax.optimization_barrier(jnp.sum(spectra[:, :, None, None] * materials[None], axis=1))
        mismatch = predicted - attenuation
        gradient = lax.optimization_barrier(jnp.sum(spectra[:, :, None, None] * mismatch[:, None], axis=0))
        materials = jnp.maximum(materials - step_size * gradient, 0.0)
    return materials

def refine(current, probe_one, samples, row_offsets, col_offsets, tile_counts):
    probe_c = probe_one[0] + 1j * probe_one[1]
    bases = (jnp.arange(TILES, dtype=jnp.int32) * TILE)[:, None]
    starts = (row_offsets + BORDER + bases).astype(jnp.int32).reshape(-1)
    lefts = col_offsets.astype(jnp.int32).reshape(-1)
    live = (jnp.arange(P_DEV, dtype=jnp.int32)[None, :] < tile_counts[:, None]).reshape(-1)
    flat = samples.reshape(-1, PROBE, PROBE)
    power = probe_one[0] * probe_one[0] + probe_one[1] * probe_one[1]
    for sweep_index in range(SWEEPS):
        padded = jnp.pad(current, ((0, 0), (BORDER, BORDER), (0, 0)))

        def step(totals, record):
            numerator, weights = totals
            row_start, col_start, active, sample = record
            anchor = jnp.zeros((), jnp.int32)
            window = lax.dynamic_slice(padded, (anchor, row_start, col_start), (2, PROBE, PROBE))
            exit_wave = probe_c * (window[0] + 1j * window[1])
            spectrum = jnp.fft.fft2(exit_wave, norm='ortho')
            magnitude = jnp.sqrt(spectrum.real ** 2 + spectrum.imag ** 2 + SMOOTH)
            projected = spectrum * (jnp.sqrt(sample.astype(jnp.float32)) / magnitude)
            change = jnp.fft.ifft2(projected, norm='ortho') - exit_wave
            correction = jnp.conj(probe_c) * change
            parts = jnp.stack([correction.real, correction.imag]).astype(numerator.dtype)
            previous = lax.dynamic_slice(numerator, (anchor, row_start, col_start), (2, PROBE, PROBE))
            numerator = lax.dynamic_update_slice(numerator, previous + jnp.where(active, parts, 0.0), (anchor, row_start, col_start))
            older = lax.dynamic_slice(weights, (row_start, col_start), (PROBE, PROBE))
            weights = lax.dynamic_update_slice(weights, older + jnp.where(active, power, 0.0), (row_start, col_start))
            return ((numerator, weights), None)
        init = (jnp.zeros_like(padded), jnp.zeros_like(padded[0]))
        (numerator, weights), _ = lax.scan(step, init, (starts, lefts, live, flat))
        current = current + numerator[:, BORDER:BORDER + HEIGHT] / (weights[BORDER:BORDER + HEIGHT] + DAMPING)
    return current

def reference(object_tiles, probe_field, intensity, row_offsets, col_offsets, tile_counts, material_spectra):
    finals = []
    for energy_index in range(ENERGIES):
        finals.append(refine(object_tiles[energy_index], probe_field[energy_index], intensity[energy_index], row_offsets, col_offsets, tile_counts))
    final = jnp.stack(finals)
    squared = final[:, 0] ** 2 + final[:, 1] ** 2 + SMOOTH
    attenuation = -0.5 * jnp.log(squared)
    materials = unmix_maps(attenuation, material_spectra)
    thickness = lax.optimization_barrier(jnp.sum(material_spectra[:, :, None, None] * materials[None], axis=1))
    scale_out = jnp.exp(-thickness) / jnp.sqrt(squared)
    model_object = final * scale_out[:, None]
    return (materials, model_object)
```

```python
import jax
import jax.numpy as jnp
import ml_dtypes
import numpy as np
from jax import lax
from jax.experimental import pallas as pl
from jax.experimental.pallas import tpu as pltpu
from jax.sharding import PartitionSpec as P

PROBE = 128
NN_ITERS = 8
SMOOTH = 0.01
DAMPING = 0.5
SIDE = 256
DEPTH = 64
SLOTS = 8
PAD = 8
ENERGIES = 8
RING = 4
PIECE = 16
MATERIALS = 3

F32 = jnp.float32
BF16 = jnp.bfloat16
MESH = pl.DeviceIdType.MESH


def dft_tables():
    k = np.arange(PROBE)
    angles = 2.0 * np.pi / PROBE * (np.outer(k, k) % PROBE)
    cos, sin = np.cos(angles) / np.sqrt(PROBE), np.sin(angles) / np.sqrt(PROBE)
    table = np.block([[cos, -sin], [sin, cos]])
    out = []
    for full in (table, table.T):
        high = full.astype(np.float32).astype(ml_dtypes.bfloat16)
        low = (full - high.astype(np.float64)).astype(np.float32).astype(ml_dtypes.bfloat16)
        out += [high, low]
    return np.stack(out)


def halves(x):
    high = x.astype(BF16)
    return high, (x - high.astype(F32)).astype(BF16)


def mul(a, b):
    return jnp.dot(a, b, preferred_element_type=F32)


def right_apply(x, high, low):
    xh, xl = halves(x)
    return mul(xh, high) + mul(xl, high) + mul(xh, low)


def left_apply(high, low, x):
    xh, xl = halves(x)
    return mul(high, xh) + mul(high, xl) + mul(low, xh)


def swap_blocks(x):
    n = PROBE
    top = jnp.concatenate([x[:n, :n], x[n:, :n]], axis=1)
    bottom = jnp.concatenate([x[:n, n:], x[n:, n:]], axis=1)
    return jnp.concatenate([top, bottom], axis=0)


def kernel(
    obj, probe, inten, tables, rows, cols, count, spec,
    maps_out, model_out,
    ext, prb, itn, tab, root, part, pw, wsum, wrecv, num, nrecv, unit, att, gath, maps, model,
    load_sem, halo_send, halo_recv, w_send, w_recv, n_send, n_recv, a_send, a_recv, g_send, g_recv, out_sem,
):
    tile = lax.axis_index("tile")
    me = lax.axis_index("energy")
    tiles = lax.axis_size("tile")
    plane, y = me // RING, lax.rem(me, RING)
    has_up, has_dn = tile > 0, tile < tiles - 1
    up, dn = tile - 1, tile + 1

    def peer(d):
        return lax.rem(me + d, ENERGIES)

    barrier = pltpu.get_barrier_semaphore()

    def greet(where):
        pl.semaphore_signal(barrier, inc=1, device_id=where, device_id_type=MESH)

    @pl.when(has_up)
    def _():
        greet((up, me))

    @pl.when(has_dn)
    def _():
        greet((dn, me))

    for d in range(1, ENERGIES):
        greet((tile, peer(d)))

    loads = [
        pltpu.make_async_copy(probe.at[0], prb, load_sem.at[0]),
        pltpu.make_async_copy(inten.at[0, 0], itn, load_sem.at[1]),
        pltpu.make_async_copy(tables, tab, load_sem.at[2]),
    ] + [
        pltpu.make_async_copy(
            obj.at[0, :, :, pl.ds(h * PROBE, PROBE)], ext.at[:, h, pl.ds(DEPTH, SIDE), :], load_sem.at[3 + h]
        )
        for h in range(2)
    ]
    for load in loads:
        load.start()

    greeted = ENERGIES - 1 + has_up.astype(jnp.int32) + has_dn.astype(jnp.int32)
    pl.semaphore_wait(barrier, greeted)

    def remote(src, dst, send, recv, where):
        return pltpu.make_async_remote_copy(
            src_ref=src, dst_ref=dst, send_sem=send, recv_sem=recv, device_id=where, device_id_type=MESH
        )

    def border_pair(src_up, dst_up, src_dn, dst_dn, send, recv, first):
        return (
            remote(src_up, dst_up, send.at[first], recv.at[first], (up, me)),
            remote(src_dn, dst_dn, send.at[first + 1], recv.at[first + 1], (dn, me)),
        )

    def start_borders(pairs):
        @pl.when(has_up)
        def _():
            for to_up, _ in pairs:
                to_up.start()

        @pl.when(has_dn)
        def _():
            for _, to_dn in pairs:
                to_dn.start()

    def wait_borders(pairs):
        @pl.when(has_dn)
        def _():
            for to_up, _ in pairs:
                to_up.wait_recv()

        @pl.when(has_up)
        def _():
            for _, to_dn in pairs:
                to_dn.wait_recv()

    def sent_borders(pairs):
        @pl.when(has_up)
        def _():
            for to_up, _ in pairs:
                to_up.wait_send()

        @pl.when(has_dn)
        def _():
            for _, to_dn in pairs:
                to_dn.wait_send()

    last = SIDE + DEPTH
    halo = [
        border_pair(
            obj.at[0, :, pl.ds(0, DEPTH), pl.ds(h * PROBE, PROBE)],
            ext.at[:, h, pl.ds(last, DEPTH), :],
            obj.at[0, :, pl.ds(SIDE - DEPTH, DEPTH), pl.ds(h * PROBE, PROBE)],
            ext.at[:, h, pl.ds(0, DEPTH), :],
            halo_send, halo_recv, 2 * h,
        )
        for h in range(2)
    ]
    start_borders(halo)

    @pl.when(jnp.logical_not(has_up))
    def _():
        ext[:, :, 0:DEPTH, :] = jnp.zeros((2, 2, DEPTH, PROBE), F32)
        wrecv[0] = jnp.zeros((2, DEPTH, PROBE), F32)
        nrecv[0] = jnp.zeros((2, 2, DEPTH, PROBE), F32)

    @pl.when(jnp.logical_not(has_dn))
    def _():
        ext[:, :, last:, :] = jnp.zeros((2, 2, DEPTH, PROBE), F32)
        wrecv[1] = jnp.zeros((2, DEPTH, PROBE), F32)
        nrecv[1] = jnp.zeros((2, 2, DEPTH, PROBE), F32)

    part[:, :, 0:PAD, :] = jnp.zeros((SLOTS, 2, PAD, PROBE), F32)
    part[:, :, PAD + PROBE :, :] = jnp.zeros((SLOTS, 2, PAD, PROBE), F32)
    pw[:, 0:PAD, :] = jnp.zeros((SLOTS, PAD, PROBE), F32)
    pw[:, PAD + PROBE :, :] = jnp.zeros((SLOTS, PAD, PROBE), F32)

    live = count[0]
    lefts = [cols[0, j] for j in range(SLOTS)]
    tops = [jnp.where(j < live, rows[0, j] + DEPTH, 8 * SIDE) for j in range(SLOTS)]
    lane8 = lax.broadcasted_iota(jnp.int32, (8, PROBE), 1)

    loads[0].wait()
    probe_re, probe_im = prb[0], prb[1]
    power = probe_re * probe_re + probe_im * probe_im
    for j in range(SLOTS):
        pw[j, PAD : PAD + PROBE, :] = pltpu.roll(power, lax.rem(lefts[j], PROBE), 1)

    def placed(read, group, terms):
        left = [jnp.zeros((8, PROBE), F32) for _ in range(terms)]
        right = [jnp.zeros((8, PROBE), F32) for _ in range(terms)]
        for j in range(SLOTS):
            at = jnp.clip(8 * group - tops[j], -PAD, PROBE) + PAD
            inside = lane8 >= lefts[j]
            for c in range(terms):
                value = read(j, c, pl.ds(at, 8))
                left[c] = left[c] + jnp.where(inside, value, 0.0)
                right[c] = right[c] + jnp.where(inside, 0.0, value)
        return left, right

    def place_weights(group, carry):
        left, right = placed(lambda j, c, where: pw[j, where, :], group, 1)
        at = pl.ds(pl.multiple_of(8 * group, 8), 8)
        wsum[0, at, :] = left[0]
        wsum[1, at, :] = right[0]
        return carry

    edge = DEPTH // 8
    whole = (SIDE + 2 * DEPTH) // 8
    lax.fori_loop(0, edge, place_weights, 0)
    lax.fori_loop(whole - edge, whole, place_weights, 0)
    weights = [
        border_pair(
            wsum.at[:, pl.ds(0, DEPTH), :], wrecv.at[1],
            wsum.at[:, pl.ds(last, DEPTH), :], wrecv.at[0],
            w_send, w_recv, 0,
        )
    ]
    start_borders(weights)
    lax.fori_loop(edge, whole - edge, place_weights, 0)

    loads[1].wait()

    def take_roots(pair, carry):
        for s in range(2):
            root[pair, :, s * PROBE : (s + 1) * PROBE] = jnp.sqrt(itn[2 * pair + s].astype(F32))
        return carry

    lax.fori_loop(0, SLOTS // 2, take_roots, 0)

    def coef(e, k):
        return spec[e, k]

    gram = [[None] * MATERIALS for _ in range(MATERIALS)]
    for k in range(MATERIALS):
        for l in range(k, MATERIALS):
            total = coef(0, k) * coef(0, l)
            for e in range(1, ENERGIES):
                total = total + coef(e, k) * coef(e, l)
            gram[k][l] = gram[l][k] = total
    squares = gram[0][0] + gram[1][1] + gram[2][2]

    for load in loads[2:]:
        load.wait()
    wait_borders(halo)

    lane = lax.broadcasted_iota(jnp.int32, (PROBE, PROBE), 1)

    def project(pair, carry):
        exits = []
        for s in range(2):
            j = 2 * pair + s
            top, left = rows[0, j] + DEPTH, cols[0, j]
            turn = lax.rem(PROBE - left, PROBE)
            first = lane < PROBE - left
            view = [
                jnp.where(
                    first,
                    pltpu.roll(ext[c, 0, pl.ds(top, PROBE), :], turn, 1),
                    pltpu.roll(ext[c, 1, pl.ds(top, PROBE), :], turn, 1),
                )
                for c in range(2)
            ]
            pr, pi = prb[0], prb[1]
            exits.append(jnp.concatenate([pr * view[0] - pi * view[1], pr * view[1] + pi * view[0]], axis=1))
        exit_wave = jnp.concatenate(exits, axis=0)
        t_high, t_low, u_high, u_low = tab[0], tab[1], tab[2], tab[3]
        half = swap_blocks(right_apply(exit_wave, t_high, t_low))
        spectrum = left_apply(u_high, u_low, half)
        sr, si = spectrum[:PROBE], spectrum[PROBE:]
        factor = root[pair] * lax.rsqrt(sr * sr + si * si + SMOOTH)
        half = swap_blocks(left_apply(t_high, t_low, jnp.concatenate([sr * factor, si * factor], axis=0)))
        change = right_apply(half, u_high, u_low) - exit_wave
        for s in range(2):
            j = 2 * pair + s
            cr = change[s * PROBE : (s + 1) * PROBE, :PROBE]
            ci = change[s * PROBE : (s + 1) * PROBE, PROBE:]
            pr, pi = prb[0], prb[1]
            turn = lax.rem(cols[0, j], PROBE)
            part[j, 0, PAD : PAD + PROBE, :] = pltpu.roll(pr * cr + pi * ci, turn, 1)
            part[j, 1, PAD : PAD + PROBE, :] = pltpu.roll(pr * ci - pi * cr, turn, 1)
        return carry

    lax.fori_loop(0, SLOTS // 2, project, 0)

    def numerators(group):
        return placed(lambda j, c, where: part[j, c, where, :], group, 2)

    def place_parts(group, carry):
        left, right = numerators(group)
        at = pl.ds(pl.multiple_of(8 * group, 8), 8)
        for c in range(2):
            num[c, 0, at, :] = left[c]
            num[c, 1, at, :] = right[c]
        return carry

    lax.fori_loop(0, edge, place_parts, 0)
    lax.fori_loop(whole - edge, whole, place_parts, 0)
    borders = [
        border_pair(
            num.at[:, :, pl.ds(0, DEPTH), :], nrecv.at[1],
            num.at[:, :, pl.ds(last, DEPTH), :], nrecv.at[0],
            n_send, n_recv, 0,
        )
    ]
    start_borders(borders)

    def renew(group, h, numerator, weight):
        at = pl.ds(pl.multiple_of(8 * group, 8), 8)
        own = pl.ds(pl.multiple_of(8 * group - DEPTH, 8), 8)
        inverse = 1.0 / (weight + DAMPING)
        new = [ext[c, h, at, :] + numerator[c] * inverse for c in range(2)]
        squared = new[0] * new[0] + new[1] * new[1] + SMOOTH
        scale = lax.rsqrt(squared)
        for c in range(2):
            unit[c, own, h * PROBE : (h + 1) * PROBE] = new[c] * scale
        att[own, h * PROBE : (h + 1) * PROBE] = -0.5 * jnp.log(squared)

    def inner_rows(group, carry):
        at = pl.ds(pl.multiple_of(8 * group, 8), 8)
        for h, sums in enumerate(numerators(group)):
            renew(group, h, sums, wsum[h, at, :])
        return carry

    def first_row(f, p):
        fp, fy = f // RING, lax.rem(f, RING)
        start = DEPTH + DEPTH * fp + PIECE * fy if p == 0 else (SIDE - DEPTH) * fp + PIECE * fy
        return pl.multiple_of(start, PIECE)

    def regroup(p):
        return [
            remote(
                att.at[pl.ds(first_row(peer(d), p), PIECE), :], gath.at[p, me],
                a_send.at[p, d - 1], a_recv.at[p, d - 1], (tile, peer(d)),
            )
            for d in range(1, ENERGIES)
        ]

    def send_pixels(p):
        copies = regroup(p)
        for copy in copies:
            copy.start()
        gath[p, me] = att[pl.ds(first_row(me, p), PIECE), :]
        return copies

    lax.fori_loop(2 * edge, whole - 2 * edge, inner_rows, 0)
    to_energies = [send_pixels(0), None]

    lax.fori_loop(edge, 2 * edge, place_parts, 0)
    lax.fori_loop(whole - 2 * edge, whole - edge, place_parts, 0)

    yp = (tile, plane * RING + lax.rem(y + 1, RING))
    ym = (tile, plane * RING + lax.rem(y + RING - 1, RING))
    zz = (tile, (1 - plane) * RING + y)
    far = plane * RING + lax.rem(y + 2, RING)

    def hop(p, route, owner, start, size, where):
        at = pl.ds(pl.multiple_of(first_row(owner, p) + start, 8), size)
        return remote(maps.at[:, at, :], maps.at[:, at, :], g_send.at[p, route], g_recv.at[p, route], where)

    def hops(p):
        return [
            hop(p, 0, me, 0, PIECE, zz),
            hop(p, 1, me, 0, PIECE, yp),
            hop(p, 2, me, 0, PIECE, ym),
            hop(p, 3, zz[1], 0, PIECE, yp),
            hop(p, 4, zz[1], 0, PIECE, ym),
            hop(p, 5, ym[1], 0, PIECE // 2, yp),
            hop(p, 6, yp[1], PIECE // 2, PIECE // 2, ym),
            hop(p, 7, far, 0, PIECE, zz),
        ]

    ways = [hops(0), hops(1)]

    def decompose(p):
        for copy in to_energies[p]:
            copy.wait_recv()
        step = 1.0 / jnp.full((PIECE, SIDE), squares, F32)
        pulls = []
        for k in range(MATERIALS):
            total = coef(0, k) * gath[p, 0]
            for e in range(1, ENERGIES):
                total = total + coef(e, k) * gath[p, e]
            pulls.append(total)
        levels = [jnp.maximum(step * pull, 0.0) for pull in pulls]
        for _ in range(NN_ITERS - 1):
            levels = [
                jnp.maximum(
                    levels[k]
                    - step
                    * (gram[k][0] * levels[0] + gram[k][1] * levels[1] + gram[k][2] * levels[2] - pulls[k]),
                    0.0,
                )
                for k in range(MATERIALS)
            ]
        for k in range(MATERIALS):
            maps[k, pl.ds(first_row(me, p), PIECE), :] = levels[k]
        for way in ways[p][:3]:
            way.start()

    own_spec = [spec[me, k] for k in range(MATERIALS)]
    finished = []

    def finish(owner, p):
        at = pl.ds(first_row(owner, p), PIECE)
        thickness = own_spec[0] * maps[0, at, :] + own_spec[1] * maps[1, at, :] + own_spec[2] * maps[2, at, :]
        fade = jnp.exp(-thickness)
        for c in range(2):
            model[c, at, :] = unit[c, at, :] * fade
        index = 2 * len(finished)
        copies = (
            pltpu.make_async_copy(maps.at[:, at, :], maps_out.at[:, at, :], out_sem.at[index]),
            pltpu.make_async_copy(model.at[:, at, :], model_out.at[0, :, at, :], out_sem.at[index + 1]),
        )
        for copy in copies:
            copy.start()
        finished.append(copies)

    decompose(0)

    wait_borders(weights)
    wait_borders(borders)

    def outer_rows(group, carry):
        for side, base in ((0, edge), (1, whole - 2 * edge)):
            row = pl.ds(pl.multiple_of(8 * group, 8), 8)
            at = pl.ds(pl.multiple_of(8 * (group + base), 8), 8)
            for h in range(2):
                sums = [num[c, h, at, :] + nrecv[side, c, h, row, :] for c in range(2)]
                renew(group + base, h, sums, wsum[h, at, :] + wrecv[side, h, row, :])
        return carry

    lax.fori_loop(0, edge, outer_rows, 0)
    to_energies[1] = send_pixels(1)

    def relay_first(p):
        ways[p][0].wait_recv()
        ways[p][3].start()
        ways[p][4].start()
        ways[p][1].wait_recv()
        ways[p][5].start()
        ways[p][2].wait_recv()
        ways[p][6].start()

    def relay_far(p):
        ways[p][5].wait_recv()
        ways[p][6].wait_recv()
        ways[p][7].start()

    relay_first(0)
    finish(me, 0)
    decompose(1)
    finish(zz[1], 0)
    finish(ym[1], 0)
    finish(yp[1], 0)
    relay_far(0)
    finish(far, 0)
    relay_first(1)
    finish(me, 1)
    finish(zz[1], 1)
    finish(ym[1], 1)
    finish(yp[1], 1)
    relay_far(1)
    finish(far, 1)
    for p in range(2):
        for route, owner in ((3, (1 - plane) * RING + lax.rem(y + RING - 1, RING)), (4, (1 - plane) * RING + lax.rem(y + 1, RING)), (7, (1 - plane) * RING + lax.rem(y + 2, RING))):
            ways[p][route].wait_recv()
            finish(owner, p)

    sent_borders(halo + weights + borders)
    for p in range(2):
        for copy in to_energies[p] + ways[p]:
            copy.wait_send()
    for copies in finished:
        for copy in copies:
            copy.wait()


def body(object_tiles, probe_field, intensity, row_offsets, col_offsets, tile_counts, material_spectra):
    tables = jnp.asarray(dft_tables())
    anywhere = pl.BlockSpec(memory_space=pl.ANY)
    scalars = pl.BlockSpec(memory_space=pltpu.SMEM)
    dma = pltpu.SemaphoreType.DMA
    maps, model = pl.pallas_call(
        kernel,
        out_shape=(
            jax.ShapeDtypeStruct((MATERIALS, SIDE, SIDE), F32),
            jax.ShapeDtypeStruct((1, 2, SIDE, SIDE), F32),
        ),
        in_specs=[anywhere] * 4 + [scalars] * 4,
        out_specs=(anywhere, anywhere),
        scratch_shapes=[
            pltpu.VMEM((2, 2, SIDE + 2 * DEPTH, PROBE), F32),
            pltpu.VMEM((2, PROBE, PROBE), F32),
            pltpu.VMEM((SLOTS, PROBE, PROBE), BF16),
            pltpu.VMEM((4, SIDE, SIDE), BF16),
            pltpu.VMEM((SLOTS // 2, PROBE, SIDE), F32),
            pltpu.VMEM((SLOTS, 2, PROBE + 2 * PAD, PROBE), F32),
            pltpu.VMEM((SLOTS, PROBE + 2 * PAD, PROBE), F32),
            pltpu.VMEM((2, SIDE + 2 * DEPTH, PROBE), F32),
            pltpu.VMEM((2, 2, DEPTH, PROBE), F32),
            pltpu.VMEM((2, 2, SIDE + 2 * DEPTH, PROBE), F32),
            pltpu.VMEM((2, 2, 2, DEPTH, PROBE), F32),
            pltpu.VMEM((2, SIDE, SIDE), F32),
            pltpu.VMEM((SIDE, SIDE), F32),
            pltpu.VMEM((2, ENERGIES, PIECE, SIDE), F32),
            pltpu.VMEM((MATERIALS, SIDE, SIDE), F32),
            pltpu.VMEM((2, SIDE, SIDE), F32),
            dma((5,)),
            dma((4,)), dma((4,)),
            dma((2,)), dma((2,)),
            dma((2,)), dma((2,)),
            dma((2, ENERGIES - 1)), dma((2, ENERGIES - 1)),
            dma((2, 8)), dma((2, 8)),
            dma((4 * ENERGIES,)),
        ],
        compiler_params=pltpu.CompilerParams(collective_id=0, has_side_effects=True),
        name="refine",
    )(object_tiles, probe_field, intensity, tables, row_offsets, col_offsets, tile_counts, material_spectra)
    return (maps, model)


def solution(mesh):
    placed = (
        P("energy", None, "tile", None),
        P("energy", None, None, None),
        P("energy", "tile", None, None, None),
        P("tile", None),
        P("tile", None),
        P("tile"),
        P(),
    )
    return jax.shard_map(
        body,
        mesh=mesh,
        in_specs=placed,
        out_specs=(P(None, "tile", None), P("energy", None, "tile", None)),
        check_vma=False,
    )
```

```python
import jax
import jax.numpy as jnp
import ml_dtypes
import numpy as np
from jax import lax
from jax.experimental import pallas as pl
from jax.experimental.pallas import tpu as pltpu
from jax.sharding import PartitionSpec as P

PROBE = 128
NN_ITERS = 8
SMOOTH = 0.01
DAMPING = 0.5
SIDE = 256
DEPTH = 64
SLOTS = 8
PAD = 8
ENERGIES = 8
RING = 4
PIECE = 16
MATERIALS = 3
UNROLL = 4

F32 = jnp.float32
BF16 = jnp.bfloat16
MESH = pl.DeviceIdType.MESH


def dft_tables():
    k = np.arange(PROBE)
    angles = 2.0 * np.pi / PROBE * (np.outer(k, k) % PROBE)
    cos, sin = np.cos(angles) / np.sqrt(PROBE), np.sin(angles) / np.sqrt(PROBE)
    table = np.block([[cos, -sin], [sin, cos]])
    out = []
    for full in (table, table.T):
        high = full.astype(np.float32).astype(ml_dtypes.bfloat16)
        low = (full - high.astype(np.float64)).astype(np.float32).astype(ml_dtypes.bfloat16)
        out += [high, low]
    return np.stack(out)


def halves(x):
    high = x.astype(BF16)
    return high, (x - high.astype(F32)).astype(BF16)


def mul(a, b):
    return jnp.dot(a, b, preferred_element_type=F32)


def right_apply(x, high, low):
    xh, xl = halves(x)
    return mul(xh, high) + mul(xl, high) + mul(xh, low)


def left_apply(high, low, x):
    xh, xl = halves(x)
    return mul(high, xh) + mul(high, xl) + mul(low, xh)


def swap_blocks(x):
    n = PROBE
    top = jnp.concatenate([x[:n, :n], x[n:, :n]], axis=1)
    bottom = jnp.concatenate([x[:n, n:], x[n:, n:]], axis=1)
    return jnp.concatenate([top, bottom], axis=0)


def kernel(
    obj, probe, inten, tables, rows_in, cols_in, count, spec_in,
    maps, model,
    ext, prb, itn, tab, root, part, pw, wsum, wrecv, num, nrecv, unit, att, gath, rows, cols, spec,
    load_sem, halo_send, halo_recv, w_send, w_recv, n_send, n_recv, a_send, a_recv, g_send, g_recv,
):
    tile = lax.axis_index("tile")
    me = lax.axis_index("energy")
    tiles = lax.axis_size("tile")
    plane, y = me // RING, lax.rem(me, RING)
    has_up, has_dn = tile > 0, tile < tiles - 1
    up, dn = tile - 1, tile + 1

    def peer(d):
        return lax.rem(me + d, ENERGIES)

    barrier = pltpu.get_barrier_semaphore()

    def greet(where):
        pl.semaphore_signal(barrier, inc=1, device_id=where, device_id_type=MESH)

    @pl.when(has_up)
    def _():
        greet((up, me))

    @pl.when(has_dn)
    def _():
        greet((dn, me))

    for d in range(1, ENERGIES):
        greet((tile, peer(d)))

    loads = [
        pltpu.make_async_copy(probe.at[0], prb, load_sem.at[0]),
        pltpu.make_async_copy(inten.at[0, 0], itn, load_sem.at[1]),
        pltpu.make_async_copy(tables, tab, load_sem.at[2]),
    ] + [
        pltpu.make_async_copy(
            obj.at[0, :, :, pl.ds(h * PROBE, PROBE)], ext.at[:, h, pl.ds(DEPTH, SIDE), :], load_sem.at[3 + h]
        )
        for h in range(2)
    ]
    scalars = [
        pltpu.make_async_copy(rows_in, rows, load_sem.at[5]),
        pltpu.make_async_copy(cols_in, cols, load_sem.at[6]),
        pltpu.make_async_copy(spec_in, spec, load_sem.at[7]),
    ]
    for load in scalars + loads:
        load.start()

    greeted = ENERGIES - 1 + has_up.astype(jnp.int32) + has_dn.astype(jnp.int32)
    pl.semaphore_wait(barrier, greeted)

    def remote(src, dst, send, recv, where):
        return pltpu.make_async_remote_copy(
            src_ref=src, dst_ref=dst, send_sem=send, recv_sem=recv, device_id=where, device_id_type=MESH
        )

    def border_pair(src_up, dst_up, src_dn, dst_dn, send, recv, first):
        return (
            remote(src_up, dst_up, send.at[first], recv.at[first], (up, me)),
            remote(src_dn, dst_dn, send.at[first + 1], recv.at[first + 1], (dn, me)),
        )

    def start_borders(pairs):
        @pl.when(has_up)
        def _():
            for to_up, _ in pairs:
                to_up.start()

        @pl.when(has_dn)
        def _():
            for _, to_dn in pairs:
                to_dn.start()

    def wait_borders(pairs):
        @pl.when(has_dn)
        def _():
            for to_up, _ in pairs:
                to_up.wait_recv()

        @pl.when(has_up)
        def _():
            for _, to_dn in pairs:
                to_dn.wait_recv()

    def sent_borders(pairs):
        @pl.when(has_up)
        def _():
            for to_up, _ in pairs:
                to_up.wait_send()

        @pl.when(has_dn)
        def _():
            for _, to_dn in pairs:
                to_dn.wait_send()

    last = SIDE + DEPTH
    halo = [
        border_pair(
            obj.at[0, :, pl.ds(0, DEPTH), pl.ds(h * PROBE, PROBE)],
            ext.at[:, h, pl.ds(last, DEPTH), :],
            obj.at[0, :, pl.ds(SIDE - DEPTH, DEPTH), pl.ds(h * PROBE, PROBE)],
            ext.at[:, h, pl.ds(0, DEPTH), :],
            halo_send, halo_recv, 2 * h,
        )
        for h in range(2)
    ]
    start_borders(halo)

    @pl.when(jnp.logical_not(has_up))
    def _():
        ext[:, :, 0:DEPTH, :] = jnp.zeros((2, 2, DEPTH, PROBE), F32)
        wrecv[0] = jnp.zeros((2, DEPTH, PROBE), F32)
        nrecv[0] = jnp.zeros((2, 2, DEPTH, PROBE), F32)

    @pl.when(jnp.logical_not(has_dn))
    def _():
        ext[:, :, last:, :] = jnp.zeros((2, 2, DEPTH, PROBE), F32)
        wrecv[1] = jnp.zeros((2, DEPTH, PROBE), F32)
        nrecv[1] = jnp.zeros((2, 2, DEPTH, PROBE), F32)

    part[:, :, 0:PAD, :] = jnp.zeros((SLOTS, 2, PAD, PROBE), F32)
    part[:, :, PAD + PROBE :, :] = jnp.zeros((SLOTS, 2, PAD, PROBE), F32)
    pw[:, 0:PAD, :] = jnp.zeros((SLOTS, PAD, PROBE), F32)
    pw[:, PAD + PROBE :, :] = jnp.zeros((SLOTS, PAD, PROBE), F32)

    for load in scalars:
        load.wait()
    live = count[0]
    lefts = [cols[0, j] for j in range(SLOTS)]
    tops = [jnp.where(j < live, rows[0, j] + DEPTH, 8 * SIDE) for j in range(SLOTS)]
    lane8 = lax.broadcasted_iota(jnp.int32, (8, PROBE), 1)

    loads[0].wait()
    probe_re, probe_im = prb[0], prb[1]
    power = probe_re * probe_re + probe_im * probe_im
    for j in range(SLOTS):
        pw[j, PAD : PAD + PROBE, :] = pltpu.roll(power, lax.rem(lefts[j], PROBE), 1)

    def placed(read, group, terms):
        left = [jnp.zeros((8, PROBE), F32) for _ in range(terms)]
        right = [jnp.zeros((8, PROBE), F32) for _ in range(terms)]
        for j in range(SLOTS):
            at = jnp.clip(8 * group - tops[j], -PAD, PROBE) + PAD
            inside = lane8 >= lefts[j]
            for c in range(terms):
                value = read(j, c, pl.ds(at, 8))
                left[c] = left[c] + jnp.where(inside, value, 0.0)
                right[c] = right[c] + jnp.where(inside, 0.0, value)
        return left, right

    def place_weights(group, carry):
        left, right = placed(lambda j, c, where: pw[j, where, :], group, 1)
        at = pl.ds(pl.multiple_of(8 * group, 8), 8)
        wsum[0, at, :] = left[0]
        wsum[1, at, :] = right[0]
        return carry

    edge = DEPTH // 8
    whole = (SIDE + 2 * DEPTH) // 8
    lax.fori_loop(0, edge, place_weights, 0)
    lax.fori_loop(whole - edge, whole, place_weights, 0)
    weights = [
        border_pair(
            wsum.at[:, pl.ds(0, DEPTH), :], wrecv.at[1],
            wsum.at[:, pl.ds(last, DEPTH), :], wrecv.at[0],
            w_send, w_recv, 0,
        )
    ]
    start_borders(weights)
    lax.fori_loop(edge, whole - edge, place_weights, 0)

    loads[1].wait()

    def take_roots(pair, carry):
        for s in range(2):
            root[pair, :, s * PROBE : (s + 1) * PROBE] = jnp.sqrt(itn[2 * pair + s].astype(F32))
        return carry

    lax.fori_loop(0, SLOTS // 2, take_roots, 0)

    def coef(e, k):
        return spec[k, e]

    gram = [[None] * MATERIALS for _ in range(MATERIALS)]
    for k in range(MATERIALS):
        for l in range(k, MATERIALS):
            total = coef(0, k) * coef(0, l)
            for e in range(1, ENERGIES):
                total = total + coef(e, k) * coef(e, l)
            gram[k][l] = gram[l][k] = total
    squares = gram[0][0] + gram[1][1] + gram[2][2]

    for load in loads[2:]:
        load.wait()
    wait_borders(halo)

    lane = lax.broadcasted_iota(jnp.int32, (PROBE, PROBE), 1)

    def project(pair, carry):
        exits = []
        for s in range(2):
            j = 2 * pair + s
            top, left = rows[0, j] + DEPTH, cols[0, j]
            turn = lax.rem(PROBE - left, PROBE)
            first = lane < PROBE - left
            view = [
                jnp.where(
                    first,
                    pltpu.roll(ext[c, 0, pl.ds(top, PROBE), :], turn, 1),
                    pltpu.roll(ext[c, 1, pl.ds(top, PROBE), :], turn, 1),
                )
                for c in range(2)
            ]
            pr, pi = prb[0], prb[1]
            exits.append(jnp.concatenate([pr * view[0] - pi * view[1], pr * view[1] + pi * view[0]], axis=1))
        exit_wave = jnp.concatenate(exits, axis=0)
        t_high, t_low, u_high, u_low = tab[0], tab[1], tab[2], tab[3]
        half = swap_blocks(right_apply(exit_wave, t_high, t_low))
        spectrum = left_apply(u_high, u_low, half)
        sr, si = spectrum[:PROBE], spectrum[PROBE:]
        factor = root[pair] * lax.rsqrt(sr * sr + si * si + SMOOTH)
        half = swap_blocks(left_apply(t_high, t_low, jnp.concatenate([sr * factor, si * factor], axis=0)))
        change = right_apply(half, u_high, u_low) - exit_wave
        for s in range(2):
            j = 2 * pair + s
            cr = change[s * PROBE : (s + 1) * PROBE, :PROBE]
            ci = change[s * PROBE : (s + 1) * PROBE, PROBE:]
            pr, pi = prb[0], prb[1]
            turn = lax.rem(cols[0, j], PROBE)
            part[j, 0, PAD : PAD + PROBE, :] = pltpu.roll(pr * cr + pi * ci, turn, 1)
            part[j, 1, PAD : PAD + PROBE, :] = pltpu.roll(pr * ci - pi * cr, turn, 1)
        return carry

    lax.fori_loop(0, SLOTS // 2, project, 0, unroll=UNROLL)

    def numerators(group):
        return placed(lambda j, c, where: part[j, c, where, :], group, 2)

    def place_parts(group, carry):
        left, right = numerators(group)
        at = pl.ds(pl.multiple_of(8 * group, 8), 8)
        for c in range(2):
            num[c, 0, at, :] = left[c]
            num[c, 1, at, :] = right[c]
        return carry

    lax.fori_loop(0, edge, place_parts, 0)
    lax.fori_loop(whole - edge, whole, place_parts, 0)
    borders = [
        border_pair(
            num.at[:, :, pl.ds(0, DEPTH), :], nrecv.at[1],
            num.at[:, :, pl.ds(last, DEPTH), :], nrecv.at[0],
            n_send, n_recv, 0,
        )
    ]
    start_borders(borders)

    def renew(group, h, numerator, weight):
        at = pl.ds(pl.multiple_of(8 * group, 8), 8)
        own = pl.ds(pl.multiple_of(8 * group - DEPTH, 8), 8)
        inverse = 1.0 / (weight + DAMPING)
        new = [ext[c, h, at, :] + numerator[c] * inverse for c in range(2)]
        squared = new[0] * new[0] + new[1] * new[1] + SMOOTH
        scale = lax.rsqrt(squared)
        for c in range(2):
            unit[c, own, h * PROBE : (h + 1) * PROBE] = new[c] * scale
        att[own, h * PROBE : (h + 1) * PROBE] = -0.5 * jnp.log(squared)

    def inner_rows(group, carry):
        at = pl.ds(pl.multiple_of(8 * group, 8), 8)
        for h, sums in enumerate(numerators(group)):
            renew(group, h, sums, wsum[h, at, :])
        return carry

    def first_row(f, p):
        fp, fy = f // RING, lax.rem(f, RING)
        start = DEPTH + DEPTH * fp + PIECE * fy if p == 0 else (SIDE - DEPTH) * fp + PIECE * fy
        return pl.multiple_of(start, PIECE)

    def regroup(p):
        return [
            remote(
                att.at[pl.ds(first_row(peer(d), p), PIECE), :], gath.at[p, me],
                a_send.at[p, d - 1], a_recv.at[p, d - 1], (tile, peer(d)),
            )
            for d in range(1, ENERGIES)
        ]

    def send_pixels(p):
        copies = regroup(p)
        for copy in copies:
            copy.start()
        gath[p, me] = att[pl.ds(first_row(me, p), PIECE), :]
        return copies

    lax.fori_loop(2 * edge, whole - 2 * edge, inner_rows, 0)
    to_energies = [send_pixels(0), None]

    lax.fori_loop(edge, 2 * edge, place_parts, 0)
    lax.fori_loop(whole - 2 * edge, whole - edge, place_parts, 0)

    yp = (tile, plane * RING + lax.rem(y + 1, RING))
    ym = (tile, plane * RING + lax.rem(y + RING - 1, RING))
    zz = (tile, (1 - plane) * RING + y)
    far = plane * RING + lax.rem(y + 2, RING)

    def hop(p, route, owner, start, size, where):
        at = pl.ds(pl.multiple_of(first_row(owner, p) + start, 8), size)
        return remote(maps.at[:, at, :], maps.at[:, at, :], g_send.at[p, route], g_recv.at[p, route], where)

    def hops(p):
        return [
            hop(p, 0, me, 0, PIECE, zz),
            hop(p, 1, me, 0, PIECE, yp),
            hop(p, 2, me, 0, PIECE, ym),
            hop(p, 3, zz[1], 0, PIECE, yp),
            hop(p, 4, zz[1], 0, PIECE, ym),
            hop(p, 5, ym[1], 0, PIECE // 2, yp),
            hop(p, 6, yp[1], PIECE // 2, PIECE // 2, ym),
            hop(p, 7, far, 0, PIECE, zz),
        ]

    ways = [hops(0), hops(1)]

    def decompose(p):
        for copy in to_energies[p]:
            copy.wait_recv()
        step = 1.0 / jnp.full((PIECE, SIDE), squares, F32)
        pulls = []
        for k in range(MATERIALS):
            total = coef(0, k) * gath[p, 0]
            for e in range(1, ENERGIES):
                total = total + coef(e, k) * gath[p, e]
            pulls.append(total)
        levels = [jnp.maximum(step * pull, 0.0) for pull in pulls]
        for _ in range(NN_ITERS - 1):
            levels = [
                jnp.maximum(
                    levels[k]
                    - step
                    * (gram[k][0] * levels[0] + gram[k][1] * levels[1] + gram[k][2] * levels[2] - pulls[k]),
                    0.0,
                )
                for k in range(MATERIALS)
            ]
        for k in range(MATERIALS):
            maps[k, pl.ds(first_row(me, p), PIECE), :] = levels[k]
        for way in ways[p][:3]:
            way.start()

    wait_borders(weights)
    wait_borders(borders)

    def outer_rows(group, carry):
        for side, base in ((0, edge), (1, whole - 2 * edge)):
            row = pl.ds(pl.multiple_of(8 * group, 8), 8)
            at = pl.ds(pl.multiple_of(8 * (group + base), 8), 8)
            for h in range(2):
                sums = [num[c, h, at, :] + nrecv[side, c, h, row, :] for c in range(2)]
                renew(group + base, h, sums, wsum[h, at, :] + wrecv[side, h, row, :])
        return carry

    lax.fori_loop(0, edge, outer_rows, 0)
    to_energies[1] = send_pixels(1)

    def relay_first(p):
        ways[p][0].wait_recv()
        ways[p][3].start()
        ways[p][4].start()
        ways[p][1].wait_recv()
        ways[p][5].start()
        ways[p][2].wait_recv()
        ways[p][6].start()

    def relay_far(p):
        ways[p][5].wait_recv()
        ways[p][6].wait_recv()
        ways[p][7].start()

    own_spec = [spec[k, me] for k in range(MATERIALS)]

    def finish(owner, p):
        at = pl.ds(first_row(owner, p), PIECE)
        thickness = own_spec[0] * maps[0, at, :] + own_spec[1] * maps[1, at, :] + own_spec[2] * maps[2, at, :]
        fade = jnp.exp(-thickness)
        for c in range(2):
            model[c, at, :] = unit[c, at, :] * fade

    decompose(0)
    decompose(1)
    for p in range(2):
        finish(me, p)
    for p in range(2):
        relay_first(p)
        for owner in (zz[1], ym[1], yp[1]):
            finish(owner, p)
    for p in range(2):
        relay_far(p)
        finish(far, p)
    for p in range(2):
        for route, owner in ((3, ym), (4, yp), (7, (tile, far))):
            ways[p][route].wait_recv()
            finish(lax.rem(owner[1] + RING, ENERGIES), p)

    sent_borders(halo + weights + borders)
    for p in range(2):
        for copy in to_energies[p] + ways[p]:
            copy.wait_send()


def put_out(maps, model, maps_out, model_out, sems):
    copies = [
        pltpu.make_async_copy(maps, maps_out, sems.at[0]),
        pltpu.make_async_copy(model, model_out.at[0], sems.at[1]),
    ]
    for copy in copies:
        copy.start()
    for copy in copies:
        copy.wait()


def stay(*arrays):
    return [pltpu.with_memory_space_constraint(array, pltpu.HBM) for array in arrays]


def body(object_tiles, probe_field, intensity, row_offsets, col_offsets, tile_counts, material_spectra):
    tables = jnp.asarray(dft_tables())
    anywhere = pl.BlockSpec(memory_space=pl.ANY)
    dma = pltpu.SemaphoreType.DMA
    vmem = pl.BlockSpec(memory_space=pltpu.VMEM)
    maps, model = pl.pallas_call(
        kernel,
        out_shape=(
            jax.ShapeDtypeStruct((MATERIALS, SIDE, SIDE), F32),
            jax.ShapeDtypeStruct((2, SIDE, SIDE), F32),
        ),
        in_specs=[anywhere] * 6 + [pl.BlockSpec(memory_space=pltpu.SMEM), anywhere],
        out_specs=(vmem, vmem),
        scratch_shapes=[
            pltpu.VMEM((2, 2, SIDE + 2 * DEPTH, PROBE), F32),
            pltpu.VMEM((2, PROBE, PROBE), F32),
            pltpu.VMEM((SLOTS, PROBE, PROBE), BF16),
            pltpu.VMEM((4, SIDE, SIDE), BF16),
            pltpu.VMEM((SLOTS // 2, PROBE, SIDE), F32),
            pltpu.VMEM((SLOTS, 2, PROBE + 2 * PAD, PROBE), F32),
            pltpu.VMEM((SLOTS, PROBE + 2 * PAD, PROBE), F32),
            pltpu.VMEM((2, SIDE + 2 * DEPTH, PROBE), F32),
            pltpu.VMEM((2, 2, DEPTH, PROBE), F32),
            pltpu.VMEM((2, 2, SIDE + 2 * DEPTH, PROBE), F32),
            pltpu.VMEM((2, 2, 2, DEPTH, PROBE), F32),
            pltpu.VMEM((2, SIDE, SIDE), F32),
            pltpu.VMEM((SIDE, SIDE), F32),
            pltpu.VMEM((2, ENERGIES, PIECE, SIDE), F32),
            pltpu.SMEM((1, SLOTS), jnp.int32),
            pltpu.SMEM((1, SLOTS), jnp.int32),
            pltpu.SMEM((MATERIALS, ENERGIES), F32),
            dma((8,)),
            dma((4,)), dma((4,)),
            dma((2,)), dma((2,)),
            dma((2,)), dma((2,)),
            dma((2, ENERGIES - 1)), dma((2, ENERGIES - 1)),
            dma((2, 8)), dma((2, 8)),
        ],
        compiler_params=pltpu.CompilerParams(collective_id=0, has_side_effects=True, vmem_limit_bytes=24 * 2**20),
        name="refine",
    )(*stay(object_tiles, probe_field, intensity, tables, row_offsets, col_offsets), tile_counts, *stay(material_spectra.T))
    return pl.pallas_call(
        put_out,
        out_shape=(
            jax.ShapeDtypeStruct((MATERIALS, SIDE, SIDE), F32),
            jax.ShapeDtypeStruct((1, 2, SIDE, SIDE), F32),
        ),
        in_specs=[vmem, vmem],
        out_specs=(anywhere, anywhere),
        scratch_shapes=[dma((2,))],
        compiler_params=pltpu.CompilerParams(vmem_limit_bytes=8 * 2**20),
        name="put_out",
    )(maps, model)


def solution(mesh):
    placed = (
        P("energy", None, "tile", None),
        P("energy", None, None, None),
        P("energy", "tile", None, None, None),
        P("tile", None),
        P("tile", None),
        P("tile"),
        P(),
    )
    return jax.shard_map(
        body,
        mesh=mesh,
        in_specs=placed,
        out_specs=(P(None, "tile", None), P("energy", None, "tile", None)),
        check_vma=False,
    )
```

```python
import jax
import jax.numpy as jnp
import ml_dtypes
import numpy as np
from jax import lax
from jax.experimental import pallas as pl
from jax.experimental.pallas import tpu as pltpu
from jax.sharding import PartitionSpec as P

PROBE = 128
NN_ITERS = 8
SMOOTH = 0.01
DAMPING = 0.5
SIDE = 256
DEPTH = 64
SLOTS = 8
PAD = 8
ENERGIES = 8
RING = 4
PIECE = 16
MATERIALS = 3
UNROLL = 4

F32 = jnp.float32
BF16 = jnp.bfloat16
MESH = pl.DeviceIdType.MESH


def dft_tables():
    k = np.arange(PROBE)
    angles = 2.0 * np.pi / PROBE * (np.outer(k, k) % PROBE)
    cos, sin = np.cos(angles) / np.sqrt(PROBE), np.sin(angles) / np.sqrt(PROBE)
    table = np.block([[cos, -sin], [sin, cos]])
    out = []
    for full in (table, table.T):
        high = full.astype(np.float32).astype(ml_dtypes.bfloat16)
        low = (full - high.astype(np.float64)).astype(np.float32).astype(ml_dtypes.bfloat16)
        out += [high, low]
    return np.stack(out)


def halves(x):
    high = x.astype(BF16)
    return high, (x - high.astype(F32)).astype(BF16)


def mul(a, b):
    return jnp.dot(a, b, preferred_element_type=F32)


def right_apply(x, high, low):
    xh, xl = halves(x)
    return mul(xh, high) + mul(xl, high) + mul(xh, low)


def left_apply(high, low, x):
    xh, xl = halves(x)
    return mul(high, xh) + mul(high, xl) + mul(low, xh)


def swap_blocks(x):
    n = PROBE
    top = jnp.concatenate([x[:n, :n], x[n:, :n]], axis=1)
    bottom = jnp.concatenate([x[:n, n:], x[n:, n:]], axis=1)
    return jnp.concatenate([top, bottom], axis=0)


def kernel(
    obj, probe, inten, tables, rows_in, cols_in, count, spec_in,
    maps, model,
    ext, prb, itn, tab, root, part, pw, wsum, wrecv, num, nrecv, unit, att, gath, rows, cols, spec,
    load_sem, halo_send, halo_recv, w_send, w_recv, n_send, n_recv, a_send, a_recv, g_send, g_recv,
):
    tile = lax.axis_index("tile")
    me = lax.axis_index("energy")
    tiles = lax.axis_size("tile")
    plane, y = me // RING, lax.rem(me, RING)
    has_up, has_dn = tile > 0, tile < tiles - 1
    up, dn = tile - 1, tile + 1

    def peer(d):
        return lax.rem(me + d, ENERGIES)

    barrier = pltpu.get_barrier_semaphore()

    def greet(where):
        pl.semaphore_signal(barrier, inc=1, device_id=where, device_id_type=MESH)

    @pl.when(has_up)
    def _():
        greet((up, me))

    @pl.when(has_dn)
    def _():
        greet((dn, me))

    for d in range(1, ENERGIES):
        greet((tile, peer(d)))

    loads = [
        pltpu.make_async_copy(probe.at[0], prb, load_sem.at[0]),
        pltpu.make_async_copy(inten.at[0, 0], itn, load_sem.at[1]),
        pltpu.make_async_copy(tables, tab, load_sem.at[2]),
    ] + [
        pltpu.make_async_copy(
            obj.at[0, :, :, pl.ds(h * PROBE, PROBE)], ext.at[:, h, pl.ds(DEPTH, SIDE), :], load_sem.at[3 + h]
        )
        for h in range(2)
    ]
    scalars = [
        pltpu.make_async_copy(rows_in, rows, load_sem.at[5]),
        pltpu.make_async_copy(cols_in, cols, load_sem.at[6]),
        pltpu.make_async_copy(spec_in, spec, load_sem.at[7]),
    ]
    for load in scalars + loads:
        load.start()

    greeted = ENERGIES - 1 + has_up.astype(jnp.int32) + has_dn.astype(jnp.int32)
    pl.semaphore_wait(barrier, greeted)

    def remote(src, dst, send, recv, where):
        return pltpu.make_async_remote_copy(
            src_ref=src, dst_ref=dst, send_sem=send, recv_sem=recv, device_id=where, device_id_type=MESH
        )

    def border_pair(src_up, dst_up, src_dn, dst_dn, send, recv, first):
        return (
            remote(src_up, dst_up, send.at[first], recv.at[first], (up, me)),
            remote(src_dn, dst_dn, send.at[first + 1], recv.at[first + 1], (dn, me)),
        )

    shares_up = lax.rem(tile, 2) == 1

    def start_borders(pairs):
        @pl.when(shares_up)
        def _():
            for to_up, _ in pairs:
                to_up.start()

        @pl.when(has_dn)
        def _():
            for _, to_dn in pairs:
                to_dn.start()

        @pl.when(jnp.logical_and(has_up, jnp.logical_not(shares_up)))
        def _():
            for to_up, _ in pairs:
                to_up.start()

    def wait_borders(pairs):
        @pl.when(has_dn)
        def _():
            for to_up, _ in pairs:
                to_up.wait_recv()

        @pl.when(has_up)
        def _():
            for _, to_dn in pairs:
                to_dn.wait_recv()

    def sent_borders(pairs):
        @pl.when(has_up)
        def _():
            for to_up, _ in pairs:
                to_up.wait_send()

        @pl.when(has_dn)
        def _():
            for _, to_dn in pairs:
                to_dn.wait_send()

    last = SIDE + DEPTH
    halo = [
        border_pair(
            obj.at[0, :, pl.ds(0, DEPTH), pl.ds(h * PROBE, PROBE)],
            ext.at[:, h, pl.ds(last, DEPTH), :],
            obj.at[0, :, pl.ds(SIDE - DEPTH, DEPTH), pl.ds(h * PROBE, PROBE)],
            ext.at[:, h, pl.ds(0, DEPTH), :],
            halo_send, halo_recv, 2 * h,
        )
        for h in range(2)
    ]
    start_borders(halo)

    @pl.when(jnp.logical_not(has_up))
    def _():
        ext[:, :, 0:DEPTH, :] = jnp.zeros((2, 2, DEPTH, PROBE), F32)
        wrecv[0] = jnp.zeros((2, DEPTH, PROBE), F32)
        nrecv[0] = jnp.zeros((2, 2, DEPTH, PROBE), F32)

    @pl.when(jnp.logical_not(has_dn))
    def _():
        ext[:, :, last:, :] = jnp.zeros((2, 2, DEPTH, PROBE), F32)
        wrecv[1] = jnp.zeros((2, DEPTH, PROBE), F32)
        nrecv[1] = jnp.zeros((2, 2, DEPTH, PROBE), F32)

    part[:, :, 0:PAD, :] = jnp.zeros((SLOTS, 2, PAD, PROBE), F32)
    part[:, :, PAD + PROBE :, :] = jnp.zeros((SLOTS, 2, PAD, PROBE), F32)
    pw[:, 0:PAD, :] = jnp.zeros((SLOTS, PAD, PROBE), F32)
    pw[:, PAD + PROBE :, :] = jnp.zeros((SLOTS, PAD, PROBE), F32)

    for load in scalars:
        load.wait()
    live = count[0]
    lefts = [cols[0, j] for j in range(SLOTS)]
    tops = [jnp.where(j < live, rows[0, j] + DEPTH, 8 * SIDE) for j in range(SLOTS)]
    lane8 = lax.broadcasted_iota(jnp.int32, (8, PROBE), 1)

    loads[0].wait()
    probe_re, probe_im = prb[0], prb[1]
    power = probe_re * probe_re + probe_im * probe_im
    for j in range(SLOTS):
        pw[j, PAD : PAD + PROBE, :] = pltpu.roll(power, lax.rem(lefts[j], PROBE), 1)

    def placed(read, group, terms):
        left = [jnp.zeros((8, PROBE), F32) for _ in range(terms)]
        right = [jnp.zeros((8, PROBE), F32) for _ in range(terms)]
        for j in range(SLOTS):
            at = jnp.clip(8 * group - tops[j], -PAD, PROBE) + PAD
            inside = lane8 >= lefts[j]
            for c in range(terms):
                value = read(j, c, pl.ds(at, 8))
                left[c] = left[c] + jnp.where(inside, value, 0.0)
                right[c] = right[c] + jnp.where(inside, 0.0, value)
        return left, right

    def place_weights(group, carry):
        left, right = placed(lambda j, c, where: pw[j, where, :], group, 1)
        at = pl.ds(pl.multiple_of(8 * group, 8), 8)
        wsum[0, at, :] = left[0]
        wsum[1, at, :] = right[0]
        return carry

    edge = DEPTH // 8
    whole = (SIDE + 2 * DEPTH) // 8
    lax.fori_loop(0, edge, place_weights, 0)
    lax.fori_loop(whole - edge, whole, place_weights, 0)
    weights = [
        border_pair(
            wsum.at[:, pl.ds(0, DEPTH), :], wrecv.at[1],
            wsum.at[:, pl.ds(last, DEPTH), :], wrecv.at[0],
            w_send, w_recv, 0,
        )
    ]
    start_borders(weights)
    lax.fori_loop(edge, whole - edge, place_weights, 0)

    loads[1].wait()

    def take_roots(pair, carry):
        for s in range(2):
            root[pair, :, s * PROBE : (s + 1) * PROBE] = jnp.sqrt(itn[2 * pair + s].astype(F32))
        return carry

    lax.fori_loop(0, SLOTS // 2, take_roots, 0)

    def coef(e, k):
        return spec[k, e]

    gram = [[None] * MATERIALS for _ in range(MATERIALS)]
    for k in range(MATERIALS):
        for l in range(k, MATERIALS):
            total = coef(0, k) * coef(0, l)
            for e in range(1, ENERGIES):
                total = total + coef(e, k) * coef(e, l)
            gram[k][l] = gram[l][k] = total
    squares = gram[0][0] + gram[1][1] + gram[2][2]

    for load in loads[2:]:
        load.wait()
    wait_borders(halo)

    lane = lax.broadcasted_iota(jnp.int32, (PROBE, PROBE), 1)

    def project(pair, carry):
        exits = []
        for s in range(2):
            j = 2 * pair + s
            top, left = rows[0, j] + DEPTH, cols[0, j]
            turn = lax.rem(PROBE - left, PROBE)
            first = lane < PROBE - left
            view = [
                jnp.where(
                    first,
                    pltpu.roll(ext[c, 0, pl.ds(top, PROBE), :], turn, 1),
                    pltpu.roll(ext[c, 1, pl.ds(top, PROBE), :], turn, 1),
                )
                for c in range(2)
            ]
            pr, pi = prb[0], prb[1]
            exits.append(jnp.concatenate([pr * view[0] - pi * view[1], pr * view[1] + pi * view[0]], axis=1))
        exit_wave = jnp.concatenate(exits, axis=0)
        t_high, t_low, u_high, u_low = tab[0], tab[1], tab[2], tab[3]
        half = swap_blocks(right_apply(exit_wave, t_high, t_low))
        spectrum = left_apply(u_high, u_low, half)
        sr, si = spectrum[:PROBE], spectrum[PROBE:]
        factor = root[pair] * lax.rsqrt(sr * sr + si * si + SMOOTH)
        half = swap_blocks(left_apply(t_high, t_low, jnp.concatenate([sr * factor, si * factor], axis=0)))
        change = right_apply(half, u_high, u_low) - exit_wave
        for s in range(2):
            j = 2 * pair + s
            cr = change[s * PROBE : (s + 1) * PROBE, :PROBE]
            ci = change[s * PROBE : (s + 1) * PROBE, PROBE:]
            pr, pi = prb[0], prb[1]
            turn = lax.rem(cols[0, j], PROBE)
            part[j, 0, PAD : PAD + PROBE, :] = pltpu.roll(pr * cr + pi * ci, turn, 1)
            part[j, 1, PAD : PAD + PROBE, :] = pltpu.roll(pr * ci - pi * cr, turn, 1)
        return carry

    lax.fori_loop(0, SLOTS // 2, project, 0, unroll=UNROLL)

    def numerators(group):
        return placed(lambda j, c, where: part[j, c, where, :], group, 2)

    def place_parts(group, carry):
        left, right = numerators(group)
        at = pl.ds(pl.multiple_of(8 * group, 8), 8)
        for c in range(2):
            num[c, 0, at, :] = left[c]
            num[c, 1, at, :] = right[c]
        return carry

    lax.fori_loop(0, edge, place_parts, 0)
    lax.fori_loop(whole - edge, whole, place_parts, 0)
    borders = [
        border_pair(
            num.at[:, :, pl.ds(0, DEPTH), :], nrecv.at[1],
            num.at[:, :, pl.ds(last, DEPTH), :], nrecv.at[0],
            n_send, n_recv, 0,
        )
    ]
    start_borders(borders)

    def renew(group, h, numerator, weight):
        at = pl.ds(pl.multiple_of(8 * group, 8), 8)
        own = pl.ds(pl.multiple_of(8 * group - DEPTH, 8), 8)
        inverse = 1.0 / (weight + DAMPING)
        new = [ext[c, h, at, :] + numerator[c] * inverse for c in range(2)]
        squared = new[0] * new[0] + new[1] * new[1] + SMOOTH
        scale = lax.rsqrt(squared)
        for c in range(2):
            unit[c, own, h * PROBE : (h + 1) * PROBE] = new[c] * scale
        att[own, h * PROBE : (h + 1) * PROBE] = -0.5 * jnp.log(squared)

    def inner_rows(group, carry):
        at = pl.ds(pl.multiple_of(8 * group, 8), 8)
        for h, sums in enumerate(numerators(group)):
            renew(group, h, sums, wsum[h, at, :])
        return carry

    def first_row(f, p):
        fp, fy = f // RING, lax.rem(f, RING)
        start = DEPTH + DEPTH * fp + PIECE * fy if p == 0 else (SIDE - DEPTH) * fp + PIECE * fy
        return pl.multiple_of(start, PIECE)

    def regroup(p):
        return [
            remote(
                att.at[pl.ds(first_row(peer(d), p), PIECE), :], gath.at[p, me],
                a_send.at[p, d - 1], a_recv.at[p, d - 1], (tile, peer(d)),
            )
            for d in range(1, ENERGIES)
        ]

    def send_pixels(p):
        copies = regroup(p)
        for copy in copies:
            copy.start()
        gath[p, me] = att[pl.ds(first_row(me, p), PIECE), :]
        return copies

    lax.fori_loop(2 * edge, whole - 2 * edge, inner_rows, 0)
    to_energies = [send_pixels(0), None]

    lax.fori_loop(edge, 2 * edge, place_parts, 0)
    lax.fori_loop(whole - 2 * edge, whole - edge, place_parts, 0)

    def device(planes, steps):
        return lax.rem(plane + planes, 2) * RING + lax.rem(y + steps + RING, RING)

    steps = ((1, 2), (0, 1), (0, -1), (1, 0), (0, 2), (1, 1), (1, -1))

    def hops(p):
        at = pl.ds(first_row(me, p), PIECE)
        return [
            remote(
                maps.at[:, at, :], maps.at[:, at, :], g_send.at[p, i], g_recv.at[p, i], (tile, device(planes, step))
            )
            for i, (planes, step) in enumerate(steps)
        ]

    ways = [hops(0), hops(1)]

    def decompose(p):
        for copy in to_energies[p]:
            copy.wait_recv()
        step = 1.0 / jnp.full((PIECE, SIDE), squares, F32)
        pulls = []
        for k in range(MATERIALS):
            total = coef(0, k) * gath[p, 0]
            for e in range(1, ENERGIES):
                total = total + coef(e, k) * gath[p, e]
            pulls.append(total)
        levels = [jnp.maximum(step * pull, 0.0) for pull in pulls]
        for _ in range(NN_ITERS - 1):
            levels = [
                jnp.maximum(
                    levels[k]
                    - step
                    * (gram[k][0] * levels[0] + gram[k][1] * levels[1] + gram[k][2] * levels[2] - pulls[k]),
                    0.0,
                )
                for k in range(MATERIALS)
            ]
        for k in range(MATERIALS):
            maps[k, pl.ds(first_row(me, p), PIECE), :] = levels[k]
        for way in ways[p]:
            way.start()

    wait_borders(weights)
    wait_borders(borders)

    def outer_rows(group, carry):
        for side, base in ((0, edge), (1, whole - 2 * edge)):
            row = pl.ds(pl.multiple_of(8 * group, 8), 8)
            at = pl.ds(pl.multiple_of(8 * (group + base), 8), 8)
            for h in range(2):
                sums = [num[c, h, at, :] + nrecv[side, c, h, row, :] for c in range(2)]
                renew(group + base, h, sums, wsum[h, at, :] + wrecv[side, h, row, :])
        return carry

    lax.fori_loop(0, edge, outer_rows, 0)
    to_energies[1] = send_pixels(1)

    own_spec = [spec[k, me] for k in range(MATERIALS)]

    def finish(owner, p):
        at = pl.ds(first_row(owner, p), PIECE)
        thickness = own_spec[0] * maps[0, at, :] + own_spec[1] * maps[1, at, :] + own_spec[2] * maps[2, at, :]
        fade = jnp.exp(-thickness)
        for c in range(2):
            model[c, at, :] = unit[c, at, :] * fade

    decompose(0)
    decompose(1)
    for p in range(2):
        finish(me, p)
    for p in range(2):
        for i in (1, 2, 3, 4, 5, 6, 0):
            ways[p][i].wait_recv()
            finish(device(steps[i][0], -steps[i][1]), p)

    sent_borders(halo + weights + borders)
    for p in range(2):
        for copy in to_energies[p] + ways[p]:
            copy.wait_send()


def put_out(maps, model, maps_out, model_out, sems):
    copies = [
        pltpu.make_async_copy(maps, maps_out, sems.at[0]),
        pltpu.make_async_copy(model, model_out.at[0], sems.at[1]),
    ]
    for copy in copies:
        copy.start()
    for copy in copies:
        copy.wait()


def stay(*arrays):
    return [pltpu.with_memory_space_constraint(array, pltpu.HBM) for array in arrays]


def body(object_tiles, probe_field, intensity, row_offsets, col_offsets, tile_counts, material_spectra):
    tables = jnp.asarray(dft_tables())
    anywhere = pl.BlockSpec(memory_space=pl.ANY)
    dma = pltpu.SemaphoreType.DMA
    vmem = pl.BlockSpec(memory_space=pltpu.VMEM)
    maps, model = pl.pallas_call(
        kernel,
        out_shape=(
            jax.ShapeDtypeStruct((MATERIALS, SIDE, SIDE), F32),
            jax.ShapeDtypeStruct((2, SIDE, SIDE), F32),
        ),
        in_specs=[anywhere] * 6 + [pl.BlockSpec(memory_space=pltpu.SMEM), anywhere],
        out_specs=(vmem, vmem),
        scratch_shapes=[
            pltpu.VMEM((2, 2, SIDE + 2 * DEPTH, PROBE), F32),
            pltpu.VMEM((2, PROBE, PROBE), F32),
            pltpu.VMEM((SLOTS, PROBE, PROBE), BF16),
            pltpu.VMEM((4, SIDE, SIDE), BF16),
            pltpu.VMEM((SLOTS // 2, PROBE, SIDE), F32),
            pltpu.VMEM((SLOTS, 2, PROBE + 2 * PAD, PROBE), F32),
            pltpu.VMEM((SLOTS, PROBE + 2 * PAD, PROBE), F32),
            pltpu.VMEM((2, SIDE + 2 * DEPTH, PROBE), F32),
            pltpu.VMEM((2, 2, DEPTH, PROBE), F32),
            pltpu.VMEM((2, 2, SIDE + 2 * DEPTH, PROBE), F32),
            pltpu.VMEM((2, 2, 2, DEPTH, PROBE), F32),
            pltpu.VMEM((2, SIDE, SIDE), F32),
            pltpu.VMEM((SIDE, SIDE), F32),
            pltpu.VMEM((2, ENERGIES, PIECE, SIDE), F32),
            pltpu.SMEM((1, SLOTS), jnp.int32),
            pltpu.SMEM((1, SLOTS), jnp.int32),
            pltpu.SMEM((MATERIALS, ENERGIES), F32),
            dma((8,)),
            dma((4,)), dma((4,)),
            dma((2,)), dma((2,)),
            dma((2,)), dma((2,)),
            dma((2, ENERGIES - 1)), dma((2, ENERGIES - 1)),
            dma((2, ENERGIES - 1)), dma((2, ENERGIES - 1)),
        ],
        compiler_params=pltpu.CompilerParams(collective_id=0, has_side_effects=True, vmem_limit_bytes=24 * 2**20),
        name="refine",
    )(*stay(object_tiles, probe_field, intensity, tables, row_offsets, col_offsets), tile_counts, *stay(material_spectra.T))
    return pl.pallas_call(
        put_out,
        out_shape=(
            jax.ShapeDtypeStruct((MATERIALS, SIDE, SIDE), F32),
            jax.ShapeDtypeStruct((1, 2, SIDE, SIDE), F32),
        ),
        in_specs=[vmem, vmem],
        out_specs=(anywhere, anywhere),
        scratch_shapes=[dma((2,))],
        compiler_params=pltpu.CompilerParams(vmem_limit_bytes=8 * 2**20),
        name="put_out",
    )(maps, model)


def solution(mesh):
    placed = (
        P("energy", None, "tile", None),
        P("energy", None, None, None),
        P("energy", "tile", None, None, None),
        P("tile", None),
        P("tile", None),
        P("tile"),
        P(),
    )
    return jax.shard_map(
        body,
        mesh=mesh,
        in_specs=placed,
        out_specs=(P(None, "tile", None), P("energy", None, "tile", None)),
        check_vma=False,
    )
```

```python
import jax
import jax.numpy as jnp
import ml_dtypes
import numpy as np
from jax import lax
from jax.experimental import pallas as pl
from jax.experimental.pallas import tpu as pltpu
from jax.sharding import PartitionSpec as P

PROBE = 128
NN_ITERS = 8
SMOOTH = 0.01
DAMPING = 0.5
SIDE = 256
DEPTH = 64
SLOTS = 8
PAD = 8
ENERGIES = 8
RING = 4
PIECES = (16, 8, 8)
FAR_FIRST = (6, 2, 5, 3, 7, 1, 4)
MATERIALS = 3

F32 = jnp.float32
BF16 = jnp.bfloat16
MESH = pl.DeviceIdType.MESH


def dft_tables():
    k = np.arange(PROBE)
    angles = 2.0 * np.pi / PROBE * (np.outer(k, k) % PROBE)
    cos, sin = np.cos(angles) / np.sqrt(PROBE), np.sin(angles) / np.sqrt(PROBE)
    table = np.block([[cos, -sin], [sin, cos]])
    out = []
    for full in (table, table.T):
        high = full.astype(np.float32).astype(ml_dtypes.bfloat16)
        low = (full - high.astype(np.float64)).astype(np.float32).astype(ml_dtypes.bfloat16)
        out += [high, low]
    return np.stack(out)


def halves(x):
    high = x.astype(BF16)
    return high, (x - high.astype(F32)).astype(BF16)


def mul(a, b):
    return jnp.dot(a, b, preferred_element_type=F32)


def right_apply(x, high, low):
    xh, xl = halves(x)
    return mul(xh, high) + mul(xl, high) + mul(xh, low)


def left_apply(high, low, x):
    xh, xl = halves(x)
    return mul(high, xh) + mul(high, xl) + mul(low, xh)


def swap_blocks(x):
    n = PROBE
    top = jnp.concatenate([x[:n, :n], x[n:, :n]], axis=1)
    bottom = jnp.concatenate([x[:n, n:], x[n:, n:]], axis=1)
    return jnp.concatenate([top, bottom], axis=0)


def kernel(
    obj, probe, inten, tables, rows_in, cols_in, count, spec_in,
    maps, model,
    ext, prb, itn, tab, root, part, pw, wsum, wrecv, num, nrecv, unit, att, gath, rows, cols, spec,
    load_sem, halo_send, halo_recv, w_send, w_recv, n_send, n_recv, a_send, a_recv, g_send, g_recv,
):
    tile = lax.axis_index("tile")
    me = lax.axis_index("energy")
    tiles = lax.axis_size("tile")
    plane, y = me // RING, lax.rem(me, RING)
    has_up, has_dn = tile > 0, tile < tiles - 1
    up, dn = tile - 1, tile + 1

    def peer(d):
        return lax.rem(me + d, ENERGIES)

    barrier = pltpu.get_barrier_semaphore()

    def greet(where):
        pl.semaphore_signal(barrier, inc=1, device_id=where, device_id_type=MESH)

    @pl.when(has_up)
    def _():
        greet((up, me))

    @pl.when(has_dn)
    def _():
        greet((dn, me))

    for d in range(1, ENERGIES):
        greet((tile, peer(d)))

    loads = [
        pltpu.make_async_copy(probe.at[0], prb, load_sem.at[0]),
        pltpu.make_async_copy(inten.at[0, 0], itn, load_sem.at[1]),
        pltpu.make_async_copy(tables, tab, load_sem.at[2]),
    ] + [
        pltpu.make_async_copy(
            obj.at[0, :, :, pl.ds(h * PROBE, PROBE)], ext.at[:, h, pl.ds(DEPTH, SIDE), :], load_sem.at[3 + h]
        )
        for h in range(2)
    ]
    scalars = [
        pltpu.make_async_copy(rows_in, rows, load_sem.at[5]),
        pltpu.make_async_copy(cols_in, cols, load_sem.at[6]),
        pltpu.make_async_copy(spec_in, spec, load_sem.at[7]),
    ]
    for load in scalars + loads:
        load.start()

    greeted = ENERGIES - 1 + has_up.astype(jnp.int32) + has_dn.astype(jnp.int32)
    pl.semaphore_wait(barrier, greeted)

    def remote(src, dst, send, recv, where):
        return pltpu.make_async_remote_copy(
            src_ref=src, dst_ref=dst, send_sem=send, recv_sem=recv, device_id=where, device_id_type=MESH
        )

    def border_pair(src_up, dst_up, src_dn, dst_dn, send, recv, first):
        return (
            remote(src_up, dst_up, send.at[first], recv.at[first], (up, me)),
            remote(src_dn, dst_dn, send.at[first + 1], recv.at[first + 1], (dn, me)),
        )

    odd = lax.rem(tile, 2) == 1
    even = jnp.logical_not(odd)
    link_up, link_dn = jnp.logical_and(even, has_up), jnp.logical_and(odd, has_dn)
    chip_side = 1 - lax.rem(tile, 2)
    link_side = 1 - chip_side

    def when(condition, action, copies):
        @pl.when(condition)
        def _():
            for copy in copies:
                getattr(copy, action)()

    def start_link(pairs, action="start"):
        when(link_up, action, [to_up for to_up, _ in pairs])
        when(link_dn, action, [to_dn for _, to_dn in pairs])

    def start_chip(pairs, action="start"):
        when(even, action, [to_dn for _, to_dn in pairs])
        when(odd, action, [to_up for to_up, _ in pairs])

    def wait_link(pairs):
        when(link_up, "wait_recv", [to_dn for _, to_dn in pairs])
        when(link_dn, "wait_recv", [to_up for to_up, _ in pairs])

    def wait_chip(pairs):
        when(even, "wait_recv", [to_up for to_up, _ in pairs])
        when(odd, "wait_recv", [to_dn for _, to_dn in pairs])

    last = SIDE + DEPTH
    halo = [
        border_pair(
            obj.at[0, :, pl.ds(0, DEPTH), pl.ds(h * PROBE, PROBE)],
            ext.at[:, h, pl.ds(last, DEPTH), :],
            obj.at[0, :, pl.ds(SIDE - DEPTH, DEPTH), pl.ds(h * PROBE, PROBE)],
            ext.at[:, h, pl.ds(0, DEPTH), :],
            halo_send, halo_recv, 2 * h,
        )
        for h in range(2)
    ]
    start_link(halo)
    start_chip(halo)

    @pl.when(jnp.logical_not(has_up))
    def _():
        ext[:, :, 0:DEPTH, :] = jnp.zeros((2, 2, DEPTH, PROBE), F32)
        wrecv[0] = jnp.zeros((2, DEPTH, PROBE), F32)
        nrecv[0] = jnp.zeros((2, 2, DEPTH, PROBE), F32)

    @pl.when(jnp.logical_not(has_dn))
    def _():
        ext[:, :, last:, :] = jnp.zeros((2, 2, DEPTH, PROBE), F32)
        wrecv[1] = jnp.zeros((2, DEPTH, PROBE), F32)
        nrecv[1] = jnp.zeros((2, 2, DEPTH, PROBE), F32)

    part[:, :, 0:PAD, :] = jnp.zeros((SLOTS, 2, PAD, PROBE), F32)
    part[:, :, PAD + PROBE :, :] = jnp.zeros((SLOTS, 2, PAD, PROBE), F32)
    pw[:, 0:PAD, :] = jnp.zeros((SLOTS, PAD, PROBE), F32)
    pw[:, PAD + PROBE :, :] = jnp.zeros((SLOTS, PAD, PROBE), F32)

    for load in scalars:
        load.wait()
    live = count[0]
    lefts = [cols[0, j] for j in range(SLOTS)]
    tops = [jnp.where(j < live, rows[0, j] + DEPTH, 8 * SIDE) for j in range(SLOTS)]
    lane8 = lax.broadcasted_iota(jnp.int32, (8, PROBE), 1)

    loads[0].wait()
    probe_re, probe_im = prb[0], prb[1]
    power = probe_re * probe_re + probe_im * probe_im
    for j in range(SLOTS):
        pw[j, PAD : PAD + PROBE, :] = pltpu.roll(power, lax.rem(lefts[j], PROBE), 1)

    def placed(read, group, terms):
        left = [jnp.zeros((8, PROBE), F32) for _ in range(terms)]
        right = [jnp.zeros((8, PROBE), F32) for _ in range(terms)]
        for j in range(SLOTS):
            at = jnp.clip(8 * group - tops[j], -PAD, PROBE) + PAD
            inside = lane8 >= lefts[j]
            for c in range(terms):
                value = read(j, c, pl.ds(at, 8))
                left[c] = left[c] + jnp.where(inside, value, 0.0)
                right[c] = right[c] + jnp.where(inside, 0.0, value)
        return left, right

    def place_weights(group, carry):
        left, right = placed(lambda j, c, where: pw[j, where, :], group, 1)
        at = pl.ds(pl.multiple_of(8 * group, 8), 8)
        wsum[0, at, :] = left[0]
        wsum[1, at, :] = right[0]
        return carry

    edge = DEPTH // 8
    whole = (SIDE + 2 * DEPTH) // 8
    lax.fori_loop(0, edge, place_weights, 0)
    lax.fori_loop(whole - edge, whole, place_weights, 0)
    weights = [
        border_pair(
            wsum.at[:, pl.ds(0, DEPTH), :], wrecv.at[1],
            wsum.at[:, pl.ds(last, DEPTH), :], wrecv.at[0],
            w_send, w_recv, 0,
        )
    ]
    start_link(weights)
    start_chip(weights)
    lax.fori_loop(edge, whole - edge, place_weights, 0)

    loads[1].wait()

    def take_roots(pair, carry):
        for s in range(2):
            root[pair, :, s * PROBE : (s + 1) * PROBE] = jnp.sqrt(itn[2 * pair + s].astype(F32))
        return carry

    lax.fori_loop(0, SLOTS // 2, take_roots, 0)

    def coef(e, k):
        return spec[k, e]

    gram = [[None] * MATERIALS for _ in range(MATERIALS)]
    for k in range(MATERIALS):
        for l in range(k, MATERIALS):
            total = coef(0, k) * coef(0, l)
            for e in range(1, ENERGIES):
                total = total + coef(e, k) * coef(e, l)
            gram[k][l] = gram[l][k] = total
    squares = gram[0][0] + gram[1][1] + gram[2][2]

    for load in loads[2:]:
        load.wait()
    wait_chip(halo)
    wait_link(halo)

    lane = lax.broadcasted_iota(jnp.int32, (PROBE, PROBE), 1)

    def cut_windows(pair, state):
        exits = []
        for s in range(2):
            j = 2 * pair + s
            top = pl.ds(rows[0, j] + DEPTH, PROBE)
            inside = lane >= lefts[j]
            turn = lax.rem(PROBE - lefts[j], PROBE)
            view = [
                pltpu.roll(jnp.where(inside, ext[c, 0, top, :], ext[c, 1, top, :]), turn, 1) for c in range(2)
            ]
            pr, pi = prb[0], prb[1]
            exits.append(jnp.concatenate([pr * view[0] - pi * view[1], pr * view[1] + pi * view[0]], axis=1))
        state["exit"] = jnp.concatenate(exits, axis=0)

    def transform_rows(pair, state):
        state["x"] = swap_blocks(right_apply(state["exit"], tab[0], tab[1]))

    def transform_columns(pair, state):
        spectrum = left_apply(tab[2], tab[3], state["x"])
        sr, si = spectrum[:PROBE], spectrum[PROBE:]
        factor = root[pair] * lax.rsqrt(sr * sr + si * si + SMOOTH)
        state["x"] = jnp.concatenate([sr * factor, si * factor], axis=0)

    def restore_columns(pair, state):
        state["x"] = swap_blocks(left_apply(tab[0], tab[1], state["x"]))

    def restore_rows(pair, state):
        change = right_apply(state["x"], tab[2], tab[3]) - state["exit"]
        for s in range(2):
            j = 2 * pair + s
            cr = change[s * PROBE : (s + 1) * PROBE, :PROBE]
            ci = change[s * PROBE : (s + 1) * PROBE, PROBE:]
            pr, pi = prb[0], prb[1]
            turn = lax.rem(lefts[j], PROBE)
            part[j, 0, PAD : PAD + PROBE, :] = pltpu.roll(pr * cr + pi * ci, turn, 1)
            part[j, 1, PAD : PAD + PROBE, :] = pltpu.roll(pr * ci - pi * cr, turn, 1)

    states = [{} for _ in range(SLOTS // 2)]
    for stage in (cut_windows, transform_rows, transform_columns, restore_columns, restore_rows):
        for pair in range(SLOTS // 2):
            stage(pair, states[pair])

    def numerators(group):
        return placed(lambda j, c, where: part[j, c, where, :], group, 2)

    def place_parts(group, carry):
        left, right = numerators(group)
        at = pl.ds(pl.multiple_of(8 * group, 8), 8)
        for c in range(2):
            num[c, 0, at, :] = left[c]
            num[c, 1, at, :] = right[c]
        return carry

    def place_edge(side):
        lax.fori_loop(0, edge, lambda g, carry: place_parts(g + side * (whole - edge), carry), 0)

    def place_next(side):
        lax.fori_loop(0, edge, lambda g, carry: place_parts(g + edge + side * (whole - 3 * edge), carry), 0)

    borders = [
        border_pair(
            num.at[:, :, pl.ds(0, DEPTH), :], nrecv.at[1],
            num.at[:, :, pl.ds(last, DEPTH), :], nrecv.at[0],
            n_send, n_recv, 0,
        )
    ]
    place_edge(link_side)
    start_link(borders)
    place_edge(chip_side)
    start_chip(borders)

    def renew(group, h, numerator, weight):
        at = pl.ds(pl.multiple_of(8 * group, 8), 8)
        own = pl.ds(pl.multiple_of(8 * group - DEPTH, 8), 8)
        inverse = 1.0 / (weight + DAMPING)
        new = [ext[c, h, at, :] + numerator[c] * inverse for c in range(2)]
        squared = new[0] * new[0] + new[1] * new[1] + SMOOTH
        scale = lax.rsqrt(squared)
        for c in range(2):
            unit[c, own, h * PROBE : (h + 1) * PROBE] = new[c] * scale
        att[own, h * PROBE : (h + 1) * PROBE] = -0.5 * jnp.log(squared)

    def inner_rows(group, carry):
        at = pl.ds(pl.multiple_of(8 * group, 8), 8)
        for h, sums in enumerate(numerators(group)):
            renew(group, h, sums, wsum[h, at, :])
        return carry

    def first_row(f, p):
        start = (DEPTH, chip_side * (SIDE - DEPTH), link_side * (SIDE - DEPTH))[p]
        return pl.multiple_of(start + PIECES[p] * f, 8)

    spots = [sum(PIECES[:p]) for p in range(len(PIECES))]

    def send_pixels(p):
        spot = pl.ds(spots[p], PIECES[p])
        copies = [
            remote(
                att.at[pl.ds(first_row(peer(d), p), PIECES[p]), :], gath.at[me, spot, :],
                a_send.at[p, d - 1], a_recv.at[p, d - 1], (tile, peer(d)),
            )
            for d in FAR_FIRST
        ]
        for copy in copies:
            copy.start()
        gath[me, spot, :] = att[pl.ds(first_row(me, p), PIECES[p]), :]
        return copies

    lax.fori_loop(2 * edge, whole - 2 * edge, inner_rows, 0)
    to_energies = [send_pixels(0)]
    place_next(chip_side)

    def device(planes, steps):
        return lax.rem(plane + planes, 2) * RING + lax.rem(y + steps + RING, RING)

    def hop(p, i, owner, to):
        at = pl.ds(first_row(owner, p), PIECES[p])
        return remote(maps.at[:, at, :], maps.at[:, at, :], g_send.at[p, i], g_recv.at[p, i], (tile, to))

    steps = ((1, 0), (0, 2), (0, 1), (0, -1), (1, 1), (1, -1), (1, 2))

    def hops(p):
        ways = [hop(p, i, me, device(*step)) for i, step in enumerate(steps)]
        if p == 0:
            ways[4:] = [
                hop(p, 4, device(1, 0), device(0, 1)),
                hop(p, 5, device(1, 0), device(0, -1)),
                hop(p, 6, device(0, 2), device(1, 0)),
            ]
        return ways

    ways = [hops(p) for p in range(len(PIECES))]

    def decompose(p):
        for copy in to_energies[p]:
            copy.wait_recv()
        spot = pl.ds(spots[p], PIECES[p])
        step = 1.0 / jnp.full((PIECES[p], SIDE), squares, F32)
        pulls = []
        for k in range(MATERIALS):
            total = coef(0, k) * gath[0, spot, :]
            for e in range(1, ENERGIES):
                total = total + coef(e, k) * gath[e, spot, :]
            pulls.append(total)
        levels = [jnp.maximum(step * pull, 0.0) for pull in pulls]
        for _ in range(NN_ITERS - 1):
            levels = [
                jnp.maximum(
                    levels[k]
                    - step
                    * (gram[k][0] * levels[0] + gram[k][1] * levels[1] + gram[k][2] * levels[2] - pulls[k]),
                    0.0,
                )
                for k in range(MATERIALS)
            ]
        for k in range(MATERIALS):
            maps[k, pl.ds(first_row(me, p), PIECES[p]), :] = levels[k]
        for i in (0, 1, 2, 3) if p == 0 else (6, 1, 4, 5, 2, 3, 0):
            ways[p][i].start()

    def outer_rows(side):
        base = edge + side * (whole - 3 * edge)

        def rows_of(group, carry):
            row = pl.ds(pl.multiple_of(8 * group, 8), 8)
            at = pl.ds(pl.multiple_of(8 * (group + base), 8), 8)
            for h in range(2):
                sums = [num[c, h, at, :] + nrecv[side, c, h, row, :] for c in range(2)]
                renew(group + base, h, sums, wsum[h, at, :] + wrecv[side, h, row, :])
            return carry

        lax.fori_loop(0, edge, rows_of, 0)

    wait_chip(weights + borders)
    outer_rows(chip_side)
    to_energies.append(send_pixels(1))
    place_next(link_side)

    own_spec = [spec[k, me] for k in range(MATERIALS)]

    def finish(owner, p):
        at = pl.ds(first_row(owner, p), PIECES[p])
        thickness = own_spec[0] * maps[0, at, :] + own_spec[1] * maps[1, at, :] + own_spec[2] * maps[2, at, :]
        fade = jnp.exp(-thickness)
        for c in range(2):
            model[c, at, :] = unit[c, at, :] * fade

    decompose(0)
    wait_link(weights + borders)
    outer_rows(link_side)
    to_energies.append(send_pixels(2))
    decompose(1)
    ways[0][0].wait_recv()
    ways[0][4].start()
    ways[0][5].start()
    ways[0][1].wait_recv()
    ways[0][6].start()
    finish(me, 0)
    finish(me, 1)
    finish(device(1, 0), 0)
    finish(device(0, 2), 0)
    decompose(2)
    finish(me, 2)
    for p in range(len(PIECES)):
        for i, (planes, step) in enumerate(steps):
            if p > 0 or i > 1:
                ways[p][i].wait_recv()
                finish(device(planes, -step), p)

    start_link(halo + weights + borders, "wait_send")
    start_chip(halo + weights + borders, "wait_send")
    for copy in sum(to_energies + ways, []):
        copy.wait_send()


def put_out(maps, model, maps_out, model_out, sems):
    copies = [
        pltpu.make_async_copy(maps, maps_out, sems.at[0]),
        pltpu.make_async_copy(model, model_out.at[0], sems.at[1]),
    ]
    for copy in copies:
        copy.start()
    for copy in copies:
        copy.wait()


def stay(*arrays):
    return [pltpu.with_memory_space_constraint(array, pltpu.HBM) for array in arrays]


def body(object_tiles, probe_field, intensity, row_offsets, col_offsets, tile_counts, material_spectra):
    tables = jnp.asarray(dft_tables())
    anywhere = pl.BlockSpec(memory_space=pl.ANY)
    dma = pltpu.SemaphoreType.DMA
    vmem = pl.BlockSpec(memory_space=pltpu.VMEM)
    maps, model = pl.pallas_call(
        kernel,
        out_shape=(
            jax.ShapeDtypeStruct((MATERIALS, SIDE, SIDE), F32),
            jax.ShapeDtypeStruct((2, SIDE, SIDE), F32),
        ),
        in_specs=[anywhere] * 6 + [pl.BlockSpec(memory_space=pltpu.SMEM), anywhere],
        out_specs=(vmem, vmem),
        scratch_shapes=[
            pltpu.VMEM((2, 2, SIDE + 2 * DEPTH, PROBE), F32),
            pltpu.VMEM((2, PROBE, PROBE), F32),
            pltpu.VMEM((SLOTS, PROBE, PROBE), BF16),
            pltpu.VMEM((4, SIDE, SIDE), BF16),
            pltpu.VMEM((SLOTS // 2, PROBE, SIDE), F32),
            pltpu.VMEM((SLOTS, 2, PROBE + 2 * PAD, PROBE), F32),
            pltpu.VMEM((SLOTS, PROBE + 2 * PAD, PROBE), F32),
            pltpu.VMEM((2, SIDE + 2 * DEPTH, PROBE), F32),
            pltpu.VMEM((2, 2, DEPTH, PROBE), F32),
            pltpu.VMEM((2, 2, SIDE + 2 * DEPTH, PROBE), F32),
            pltpu.VMEM((2, 2, 2, DEPTH, PROBE), F32),
            pltpu.VMEM((2, SIDE, SIDE), F32),
            pltpu.VMEM((SIDE, SIDE), F32),
            pltpu.VMEM((ENERGIES, sum(PIECES), SIDE), F32),
            pltpu.SMEM((1, SLOTS), jnp.int32),
            pltpu.SMEM((1, SLOTS), jnp.int32),
            pltpu.SMEM((MATERIALS, ENERGIES), F32),
            dma((8,)),
            dma((4,)), dma((4,)),
            dma((2,)), dma((2,)),
            dma((2,)), dma((2,)),
            dma((len(PIECES), ENERGIES - 1)), dma((len(PIECES), ENERGIES - 1)),
            dma((len(PIECES), ENERGIES - 1)), dma((len(PIECES), ENERGIES - 1)),
        ],
        compiler_params=pltpu.CompilerParams(collective_id=0, has_side_effects=True, vmem_limit_bytes=24 * 2**20),
        name="refine",
    )(*stay(object_tiles, probe_field, intensity, tables, row_offsets, col_offsets), tile_counts, *stay(material_spectra.T))
    return pl.pallas_call(
        put_out,
        out_shape=(
            jax.ShapeDtypeStruct((MATERIALS, SIDE, SIDE), F32),
            jax.ShapeDtypeStruct((1, 2, SIDE, SIDE), F32),
        ),
        in_specs=[vmem, vmem],
        out_specs=(anywhere, anywhere),
        scratch_shapes=[dma((2,))],
        compiler_params=pltpu.CompilerParams(vmem_limit_bytes=8 * 2**20),
        name="put_out",
    )(maps, model)


def solution(mesh):
    placed = (
        P("energy", None, "tile", None),
        P("energy", None, None, None),
        P("energy", "tile", None, None, None),
        P("tile", None),
        P("tile", None),
        P("tile"),
        P(),
    )
    return jax.shard_map(
        body,
        mesh=mesh,
        in_specs=placed,
        out_specs=(P(None, "tile", None), P("energy", None, "tile", None)),
        check_vma=False,
    )
```

```python
import jax
import jax.numpy as jnp
import ml_dtypes
import numpy as np
from jax import lax
from jax.experimental import pallas as pl
from jax.experimental.pallas import tpu as pltpu
from jax.sharding import PartitionSpec as P

PROBE = 128
NN_ITERS = 8
SMOOTH = 0.01
DAMPING = 0.5
SIDE = 256
DEPTH = 64
SLOTS = 8
PAD = 8
ENERGIES = 8
RING = 4
PIECES = (16, 8, 8)
FAR_FIRST = (6, 2, 5, 3, 7, 1, 4)
MATERIALS = 3

F32 = jnp.float32
BF16 = jnp.bfloat16
MESH = pl.DeviceIdType.MESH


def dft_tables():
    k = np.arange(PROBE)
    angles = 2.0 * np.pi / PROBE * (np.outer(k, k) % PROBE)
    cos, sin = np.cos(angles) / np.sqrt(PROBE), np.sin(angles) / np.sqrt(PROBE)
    table = np.block([[cos, -sin], [sin, cos]])
    out = []
    for full in (table, table.T):
        high = full.astype(np.float32).astype(ml_dtypes.bfloat16)
        low = (full - high.astype(np.float64)).astype(np.float32).astype(ml_dtypes.bfloat16)
        out += [high, low]
    return np.stack(out)


def halves(x):
    high = x.astype(BF16)
    return high, (x - high.astype(F32)).astype(BF16)


def mul(a, b):
    return jnp.dot(a, b, preferred_element_type=F32)


def right_apply(x, high, low):
    xh, xl = halves(x)
    return mul(xh, high) + mul(xl, high) + mul(xh, low)


def left_apply(high, low, x):
    xh, xl = halves(x)
    return mul(high, xh) + mul(high, xl) + mul(low, xh)


def swap_blocks(x):
    n = PROBE
    top = jnp.concatenate([x[:n, :n], x[n:, :n]], axis=1)
    bottom = jnp.concatenate([x[:n, n:], x[n:, n:]], axis=1)
    return jnp.concatenate([top, bottom], axis=0)


def kernel(
    obj, probe, inten, tables, rows_in, cols_in, count, spec_in,
    maps, model,
    ext, prb, itn, tab, root, part, pw, wsum, wrecv, num, nrecv, unit, att, gath, rows, cols, spec,
    load_sem, b_send, halo_recv, b_recv, a_send, a_recv, g_send, g_recv,
):
    tile = lax.axis_index("tile")
    me = lax.axis_index("energy")
    tiles = lax.axis_size("tile")
    plane, y = me // RING, lax.rem(me, RING)
    has_up, has_dn = tile > 0, tile < tiles - 1
    up, dn = tile - 1, tile + 1

    def peer(d):
        return lax.rem(me + d, ENERGIES)

    barrier = pltpu.get_barrier_semaphore()

    def greet(where):
        pl.semaphore_signal(barrier, inc=1, device_id=where, device_id_type=MESH)

    @pl.when(has_up)
    def _():
        greet((up, me))

    @pl.when(has_dn)
    def _():
        greet((dn, me))

    for d in range(1, ENERGIES):
        greet((tile, peer(d)))

    loads = [
        pltpu.make_async_copy(probe.at[0], prb, load_sem.at[0]),
        pltpu.make_async_copy(inten.at[0, 0], itn, load_sem.at[1]),
        pltpu.make_async_copy(tables, tab, load_sem.at[2]),
    ] + [
        pltpu.make_async_copy(
            obj.at[0, :, :, pl.ds(h * PROBE, PROBE)], ext.at[:, h, pl.ds(DEPTH, SIDE), :], load_sem.at[3 + h]
        )
        for h in range(2)
    ]
    scalars = [
        pltpu.make_async_copy(rows_in, rows, load_sem.at[5]),
        pltpu.make_async_copy(cols_in, cols, load_sem.at[6]),
        pltpu.make_async_copy(spec_in, spec, load_sem.at[7]),
    ]
    for load in scalars + loads:
        load.start()

    greeted = ENERGIES - 1 + has_up.astype(jnp.int32) + has_dn.astype(jnp.int32)
    pl.semaphore_wait(barrier, greeted)

    def remote(src, dst, send, recv, where):
        return pltpu.make_async_remote_copy(
            src_ref=src, dst_ref=dst, send_sem=send, recv_sem=recv, device_id=where, device_id_type=MESH
        )

    def border_pair(src_up, dst_up, src_dn, dst_dn, recv):
        return (
            remote(src_up, dst_up, b_send.at[0], recv.at[0], (up, me)),
            remote(src_dn, dst_dn, b_send.at[1], recv.at[1], (dn, me)),
        )

    def block_pair(block, recv):
        return [border_pair(block, block, block, block, recv)]

    odd = lax.rem(tile, 2) == 1
    even = jnp.logical_not(odd)
    link_up, link_dn = jnp.logical_and(even, has_up), jnp.logical_and(odd, has_dn)
    chip_side = 1 - lax.rem(tile, 2)
    link_side = 1 - chip_side

    def when(condition, action, copies):
        @pl.when(condition)
        def _():
            for copy in copies:
                getattr(copy, action)()

    def start_link(pairs, action="start"):
        when(link_up, action, [to_up for to_up, _ in pairs])
        when(link_dn, action, [to_dn for _, to_dn in pairs])

    def start_chip(pairs, action="start"):
        when(even, action, [to_dn for _, to_dn in pairs])
        when(odd, action, [to_up for to_up, _ in pairs])

    def wait_link(pairs):
        when(link_up, "wait_recv", [to_dn for _, to_dn in pairs])
        when(link_dn, "wait_recv", [to_up for to_up, _ in pairs])

    def wait_chip(pairs):
        when(even, "wait_recv", [to_up for to_up, _ in pairs])
        when(odd, "wait_recv", [to_dn for _, to_dn in pairs])

    last = SIDE + DEPTH
    halo = [
        border_pair(
            obj.at[0, :, pl.ds(0, DEPTH), pl.ds(h * PROBE, PROBE)],
            ext.at[:, h, pl.ds(last, DEPTH), :],
            obj.at[0, :, pl.ds(SIDE - DEPTH, DEPTH), pl.ds(h * PROBE, PROBE)],
            ext.at[:, h, pl.ds(0, DEPTH), :],
            halo_recv,
        )
        for h in range(2)
    ]
    start_link(halo)
    start_chip(halo)

    @pl.when(jnp.logical_not(has_up))
    def _():
        ext[:, :, 0:DEPTH, :] = jnp.zeros((2, 2, DEPTH, PROBE), F32)
        wrecv[0] = jnp.zeros((2, DEPTH, PROBE), F32)
        nrecv[0] = jnp.zeros((2, 2, DEPTH, PROBE), F32)

    @pl.when(jnp.logical_not(has_dn))
    def _():
        ext[:, :, last:, :] = jnp.zeros((2, 2, DEPTH, PROBE), F32)
        wrecv[1] = jnp.zeros((2, DEPTH, PROBE), F32)
        nrecv[1] = jnp.zeros((2, 2, DEPTH, PROBE), F32)

    part[:, :, 0:PAD, :] = jnp.zeros((SLOTS, 2, PAD, PROBE), F32)
    part[:, :, PAD + PROBE :, :] = jnp.zeros((SLOTS, 2, PAD, PROBE), F32)
    pw[:, 0:PAD, :] = jnp.zeros((SLOTS, PAD, PROBE), F32)
    pw[:, PAD + PROBE :, :] = jnp.zeros((SLOTS, PAD, PROBE), F32)

    for load in scalars:
        load.wait()
    live = count[0]
    lefts = [cols[0, j] for j in range(SLOTS)]
    tops = [jnp.where(j < live, rows[0, j] + DEPTH, 8 * SIDE) for j in range(SLOTS)]
    lane8 = lax.broadcasted_iota(jnp.int32, (8, PROBE), 1)

    loads[0].wait()
    probe_re, probe_im = prb[0], prb[1]
    power = probe_re * probe_re + probe_im * probe_im
    for j in range(SLOTS):
        pw[j, PAD : PAD + PROBE, :] = pltpu.roll(power, lax.rem(lefts[j], PROBE), 1)

    def placed(read, group, terms):
        left = [jnp.zeros((8, PROBE), F32) for _ in range(terms)]
        right = [jnp.zeros((8, PROBE), F32) for _ in range(terms)]
        for j in range(SLOTS):
            at = jnp.clip(8 * group - tops[j], -PAD, PROBE) + PAD
            inside = lane8 >= lefts[j]
            for c in range(terms):
                value = read(j, c, pl.ds(at, 8))
                left[c] = left[c] + jnp.where(inside, value, 0.0)
                right[c] = right[c] + jnp.where(inside, 0.0, value)
        return left, right

    def place_weights(group, carry):
        left, right = placed(lambda j, c, where: pw[j, where, :], group, 1)
        at = pl.ds(pl.multiple_of(8 * group, 8), 8)
        wsum[0, at, :] = left[0]
        wsum[1, at, :] = right[0]
        return carry

    edge = DEPTH // 8
    whole = (SIDE + 2 * DEPTH) // 8
    lax.fori_loop(0, edge, place_weights, 0)
    lax.fori_loop(whole - edge, whole, place_weights, 0)
    weights = [
        border_pair(
            wsum.at[:, pl.ds(0, DEPTH), :], wrecv.at[1],
            wsum.at[:, pl.ds(last, DEPTH), :], wrecv.at[0],
            b_recv,
        )
    ]
    lax.fori_loop(edge, whole - edge, place_weights, 0)

    loads[1].wait()

    def take_roots(pair, carry):
        for s in range(2):
            root[pair, :, s * PROBE : (s + 1) * PROBE] = jnp.sqrt(itn[2 * pair + s].astype(F32))
        return carry

    lax.fori_loop(0, SLOTS // 2, take_roots, 0)

    def coef(e, k):
        return spec[k, e]

    gram = [[None] * MATERIALS for _ in range(MATERIALS)]
    for k in range(MATERIALS):
        for l in range(k, MATERIALS):
            total = coef(0, k) * coef(0, l)
            for e in range(1, ENERGIES):
                total = total + coef(e, k) * coef(e, l)
            gram[k][l] = gram[l][k] = total
    squares = gram[0][0] + gram[1][1] + gram[2][2]

    for load in loads[2:]:
        load.wait()
    halo_bytes = block_pair(nrecv.at[0], halo_recv)
    wait_chip(halo_bytes)
    wait_link(halo_bytes)
    start_link(weights)
    start_chip(weights)

    lane = lax.broadcasted_iota(jnp.int32, (PROBE, PROBE), 1)

    def cut_windows(pair, state):
        exits = []
        for s in range(2):
            j = 2 * pair + s
            top = pl.ds(rows[0, j] + DEPTH, PROBE)
            inside = lane >= lefts[j]
            turn = lax.rem(PROBE - lefts[j], PROBE)
            view = [
                pltpu.roll(jnp.where(inside, ext[c, 0, top, :], ext[c, 1, top, :]), turn, 1) for c in range(2)
            ]
            pr, pi = prb[0], prb[1]
            exits.append(jnp.concatenate([pr * view[0] - pi * view[1], pr * view[1] + pi * view[0]], axis=1))
        state["exit"] = jnp.concatenate(exits, axis=0)

    def transform_rows(pair, state):
        state["x"] = swap_blocks(right_apply(state["exit"], tab[0], tab[1]))

    def transform_columns(pair, state):
        spectrum = left_apply(tab[2], tab[3], state["x"])
        sr, si = spectrum[:PROBE], spectrum[PROBE:]
        factor = root[pair] * lax.rsqrt(sr * sr + si * si + SMOOTH)
        state["x"] = jnp.concatenate([sr * factor, si * factor], axis=0)

    def restore_columns(pair, state):
        state["x"] = swap_blocks(left_apply(tab[0], tab[1], state["x"]))

    def restore_rows(pair, state):
        change = right_apply(state["x"], tab[2], tab[3]) - state["exit"]
        for s in range(2):
            j = 2 * pair + s
            cr = change[s * PROBE : (s + 1) * PROBE, :PROBE]
            ci = change[s * PROBE : (s + 1) * PROBE, PROBE:]
            pr, pi = prb[0], prb[1]
            turn = lax.rem(lefts[j], PROBE)
            part[j, 0, PAD : PAD + PROBE, :] = pltpu.roll(pr * cr + pi * ci, turn, 1)
            part[j, 1, PAD : PAD + PROBE, :] = pltpu.roll(pr * ci - pi * cr, turn, 1)

    states = [{} for _ in range(SLOTS // 2)]
    for stage in (cut_windows, transform_rows, transform_columns, restore_columns, restore_rows):
        for pair in range(SLOTS // 2):
            stage(pair, states[pair])

    def numerators(group):
        return placed(lambda j, c, where: part[j, c, where, :], group, 2)

    def place_parts(group, carry):
        left, right = numerators(group)
        at = pl.ds(pl.multiple_of(8 * group, 8), 8)
        for c in range(2):
            num[c, 0, at, :] = left[c]
            num[c, 1, at, :] = right[c]
        return carry

    def place_edge(side):
        lax.fori_loop(0, edge, lambda g, carry: place_parts(g + side * (whole - edge), carry), 0)

    def place_next(side):
        lax.fori_loop(0, edge, lambda g, carry: place_parts(g + edge + side * (whole - 3 * edge), carry), 0)

    borders = [
        border_pair(
            num.at[:, :, pl.ds(0, DEPTH), :], nrecv.at[1],
            num.at[:, :, pl.ds(last, DEPTH), :], nrecv.at[0],
            b_recv,
        )
    ]
    place_edge(link_side)
    start_link(borders)
    place_edge(chip_side)
    start_chip(borders)

    def renew(group, h, numerator, weight):
        at = pl.ds(pl.multiple_of(8 * group, 8), 8)
        own = pl.ds(pl.multiple_of(8 * group - DEPTH, 8), 8)
        inverse = 1.0 / (weight + DAMPING)
        new = [ext[c, h, at, :] + numerator[c] * inverse for c in range(2)]
        squared = new[0] * new[0] + new[1] * new[1] + SMOOTH
        scale = lax.rsqrt(squared)
        for c in range(2):
            unit[c, own, h * PROBE : (h + 1) * PROBE] = new[c] * scale
        att[own, h * PROBE : (h + 1) * PROBE] = -0.5 * jnp.log(squared)

    def inner_rows(group, carry):
        at = pl.ds(pl.multiple_of(8 * group, 8), 8)
        for h, sums in enumerate(numerators(group)):
            renew(group, h, sums, wsum[h, at, :])
        return carry

    def first_row(f, p):
        start = (DEPTH, chip_side * (SIDE - DEPTH), link_side * (SIDE - DEPTH))[p]
        return pl.multiple_of(start + PIECES[p] * f, 8)

    spots = [sum(PIECES[:p]) for p in range(len(PIECES))]

    def send_pixels(p):
        spot = pl.ds(spots[p], PIECES[p])
        for d in FAR_FIRST:
            remote(
                att.at[pl.ds(first_row(peer(d), p), PIECES[p]), :], gath.at[me, spot, :],
                a_send.at[0], a_recv.at[p], (tile, peer(d)),
            ).start()
        gath[me, spot, :] = att[pl.ds(first_row(me, p), PIECES[p]), :]

    lax.fori_loop(2 * edge, whole - 2 * edge, inner_rows, 0)
    send_pixels(0)
    place_next(chip_side)

    def device(planes, steps):
        return lax.rem(plane + planes, 2) * RING + lax.rem(y + steps + RING, RING)

    def hop(p, i, owner, to):
        at = pl.ds(first_row(owner, p), PIECES[p])
        return remote(maps.at[:, at, :], maps.at[:, at, :], g_send.at[0], g_recv.at[p + 2 if p > 0 else min(i, 2)], (tile, to))

    steps = ((1, 0), (0, 2), (0, 1), (0, -1), (1, 1), (1, -1), (1, 2))

    def hops(p):
        if p > 0:
            return [hop(p, i, me, device(*step)) for i, step in enumerate(steps)]
        return [hop(p, i, me, device(*step)) for i, step in enumerate(steps[:4])] + [
            hop(p, 4, device(1, 0), device(0, 1)),
            hop(p, 5, device(1, 0), device(0, -1)),
            hop(p, 6, device(0, 2), device(1, 0)),
        ]

    ways = [hops(p) for p in range(len(PIECES))]

    def decompose(p):
        block = att.at[pl.ds(0, (ENERGIES - 1) * PIECES[p]), :]
        remote(block, block, a_send.at[0], a_recv.at[p], (tile, peer(1))).wait_recv()
        spot = pl.ds(spots[p], PIECES[p])
        step = 1.0 / jnp.full((PIECES[p], SIDE), squares, F32)
        pulls = []
        for k in range(MATERIALS):
            total = coef(0, k) * gath[0, spot, :]
            for e in range(1, ENERGIES):
                total = total + coef(e, k) * gath[e, spot, :]
            pulls.append(total)
        levels = [jnp.maximum(step * pull, 0.0) for pull in pulls]
        for _ in range(NN_ITERS - 1):
            levels = [
                jnp.maximum(
                    levels[k]
                    - step
                    * (gram[k][0] * levels[0] + gram[k][1] * levels[1] + gram[k][2] * levels[2] - pulls[k]),
                    0.0,
                )
                for k in range(MATERIALS)
            ]
        for k in range(MATERIALS):
            maps[k, pl.ds(first_row(me, p), PIECES[p]), :] = levels[k]
        for i in (0, 1, 2, 3) if p == 0 else (6, 1, 4, 5, 2, 3, 0):
            ways[p][i].start()

    def outer_rows(side):
        base = edge + side * (whole - 3 * edge)

        def rows_of(group, carry):
            row = pl.ds(pl.multiple_of(8 * group, 8), 8)
            at = pl.ds(pl.multiple_of(8 * (group + base), 8), 8)
            for h in range(2):
                sums = [num[c, h, at, :] + nrecv[side, c, h, row, :] for c in range(2)]
                renew(group + base, h, sums, wsum[h, at, :] + wrecv[side, h, row, :])
            return carry

        lax.fori_loop(0, edge, rows_of, 0)

    border_bytes = block_pair(num.at[:, :, pl.ds(0, 3 * DEPTH // 2), :], b_recv)
    wait_chip(border_bytes)
    outer_rows(chip_side)
    send_pixels(1)
    place_next(link_side)

    own_spec = [spec[k, me] for k in range(MATERIALS)]

    def finish(p):
        at = pl.ds(first_row(0, p), ENERGIES * PIECES[p])
        thickness = own_spec[0] * maps[0, at, :] + own_spec[1] * maps[1, at, :] + own_spec[2] * maps[2, at, :]
        fade = jnp.exp(-thickness)
        for c in range(2):
            model[c, at, :] = unit[c, at, :] * fade

    def arrived(p, pieces):
        block = maps.at[:, pl.ds(0, pieces * PIECES[p]), :]
        remote(block, block, g_send.at[0], g_recv.at[p + 2], (tile, peer(1))).wait_recv()

    wait_link(border_bytes)
    outer_rows(link_side)
    send_pixels(2)
    decompose(0)
    decompose(1)
    ways[0][0].wait_recv()
    ways[0][4].start()
    ways[0][5].start()
    ways[0][1].wait_recv()
    ways[0][6].start()
    decompose(2)
    for p in range(len(PIECES)):
        arrived(p, ENERGIES - 3 if p == 0 else ENERGIES - 1)
        finish(p)

    sent_bytes = block_pair(num.at[:, :, pl.ds(0, 5 * DEPTH // 2), :], b_recv)
    start_link(sent_bytes, "wait_send")
    start_chip(sent_bytes, "wait_send")
    block = att.at[pl.ds(0, (ENERGIES - 1) * sum(PIECES)), :]
    remote(block, block, a_send.at[0], a_recv.at[0], (tile, peer(1))).wait_send()
    block = maps.at[:, pl.ds(0, (ENERGIES - 1) * sum(PIECES)), :]
    remote(block, block, g_send.at[0], g_recv.at[0], (tile, peer(1))).wait_send()


def put_out(maps, model, maps_out, model_out, sems):
    copies = [
        pltpu.make_async_copy(maps, maps_out, sems.at[0]),
        pltpu.make_async_copy(model, model_out.at[0], sems.at[1]),
    ]
    for copy in copies:
        copy.start()
    for copy in copies:
        copy.wait()


def stay(*arrays):
    return [pltpu.with_memory_space_constraint(array, pltpu.HBM) for array in arrays]


def body(object_tiles, probe_field, intensity, row_offsets, col_offsets, tile_counts, material_spectra):
    tables = jnp.asarray(dft_tables())
    anywhere = pl.BlockSpec(memory_space=pl.ANY)
    dma = pltpu.SemaphoreType.DMA
    vmem = pl.BlockSpec(memory_space=pltpu.VMEM)
    maps, model = pl.pallas_call(
        kernel,
        out_shape=(
            jax.ShapeDtypeStruct((MATERIALS, SIDE, SIDE), F32),
            jax.ShapeDtypeStruct((2, SIDE, SIDE), F32),
        ),
        in_specs=[anywhere] * 6 + [pl.BlockSpec(memory_space=pltpu.SMEM), anywhere],
        out_specs=(vmem, vmem),
        scratch_shapes=[
            pltpu.VMEM((2, 2, SIDE + 2 * DEPTH, PROBE), F32),
            pltpu.VMEM((2, PROBE, PROBE), F32),
            pltpu.VMEM((SLOTS, PROBE, PROBE), BF16),
            pltpu.VMEM((4, SIDE, SIDE), BF16),
            pltpu.VMEM((SLOTS // 2, PROBE, SIDE), F32),
            pltpu.VMEM((SLOTS, 2, PROBE + 2 * PAD, PROBE), F32),
            pltpu.VMEM((SLOTS, PROBE + 2 * PAD, PROBE), F32),
            pltpu.VMEM((2, SIDE + 2 * DEPTH, PROBE), F32),
            pltpu.VMEM((2, 2, DEPTH, PROBE), F32),
            pltpu.VMEM((2, 2, SIDE + 2 * DEPTH, PROBE), F32),
            pltpu.VMEM((2, 2, 2, DEPTH, PROBE), F32),
            pltpu.VMEM((2, SIDE, SIDE), F32),
            pltpu.VMEM((SIDE, SIDE), F32),
            pltpu.VMEM((ENERGIES, sum(PIECES), SIDE), F32),
            pltpu.SMEM((1, SLOTS), jnp.int32),
            pltpu.SMEM((1, SLOTS), jnp.int32),
            pltpu.SMEM((MATERIALS, ENERGIES), F32),
            dma((8,)), dma((2,)), dma((2,)), dma((2,)), dma((1,)), dma((len(PIECES),)), dma((1,)), dma((len(PIECES) + 2,)),
        ],
        compiler_params=pltpu.CompilerParams(collective_id=0, has_side_effects=True, vmem_limit_bytes=24 * 2**20),
        name="refine",
    )(*stay(object_tiles, probe_field, intensity, tables, row_offsets, col_offsets), tile_counts, *stay(material_spectra.T))
    return pl.pallas_call(
        put_out,
        out_shape=(
            jax.ShapeDtypeStruct((MATERIALS, SIDE, SIDE), F32),
            jax.ShapeDtypeStruct((1, 2, SIDE, SIDE), F32),
        ),
        in_specs=[vmem, vmem],
        out_specs=(anywhere, anywhere),
        scratch_shapes=[dma((2,))],
        compiler_params=pltpu.CompilerParams(vmem_limit_bytes=8 * 2**20),
        name="put_out",
    )(maps, model)


def solution(mesh):
    placed = (
        P("energy", None, "tile", None),
        P("energy", None, None, None),
        P("energy", "tile", None, None, None),
        P("tile", None),
        P("tile", None),
        P("tile"),
        P(),
    )
    return jax.shard_map(
        body,
        mesh=mesh,
        in_specs=placed,
        out_specs=(P(None, "tile", None), P("energy", None, "tile", None)),
        check_vma=False,
    )
```

```python
import jax
import jax.numpy as jnp
import ml_dtypes
import numpy as np
from jax import lax
from jax.experimental import pallas as pl
from jax.experimental.pallas import tpu as pltpu
from jax.sharding import PartitionSpec as P

PROBE = 128
NN_ITERS = 8
SMOOTH = 0.01
DAMPING = 0.5
SIDE = 256
DEPTH = 64
SLOTS = 8
PAD = 8
ENERGIES = 8
RING = 4
PIECES = (16, 8, 8)
FAR_FIRST = (6, 2, 5, 3, 7, 1, 4)
MATERIALS = 3

F32 = jnp.float32
BF16 = jnp.bfloat16
MESH = pl.DeviceIdType.MESH


def dft_tables():
    k = np.arange(PROBE)
    angles = 2.0 * np.pi / PROBE * (np.outer(k, k) % PROBE)
    cos, sin = np.cos(angles) / np.sqrt(PROBE), np.sin(angles) / np.sqrt(PROBE)
    table = np.block([[cos, -sin], [sin, cos]])
    out = []
    for full in (table, table.T):
        high = full.astype(np.float32).astype(ml_dtypes.bfloat16)
        low = (full - high.astype(np.float64)).astype(np.float32).astype(ml_dtypes.bfloat16)
        out += [high, low]
    return np.stack(out)


def halves(x):
    high = x.astype(BF16)
    return high, (x - high.astype(F32)).astype(BF16)


def mul(a, b):
    return jnp.dot(a, b, preferred_element_type=F32)


def right_apply(x, high, low):
    xh, xl = halves(x)
    return mul(xh, high) + mul(xl, high) + mul(xh, low)


def left_apply(high, low, x):
    xh, xl = halves(x)
    return mul(high, xh) + mul(high, xl) + mul(low, xh)


def swap_blocks(x):
    n = PROBE
    top = jnp.concatenate([x[:n, :n], x[n:, :n]], axis=1)
    bottom = jnp.concatenate([x[:n, n:], x[n:, n:]], axis=1)
    return jnp.concatenate([top, bottom], axis=0)


def kernel(
    obj, probe, inten, tables, rows_in, cols_in, count, spec_in,
    maps, model,
    ext, prb, itn, tab, root, part, pw, wsum, wrecv, num, nrecv, unit, att, gath, rows, cols, spec,
    load_sem, b_send, halo_recv, b_recv, a_send, a_recv, g_send, g_recv,
):
    tile = lax.axis_index("tile")
    me = lax.axis_index("energy")
    tiles = lax.axis_size("tile")
    plane, y = me // RING, lax.rem(me, RING)
    has_up, has_dn = tile > 0, tile < tiles - 1
    up, dn = tile - 1, tile + 1

    def peer(d):
        return lax.rem(me + d, ENERGIES)

    barrier = pltpu.get_barrier_semaphore()

    def greet(where):
        pl.semaphore_signal(barrier, inc=1, device_id=where, device_id_type=MESH)

    @pl.when(has_up)
    def _():
        greet((up, me))

    @pl.when(has_dn)
    def _():
        greet((dn, me))

    for d in range(1, ENERGIES):
        greet((tile, peer(d)))

    loads = [
        pltpu.make_async_copy(probe.at[0], prb, load_sem.at[0]),
        pltpu.make_async_copy(inten.at[0, 0], itn, load_sem.at[1]),
        pltpu.make_async_copy(tables, tab, load_sem.at[2]),
    ] + [
        pltpu.make_async_copy(
            obj.at[0, :, :, pl.ds(h * PROBE, PROBE)], ext.at[:, h, pl.ds(DEPTH, SIDE), :], load_sem.at[3 + h]
        )
        for h in range(2)
    ]
    scalars = [
        pltpu.make_async_copy(rows_in, rows, load_sem.at[5]),
        pltpu.make_async_copy(cols_in, cols, load_sem.at[6]),
        pltpu.make_async_copy(spec_in, spec, load_sem.at[7]),
    ]
    for load in scalars + loads:
        load.start()

    greeted = ENERGIES - 1 + has_up.astype(jnp.int32) + has_dn.astype(jnp.int32)
    pl.semaphore_wait(barrier, greeted)

    def remote(src, dst, send, recv, where):
        return pltpu.make_async_remote_copy(
            src_ref=src, dst_ref=dst, send_sem=send, recv_sem=recv, device_id=where, device_id_type=MESH
        )

    def border_pair(src_up, dst_up, src_dn, dst_dn, recv):
        return (
            remote(src_up, dst_up, b_send.at[0], recv.at[0], (up, me)),
            remote(src_dn, dst_dn, b_send.at[1], recv.at[1], (dn, me)),
        )

    def block_pair(block, recv):
        return [border_pair(block, block, block, block, recv)]

    odd = lax.rem(tile, 2) == 1
    even = jnp.logical_not(odd)
    link_up, link_dn = jnp.logical_and(even, has_up), jnp.logical_and(odd, has_dn)
    chip_side = 1 - lax.rem(tile, 2)
    link_side = 1 - chip_side

    def when(condition, action, copies):
        @pl.when(condition)
        def _():
            for copy in copies:
                getattr(copy, action)()

    def start_link(pairs, action="start"):
        when(link_up, action, [to_up for to_up, _ in pairs])
        when(link_dn, action, [to_dn for _, to_dn in pairs])

    def start_chip(pairs, action="start"):
        when(even, action, [to_dn for _, to_dn in pairs])
        when(odd, action, [to_up for to_up, _ in pairs])

    def wait_link(pairs):
        when(link_up, "wait_recv", [to_dn for _, to_dn in pairs])
        when(link_dn, "wait_recv", [to_up for to_up, _ in pairs])

    def wait_chip(pairs):
        when(even, "wait_recv", [to_up for to_up, _ in pairs])
        when(odd, "wait_recv", [to_dn for _, to_dn in pairs])

    last = SIDE + DEPTH
    halo = [
        border_pair(
            obj.at[0, :, pl.ds(0, DEPTH), pl.ds(h * PROBE, PROBE)],
            ext.at[:, h, pl.ds(last, DEPTH), :],
            obj.at[0, :, pl.ds(SIDE - DEPTH, DEPTH), pl.ds(h * PROBE, PROBE)],
            ext.at[:, h, pl.ds(0, DEPTH), :],
            halo_recv,
        )
        for h in range(2)
    ]
    start_link(halo)
    start_chip(halo)

    @pl.when(jnp.logical_not(has_up))
    def _():
        ext[:, :, 0:DEPTH, :] = jnp.zeros((2, 2, DEPTH, PROBE), F32)
        wrecv[0] = jnp.zeros((2, DEPTH, PROBE), F32)
        nrecv[0] = jnp.zeros((2, 2, DEPTH, PROBE), F32)

    @pl.when(jnp.logical_not(has_dn))
    def _():
        ext[:, :, last:, :] = jnp.zeros((2, 2, DEPTH, PROBE), F32)
        wrecv[1] = jnp.zeros((2, DEPTH, PROBE), F32)
        nrecv[1] = jnp.zeros((2, 2, DEPTH, PROBE), F32)

    part[:, :, 0:PAD, :] = jnp.zeros((SLOTS, 2, PAD, PROBE), F32)
    part[:, :, PAD + PROBE :, :] = jnp.zeros((SLOTS, 2, PAD, PROBE), F32)
    pw[:, 0:PAD, :] = jnp.zeros((SLOTS, PAD, PROBE), F32)
    pw[:, PAD + PROBE :, :] = jnp.zeros((SLOTS, PAD, PROBE), F32)

    for load in scalars:
        load.wait()
    live = count[0]
    lefts = [cols[0, j] for j in range(SLOTS)]
    tops = [jnp.where(j < live, rows[0, j] + DEPTH, 8 * SIDE) for j in range(SLOTS)]
    lane8 = lax.broadcasted_iota(jnp.int32, (8, PROBE), 1)

    loads[0].wait()
    probe_re, probe_im = prb[0], prb[1]
    power = probe_re * probe_re + probe_im * probe_im
    for j in range(SLOTS):
        pw[j, PAD : PAD + PROBE, :] = pltpu.roll(power, lax.rem(lefts[j], PROBE), 1)

    def placed(read, group, terms):
        left = [jnp.zeros((8, PROBE), F32) for _ in range(terms)]
        right = [jnp.zeros((8, PROBE), F32) for _ in range(terms)]
        for j in range(SLOTS):
            at = jnp.clip(8 * group - tops[j], -PAD, PROBE) + PAD
            inside = lane8 >= lefts[j]
            for c in range(terms):
                value = read(j, c, pl.ds(at, 8))
                left[c] = left[c] + jnp.where(inside, value, 0.0)
                right[c] = right[c] + jnp.where(inside, 0.0, value)
        return left, right

    def place_weights(group, carry):
        left, right = placed(lambda j, c, where: pw[j, where, :], group, 1)
        at = pl.ds(pl.multiple_of(8 * group, 8), 8)
        wsum[0, at, :] = left[0]
        wsum[1, at, :] = right[0]
        return carry

    edge = DEPTH // 8
    whole = (SIDE + 2 * DEPTH) // 8
    lax.fori_loop(0, edge, place_weights, 0)
    lax.fori_loop(whole - edge, whole, place_weights, 0)
    weights = [
        border_pair(
            wsum.at[:, pl.ds(0, DEPTH), :], wrecv.at[1],
            wsum.at[:, pl.ds(last, DEPTH), :], wrecv.at[0],
            b_recv,
        )
    ]
    lax.fori_loop(edge, whole - edge, place_weights, 0)

    loads[1].wait()

    def take_roots(pair, carry):
        for s in range(2):
            root[pair, :, s * PROBE : (s + 1) * PROBE] = jnp.sqrt(itn[2 * pair + s].astype(F32))
        return carry

    lax.fori_loop(0, SLOTS // 2, take_roots, 0)

    def coef(e, k):
        return spec[k, e]

    gram = [[None] * MATERIALS for _ in range(MATERIALS)]
    for k in range(MATERIALS):
        for l in range(k, MATERIALS):
            total = coef(0, k) * coef(0, l)
            for e in range(1, ENERGIES):
                total = total + coef(e, k) * coef(e, l)
            gram[k][l] = gram[l][k] = total
    squares = gram[0][0] + gram[1][1] + gram[2][2]

    for load in loads[2:]:
        load.wait()
    halo_bytes = block_pair(nrecv.at[0], halo_recv)
    wait_chip(halo_bytes)
    wait_link(halo_bytes)
    start_link(weights)
    start_chip(weights)

    lane = lax.broadcasted_iota(jnp.int32, (PROBE, PROBE), 1)

    def cut_windows(pair, state):
        exits = []
        for s in range(2):
            j = 2 * pair + s
            top = pl.ds(rows[0, j] + DEPTH, PROBE)
            inside = lane >= lefts[j]
            turn = lax.rem(PROBE - lefts[j], PROBE)
            view = [
                pltpu.roll(jnp.where(inside, ext[c, 0, top, :], ext[c, 1, top, :]), turn, 1) for c in range(2)
            ]
            pr, pi = prb[0], prb[1]
            exits.append(jnp.concatenate([pr * view[0] - pi * view[1], pr * view[1] + pi * view[0]], axis=1))
        state["exit"] = jnp.concatenate(exits, axis=0)

    def transform_rows(pair, state):
        state["x"] = swap_blocks(right_apply(state["exit"], tab[0], tab[1]))

    def transform_columns(pair, state):
        spectrum = left_apply(tab[2], tab[3], state["x"])
        sr, si = spectrum[:PROBE], spectrum[PROBE:]
        factor = root[pair] * lax.rsqrt(sr * sr + si * si + SMOOTH)
        state["x"] = jnp.concatenate([sr * factor, si * factor], axis=0)

    def restore_columns(pair, state):
        state["x"] = swap_blocks(left_apply(tab[0], tab[1], state["x"]))

    def restore_rows(pair, state):
        change = right_apply(state["x"], tab[2], tab[3]) - state["exit"]
        for s in range(2):
            j = 2 * pair + s
            cr = change[s * PROBE : (s + 1) * PROBE, :PROBE]
            ci = change[s * PROBE : (s + 1) * PROBE, PROBE:]
            pr, pi = prb[0], prb[1]
            turn = lax.rem(lefts[j], PROBE)
            part[j, 0, PAD : PAD + PROBE, :] = pltpu.roll(pr * cr + pi * ci, turn, 1)
            part[j, 1, PAD : PAD + PROBE, :] = pltpu.roll(pr * ci - pi * cr, turn, 1)

    states = [{} for _ in range(SLOTS // 2)]
    for stage in (cut_windows, transform_rows, transform_columns, restore_columns, restore_rows):
        for pair in range(SLOTS // 2):
            stage(pair, states[pair])

    def numerators(group):
        return placed(lambda j, c, where: part[j, c, where, :], group, 2)

    def place_parts(group, carry):
        left, right = numerators(group)
        at = pl.ds(pl.multiple_of(8 * group, 8), 8)
        for c in range(2):
            num[c, 0, at, :] = left[c]
            num[c, 1, at, :] = right[c]
        return carry

    def place_edge(side):
        lax.fori_loop(0, edge, lambda g, carry: place_parts(g + side * (whole - edge), carry), 0)

    def place_next(side):
        lax.fori_loop(0, edge, lambda g, carry: place_parts(g + edge + side * (whole - 3 * edge), carry), 0)

    borders = [
        border_pair(
            num.at[:, :, pl.ds(0, DEPTH), :], nrecv.at[1],
            num.at[:, :, pl.ds(last, DEPTH), :], nrecv.at[0],
            b_recv,
        )
    ]
    place_edge(link_side)
    start_link(borders)
    place_edge(chip_side)
    start_chip(borders)

    def renew(group, h, numerator, weight):
        at = pl.ds(pl.multiple_of(8 * group, 8), 8)
        own = pl.ds(pl.multiple_of(8 * group - DEPTH, 8), 8)
        inverse = 1.0 / (weight + DAMPING)
        new = [ext[c, h, at, :] + numerator[c] * inverse for c in range(2)]
        squared = new[0] * new[0] + new[1] * new[1] + SMOOTH
        scale = lax.rsqrt(squared)
        for c in range(2):
            unit[c, own, h * PROBE : (h + 1) * PROBE] = new[c] * scale
        att[own, h * PROBE : (h + 1) * PROBE] = -0.5 * jnp.log(squared)

    def inner_rows(group, carry):
        at = pl.ds(pl.multiple_of(8 * group, 8), 8)
        for h, sums in enumerate(numerators(group)):
            renew(group, h, sums, wsum[h, at, :])
        return carry

    def first_row(f, p):
        start = (DEPTH, chip_side * (SIDE - DEPTH), link_side * (SIDE - DEPTH))[p]
        return pl.multiple_of(start + PIECES[p] * f, 8)

    spots = [sum(PIECES[:p]) for p in range(len(PIECES))]

    def send_pixels(p):
        spot = pl.ds(spots[p], PIECES[p])
        for d in FAR_FIRST:
            remote(
                att.at[pl.ds(first_row(peer(d), p), PIECES[p]), :], gath.at[me, spot, :],
                a_send.at[0], a_recv.at[p], (tile, peer(d)),
            ).start()
        gath[me, spot, :] = att[pl.ds(first_row(me, p), PIECES[p]), :]

    lax.fori_loop(2 * edge, whole - 2 * edge, inner_rows, 0)
    send_pixels(0)
    place_next(chip_side)

    def device(planes, steps):
        return lax.rem(plane + planes, 2) * RING + lax.rem(y + steps + RING, RING)

    def hop(p, i, owner, to):
        at = pl.ds(first_row(owner, p), PIECES[p])
        return remote(maps.at[:, at, :], maps.at[:, at, :], g_send.at[0], g_recv.at[p + 2 if p > 0 else min(i, 2)], (tile, to))

    steps = ((1, 0), (0, 2), (0, 1), (0, -1), (1, 1), (1, -1), (1, 2))

    def hops(p):
        if p > 0:
            return [hop(p, i, me, device(*step)) for i, step in enumerate(steps)]
        return [hop(p, i, me, device(*step)) for i, step in enumerate(steps[:4])] + [
            hop(p, 4, device(1, 0), device(0, 1)),
            hop(p, 5, device(1, 0), device(0, -1)),
            hop(p, 6, device(0, 2), device(1, 0)),
        ]

    ways = [hops(p) for p in range(len(PIECES))]

    def decompose(p):
        block = att.at[pl.ds(0, (ENERGIES - 1) * PIECES[p]), :]
        remote(block, block, a_send.at[0], a_recv.at[p], (tile, peer(1))).wait_recv()
        spot = pl.ds(spots[p], PIECES[p])
        step = 1.0 / jnp.full((PIECES[p], SIDE), squares, F32)
        pulls = []
        for k in range(MATERIALS):
            total = coef(0, k) * gath[0, spot, :]
            for e in range(1, ENERGIES):
                total = total + coef(e, k) * gath[e, spot, :]
            pulls.append(total)
        levels = [jnp.maximum(step * pull, 0.0) for pull in pulls]
        for _ in range(NN_ITERS - 1):
            levels = [
                jnp.maximum(
                    levels[k]
                    - step
                    * (gram[k][0] * levels[0] + gram[k][1] * levels[1] + gram[k][2] * levels[2] - pulls[k]),
                    0.0,
                )
                for k in range(MATERIALS)
            ]
        for k in range(MATERIALS):
            maps[k, pl.ds(first_row(me, p), PIECES[p]), :] = levels[k]
        for i in (0, 1, 2, 3) if p == 0 else (6, 1, 4, 5, 2, 3, 0):
            ways[p][i].start()

    def outer_rows(side):
        base = edge + side * (whole - 3 * edge)

        def rows_of(group, carry):
            row = pl.ds(pl.multiple_of(8 * group, 8), 8)
            at = pl.ds(pl.multiple_of(8 * (group + base), 8), 8)
            for h in range(2):
                sums = [num[c, h, at, :] + nrecv[side, c, h, row, :] for c in range(2)]
                renew(group + base, h, sums, wsum[h, at, :] + wrecv[side, h, row, :])
            return carry

        lax.fori_loop(0, edge, rows_of, 0)

    border_bytes = block_pair(num.at[:, :, pl.ds(0, 3 * DEPTH // 2), :], b_recv)
    wait_chip(border_bytes)
    outer_rows(chip_side)
    send_pixels(1)
    place_next(link_side)

    own_spec = [spec[k, me] for k in range(MATERIALS)]

    def finish(p):
        at = pl.ds(first_row(0, p), ENERGIES * PIECES[p])
        thickness = own_spec[0] * maps[0, at, :] + own_spec[1] * maps[1, at, :] + own_spec[2] * maps[2, at, :]
        fade = jnp.exp(-thickness)
        for c in range(2):
            model[c, at, :] = unit[c, at, :] * fade

    def arrived(p, pieces):
        block = maps.at[:, pl.ds(0, pieces * PIECES[p]), :]
        remote(block, block, g_send.at[0], g_recv.at[p + 2], (tile, peer(1))).wait_recv()

    wait_link(border_bytes)
    outer_rows(link_side)
    send_pixels(2)
    decompose(0)
    decompose(1)
    ways[0][0].wait_recv()
    ways[0][4].start()
    ways[0][5].start()
    decompose(2)
    ways[0][1].wait_recv()
    ways[0][6].start()
    for p in range(len(PIECES)):
        arrived(p, ENERGIES - 3 if p == 0 else ENERGIES - 1)
        finish(p)

    sent_bytes = block_pair(num.at[:, :, pl.ds(0, 5 * DEPTH // 2), :], b_recv)
    start_link(sent_bytes, "wait_send")
    start_chip(sent_bytes, "wait_send")
    block = att.at[pl.ds(0, (ENERGIES - 1) * sum(PIECES)), :]
    remote(block, block, a_send.at[0], a_recv.at[0], (tile, peer(1))).wait_send()
    block = maps.at[:, pl.ds(0, (ENERGIES - 1) * sum(PIECES)), :]
    remote(block, block, g_send.at[0], g_recv.at[0], (tile, peer(1))).wait_send()


def put_out(maps, model, maps_out, model_out, sems):
    copies = [
        pltpu.make_async_copy(maps, maps_out, sems.at[0]),
        pltpu.make_async_copy(model, model_out.at[0], sems.at[1]),
    ]
    for copy in copies:
        copy.start()
    for copy in copies:
        copy.wait()


def stay(*arrays):
    return [pltpu.with_memory_space_constraint(array, pltpu.HBM) for array in arrays]


def body(object_tiles, probe_field, intensity, row_offsets, col_offsets, tile_counts, material_spectra):
    tables = jnp.asarray(dft_tables())
    anywhere = pl.BlockSpec(memory_space=pl.ANY)
    dma = pltpu.SemaphoreType.DMA
    vmem = pl.BlockSpec(memory_space=pltpu.VMEM)
    maps, model = pl.pallas_call(
        kernel,
        out_shape=(
            jax.ShapeDtypeStruct((MATERIALS, SIDE, SIDE), F32),
            jax.ShapeDtypeStruct((2, SIDE, SIDE), F32),
        ),
        in_specs=[anywhere] * 6 + [pl.BlockSpec(memory_space=pltpu.SMEM), anywhere],
        out_specs=(vmem, vmem),
        scratch_shapes=[
            pltpu.VMEM((2, 2, SIDE + 2 * DEPTH, PROBE), F32),
            pltpu.VMEM((2, PROBE, PROBE), F32),
            pltpu.VMEM((SLOTS, PROBE, PROBE), BF16),
            pltpu.VMEM((4, SIDE, SIDE), BF16),
            pltpu.VMEM((SLOTS // 2, PROBE, SIDE), F32),
            pltpu.VMEM((SLOTS, 2, PROBE + 2 * PAD, PROBE), F32),
            pltpu.VMEM((SLOTS, PROBE + 2 * PAD, PROBE), F32),
            pltpu.VMEM((2, SIDE + 2 * DEPTH, PROBE), F32),
            pltpu.VMEM((2, 2, DEPTH, PROBE), F32),
            pltpu.VMEM((2, 2, SIDE + 2 * DEPTH, PROBE), F32),
            pltpu.VMEM((2, 2, 2, DEPTH, PROBE), F32),
            pltpu.VMEM((2, SIDE, SIDE), F32),
            pltpu.VMEM((SIDE, SIDE), F32),
            pltpu.VMEM((ENERGIES, sum(PIECES), SIDE), F32),
            pltpu.SMEM((1, SLOTS), jnp.int32),
            pltpu.SMEM((1, SLOTS), jnp.int32),
            pltpu.SMEM((MATERIALS, ENERGIES), F32),
            dma((8,)), dma((2,)), dma((2,)), dma((2,)), dma((1,)), dma((len(PIECES),)), dma((1,)), dma((len(PIECES) + 2,)),
        ],
        compiler_params=pltpu.CompilerParams(collective_id=0, has_side_effects=True, vmem_limit_bytes=24 * 2**20),
        name="refine",
    )(*stay(object_tiles, probe_field, intensity, tables, row_offsets, col_offsets), tile_counts, *stay(material_spectra.T))
    return pl.pallas_call(
        put_out,
        out_shape=(
            jax.ShapeDtypeStruct((MATERIALS, SIDE, SIDE), F32),
            jax.ShapeDtypeStruct((1, 2, SIDE, SIDE), F32),
        ),
        in_specs=[vmem, vmem],
        out_specs=(anywhere, anywhere),
        scratch_shapes=[dma((2,))],
        compiler_params=pltpu.CompilerParams(vmem_limit_bytes=8 * 2**20),
        name="put_out",
    )(maps, model)


def solution(mesh):
    placed = (
        P("energy", None, "tile", None),
        P("energy", None, None, None),
        P("energy", "tile", None, None, None),
        P("tile", None),
        P("tile", None),
        P("tile"),
        P(),
    )
    return jax.shard_map(
        body,
        mesh=mesh,
        in_specs=placed,
        out_specs=(P(None, "tile", None), P("energy", None, "tile", None)),
        check_vma=False,
    )
```

```python
import jax
import jax.numpy as jnp
import ml_dtypes
import numpy as np
from jax import lax
from jax.experimental import pallas as pl
from jax.experimental.pallas import tpu as pltpu
from jax.sharding import PartitionSpec as P

PROBE = 128
NN_ITERS = 8
SMOOTH = 0.01
DAMPING = 0.5
SIDE = 256
DEPTH = 64
SLOTS = 8
PAD = 8
ENERGIES = 8
RING = 4
PIECES = (16, 8, 8)
FAR_FIRST = (6, 2, 5, 3, 7, 1, 4)
MATERIALS = 3

F32 = jnp.float32
BF16 = jnp.bfloat16
MESH = pl.DeviceIdType.MESH


def dft_tables():
    k = np.arange(PROBE)
    angles = 2.0 * np.pi / PROBE * (np.outer(k, k) % PROBE)
    cos, sin = np.cos(angles) / np.sqrt(PROBE), np.sin(angles) / np.sqrt(PROBE)
    table = np.block([[cos, -sin], [sin, cos]])
    out = []
    for full in (table, table.T):
        high = full.astype(np.float32).astype(ml_dtypes.bfloat16)
        low = (full - high.astype(np.float64)).astype(np.float32).astype(ml_dtypes.bfloat16)
        out += [high, low]
    return np.stack(out)


def halves(x):
    high = x.astype(BF16)
    return high, (x - high.astype(F32)).astype(BF16)


def mul(a, b):
    return jnp.dot(a, b, preferred_element_type=F32)


def right_apply(x, high, low):
    xh, xl = halves(x)
    return mul(xh, high) + mul(xl, high) + mul(xh, low)


def left_apply(high, low, x):
    xh, xl = halves(x)
    return mul(high, xh) + mul(high, xl) + mul(low, xh)


def swap_blocks(x):
    n = PROBE
    top = jnp.concatenate([x[:n, :n], x[n:, :n]], axis=1)
    bottom = jnp.concatenate([x[:n, n:], x[n:, n:]], axis=1)
    return jnp.concatenate([top, bottom], axis=0)


def kernel(
    obj, probe, inten, tables, rows_in, cols_in, count, spec_in,
    maps, model,
    ext, prb, itn, tab, root, part, pw, wsum, wrecv, num, nrecv, unit, att, gath, rows, cols, spec,
    load_sem, b_send, halo_recv, b_recv, a_send, a_recv, g_send, g_recv,
):
    tile = lax.axis_index("tile")
    me = lax.axis_index("energy")
    tiles = lax.axis_size("tile")
    plane, y = me // RING, lax.rem(me, RING)
    has_up, has_dn = tile > 0, tile < tiles - 1
    up, dn = tile - 1, tile + 1

    def peer(d):
        return lax.rem(me + d, ENERGIES)

    barrier = pltpu.get_barrier_semaphore()

    def greet(where):
        pl.semaphore_signal(barrier, inc=1, device_id=where, device_id_type=MESH)

    @pl.when(has_up)
    def _():
        greet((up, me))

    @pl.when(has_dn)
    def _():
        greet((dn, me))

    for d in range(1, ENERGIES):
        greet((tile, peer(d)))

    loads = [
        pltpu.make_async_copy(
            obj.at[0, :, :, pl.ds(h * PROBE, PROBE)], ext.at[:, h, pl.ds(DEPTH, SIDE), :], load_sem.at[h]
        )
        for h in range(2)
    ] + [
        pltpu.make_async_copy(probe.at[0], prb, load_sem.at[2]),
        pltpu.make_async_copy(inten.at[0, 0], itn, load_sem.at[3]),
        pltpu.make_async_copy(tables, tab, load_sem.at[4]),
    ]
    scalars = [
        pltpu.make_async_copy(rows_in, rows, load_sem.at[5]),
        pltpu.make_async_copy(cols_in, cols, load_sem.at[6]),
        pltpu.make_async_copy(spec_in, spec, load_sem.at[7]),
    ]
    for load in loads[:2] + scalars + loads[2:]:
        load.start()

    greeted = ENERGIES - 1 + has_up.astype(jnp.int32) + has_dn.astype(jnp.int32)
    pl.semaphore_wait(barrier, greeted)

    def remote(src, dst, send, recv, where):
        return pltpu.make_async_remote_copy(
            src_ref=src, dst_ref=dst, send_sem=send, recv_sem=recv, device_id=where, device_id_type=MESH
        )

    def border_pair(src_up, dst_up, src_dn, dst_dn, recv):
        return (
            remote(src_up, dst_up, b_send.at[0], recv.at[0], (up, me)),
            remote(src_dn, dst_dn, b_send.at[1], recv.at[1], (dn, me)),
        )

    def block_pair(block, recv):
        return [border_pair(block, block, block, block, recv)]

    odd = lax.rem(tile, 2) == 1
    even = jnp.logical_not(odd)
    link_up, link_dn = jnp.logical_and(even, has_up), jnp.logical_and(odd, has_dn)
    chip_side = 1 - lax.rem(tile, 2)
    link_side = 1 - chip_side

    def when(condition, action, copies):
        @pl.when(condition)
        def _():
            for copy in copies:
                getattr(copy, action)()

    def start_link(pairs, action="start"):
        when(link_up, action, [to_up for to_up, _ in pairs])
        when(link_dn, action, [to_dn for _, to_dn in pairs])

    def start_chip(pairs, action="start"):
        when(even, action, [to_dn for _, to_dn in pairs])
        when(odd, action, [to_up for to_up, _ in pairs])

    def wait_link(pairs):
        when(link_up, "wait_recv", [to_dn for _, to_dn in pairs])
        when(link_dn, "wait_recv", [to_up for to_up, _ in pairs])

    def wait_chip(pairs):
        when(even, "wait_recv", [to_up for to_up, _ in pairs])
        when(odd, "wait_recv", [to_dn for _, to_dn in pairs])

    last = SIDE + DEPTH
    for load in loads[:2]:
        load.wait()
    halo = [
        border_pair(
            ext.at[:, :, pl.ds(DEPTH, DEPTH), :], ext.at[:, :, pl.ds(last, DEPTH), :],
            ext.at[:, :, pl.ds(SIDE, DEPTH), :], ext.at[:, :, pl.ds(0, DEPTH), :],
            halo_recv,
        )
    ]
    start_link(halo)
    start_chip(halo)

    @pl.when(jnp.logical_not(has_up))
    def _():
        ext[:, :, 0:DEPTH, :] = jnp.zeros((2, 2, DEPTH, PROBE), F32)
        wrecv[0] = jnp.zeros((2, DEPTH, PROBE), F32)
        nrecv[0] = jnp.zeros((2, 2, DEPTH, PROBE), F32)

    @pl.when(jnp.logical_not(has_dn))
    def _():
        ext[:, :, last:, :] = jnp.zeros((2, 2, DEPTH, PROBE), F32)
        wrecv[1] = jnp.zeros((2, DEPTH, PROBE), F32)
        nrecv[1] = jnp.zeros((2, 2, DEPTH, PROBE), F32)

    part[:, :, 0:PAD, :] = jnp.zeros((SLOTS, 2, PAD, PROBE), F32)
    part[:, :, PAD + PROBE :, :] = jnp.zeros((SLOTS, 2, PAD, PROBE), F32)
    pw[:, 0:PAD, :] = jnp.zeros((SLOTS, PAD, PROBE), F32)
    pw[:, PAD + PROBE :, :] = jnp.zeros((SLOTS, PAD, PROBE), F32)

    for load in scalars:
        load.wait()
    live = count[0]
    lefts = [cols[0, j] for j in range(SLOTS)]
    tops = [jnp.where(j < live, rows[0, j] + DEPTH, 8 * SIDE) for j in range(SLOTS)]
    lane8 = lax.broadcasted_iota(jnp.int32, (8, PROBE), 1)

    loads[2].wait()
    probe_re, probe_im = prb[0], prb[1]
    power = probe_re * probe_re + probe_im * probe_im
    for j in range(SLOTS):
        pw[j, PAD : PAD + PROBE, :] = pltpu.roll(power, lax.rem(lefts[j], PROBE), 1)

    def placed(read, group, terms):
        left = [jnp.zeros((8, PROBE), F32) for _ in range(terms)]
        right = [jnp.zeros((8, PROBE), F32) for _ in range(terms)]
        for j in range(SLOTS):
            at = jnp.clip(8 * group - tops[j], -PAD, PROBE) + PAD
            inside = lane8 >= lefts[j]
            for c in range(terms):
                value = read(j, c, pl.ds(at, 8))
                left[c] = left[c] + jnp.where(inside, value, 0.0)
                right[c] = right[c] + jnp.where(inside, 0.0, value)
        return left, right

    def place_weights(group, carry):
        left, right = placed(lambda j, c, where: pw[j, where, :], group, 1)
        at = pl.ds(pl.multiple_of(8 * group, 8), 8)
        wsum[0, at, :] = left[0]
        wsum[1, at, :] = right[0]
        return carry

    edge = DEPTH // 8
    whole = (SIDE + 2 * DEPTH) // 8
    lax.fori_loop(0, edge, place_weights, 0)
    lax.fori_loop(whole - edge, whole, place_weights, 0)
    weights = [
        border_pair(
            wsum.at[:, pl.ds(0, DEPTH), :], wrecv.at[1],
            wsum.at[:, pl.ds(last, DEPTH), :], wrecv.at[0],
            b_recv,
        )
    ]
    lax.fori_loop(edge, whole - edge, place_weights, 0)

    loads[3].wait()

    def take_roots(pair, carry):
        for s in range(2):
            root[pair, :, s * PROBE : (s + 1) * PROBE] = jnp.sqrt(itn[2 * pair + s].astype(F32))
        return carry

    lax.fori_loop(0, SLOTS // 2, take_roots, 0)

    def coef(e, k):
        return spec[k, e]

    gram = [[None] * MATERIALS for _ in range(MATERIALS)]
    for k in range(MATERIALS):
        for l in range(k, MATERIALS):
            total = coef(0, k) * coef(0, l)
            for e in range(1, ENERGIES):
                total = total + coef(e, k) * coef(e, l)
            gram[k][l] = gram[l][k] = total
    squares = gram[0][0] + gram[1][1] + gram[2][2]

    loads[4].wait()
    wait_chip(halo)
    wait_link(halo)
    start_link(weights)
    start_chip(weights)

    lane = lax.broadcasted_iota(jnp.int32, (PROBE, PROBE), 1)

    def cut_windows(pair, state):
        exits = []
        for s in range(2):
            j = 2 * pair + s
            top = pl.ds(rows[0, j] + DEPTH, PROBE)
            inside = lane >= lefts[j]
            turn = lax.rem(PROBE - lefts[j], PROBE)
            view = [
                pltpu.roll(jnp.where(inside, ext[c, 0, top, :], ext[c, 1, top, :]), turn, 1) for c in range(2)
            ]
            pr, pi = prb[0], prb[1]
            exits.append(jnp.concatenate([pr * view[0] - pi * view[1], pr * view[1] + pi * view[0]], axis=1))
        state["exit"] = jnp.concatenate(exits, axis=0)

    def transform_rows(pair, state):
        state["x"] = swap_blocks(right_apply(state["exit"], tab[0], tab[1]))

    def transform_columns(pair, state):
        spectrum = left_apply(tab[2], tab[3], state["x"])
        sr, si = spectrum[:PROBE], spectrum[PROBE:]
        factor = root[pair] * lax.rsqrt(sr * sr + si * si + SMOOTH)
        state["x"] = jnp.concatenate([sr * factor, si * factor], axis=0)

    def restore_columns(pair, state):
        state["x"] = swap_blocks(left_apply(tab[0], tab[1], state["x"]))

    def restore_rows(pair, state):
        change = right_apply(state["x"], tab[2], tab[3]) - state["exit"]
        for s in range(2):
            j = 2 * pair + s
            cr = change[s * PROBE : (s + 1) * PROBE, :PROBE]
            ci = change[s * PROBE : (s + 1) * PROBE, PROBE:]
            pr, pi = prb[0], prb[1]
            turn = lax.rem(lefts[j], PROBE)
            part[j, 0, PAD : PAD + PROBE, :] = pltpu.roll(pr * cr + pi * ci, turn, 1)
            part[j, 1, PAD : PAD + PROBE, :] = pltpu.roll(pr * ci - pi * cr, turn, 1)

    states = [{} for _ in range(SLOTS // 2)]
    for stage in (cut_windows, transform_rows, transform_columns, restore_columns, restore_rows):
        for pair in range(SLOTS // 2):
            stage(pair, states[pair])

    def numerators(group):
        return placed(lambda j, c, where: part[j, c, where, :], group, 2)

    def place_parts(group, carry):
        left, right = numerators(group)
        at = pl.ds(pl.multiple_of(8 * group, 8), 8)
        for c in range(2):
            num[c, 0, at, :] = left[c]
            num[c, 1, at, :] = right[c]
        return carry

    def place_edge(side):
        lax.fori_loop(0, edge, lambda g, carry: place_parts(g + side * (whole - edge), carry), 0)

    def place_next(side):
        lax.fori_loop(0, edge, lambda g, carry: place_parts(g + edge + side * (whole - 3 * edge), carry), 0)

    borders = [
        border_pair(
            num.at[:, :, pl.ds(0, DEPTH), :], nrecv.at[1],
            num.at[:, :, pl.ds(last, DEPTH), :], nrecv.at[0],
            b_recv,
        )
    ]
    place_edge(link_side)
    start_link(borders)
    place_edge(chip_side)
    start_chip(borders)

    def renew(group, h, numerator, weight):
        at = pl.ds(pl.multiple_of(8 * group, 8), 8)
        own = pl.ds(pl.multiple_of(8 * group - DEPTH, 8), 8)
        inverse = 1.0 / (weight + DAMPING)
        new = [ext[c, h, at, :] + numerator[c] * inverse for c in range(2)]
        squared = new[0] * new[0] + new[1] * new[1] + SMOOTH
        scale = lax.rsqrt(squared)
        for c in range(2):
            unit[c, own, h * PROBE : (h + 1) * PROBE] = new[c] * scale
        att[own, h * PROBE : (h + 1) * PROBE] = -0.5 * jnp.log(squared)

    def inner_rows(group, carry):
        at = pl.ds(pl.multiple_of(8 * group, 8), 8)
        for h, sums in enumerate(numerators(group)):
            renew(group, h, sums, wsum[h, at, :])
        return carry

    def first_row(f, p):
        start = (DEPTH, chip_side * (SIDE - DEPTH), link_side * (SIDE - DEPTH))[p]
        return pl.multiple_of(start + PIECES[p] * f, 8)

    spots = [sum(PIECES[:p]) for p in range(len(PIECES))]

    def send_pixels(p):
        spot = pl.ds(spots[p], PIECES[p])
        for d in FAR_FIRST:
            remote(
                att.at[pl.ds(first_row(peer(d), p), PIECES[p]), :], gath.at[me, spot, :],
                a_send.at[0], a_recv.at[p], (tile, peer(d)),
            ).start()
        gath[me, spot, :] = att[pl.ds(first_row(me, p), PIECES[p]), :]

    lax.fori_loop(2 * edge, whole - 2 * edge, inner_rows, 0)
    send_pixels(0)
    place_next(chip_side)

    def device(planes, steps):
        return lax.rem(plane + planes, 2) * RING + lax.rem(y + steps + RING, RING)

    def hop(p, i, owner, to):
        at = pl.ds(first_row(owner, p), PIECES[p])
        return remote(maps.at[:, at, :], maps.at[:, at, :], g_send.at[0], g_recv.at[p + 2 if p > 0 else min(i, 2)], (tile, to))

    steps = ((1, 0), (0, 2), (0, 1), (0, -1), (1, 1), (1, -1), (1, 2))

    def hops(p):
        if p > 0:
            return [hop(p, i, me, device(*step)) for i, step in enumerate(steps)]
        return [hop(p, i, me, device(*step)) for i, step in enumerate(steps[:4])] + [
            hop(p, 4, device(1, 0), device(0, 1)),
            hop(p, 5, device(1, 0), device(0, -1)),
            hop(p, 6, device(0, 2), device(1, 0)),
        ]

    ways = [hops(p) for p in range(len(PIECES))]

    def decompose(p):
        block = att.at[pl.ds(0, (ENERGIES - 1) * PIECES[p]), :]
        remote(block, block, a_send.at[0], a_recv.at[p], (tile, peer(1))).wait_recv()
        spot = pl.ds(spots[p], PIECES[p])
        step = 1.0 / jnp.full((PIECES[p], SIDE), squares, F32)
        pulls = []
        for k in range(MATERIALS):
            total = coef(0, k) * gath[0, spot, :]
            for e in range(1, ENERGIES):
                total = total + coef(e, k) * gath[e, spot, :]
            pulls.append(total)
        levels = [jnp.maximum(step * pull, 0.0) for pull in pulls]
        for _ in range(NN_ITERS - 1):
            levels = [
                jnp.maximum(
                    levels[k]
                    - step
                    * (gram[k][0] * levels[0] + gram[k][1] * levels[1] + gram[k][2] * levels[2] - pulls[k]),
                    0.0,
                )
                for k in range(MATERIALS)
            ]
        for k in range(MATERIALS):
            maps[k, pl.ds(first_row(me, p), PIECES[p]), :] = levels[k]
        for i in (0, 1, 2, 3) if p == 0 else (6, 1, 4, 5, 2, 3, 0):
            ways[p][i].start()

    def outer_rows(side):
        base = edge + side * (whole - 3 * edge)

        def rows_of(group, carry):
            row = pl.ds(pl.multiple_of(8 * group, 8), 8)
            at = pl.ds(pl.multiple_of(8 * (group + base), 8), 8)
            for h in range(2):
                sums = [num[c, h, at, :] + nrecv[side, c, h, row, :] for c in range(2)]
                renew(group + base, h, sums, wsum[h, at, :] + wrecv[side, h, row, :])
            return carry

        lax.fori_loop(0, edge, rows_of, 0)

    border_bytes = block_pair(num.at[:, :, pl.ds(0, 3 * DEPTH // 2), :], b_recv)
    wait_chip(border_bytes)
    outer_rows(chip_side)
    send_pixels(1)
    place_next(link_side)

    own_spec = [spec[k, me] for k in range(MATERIALS)]

    def finish(p):
        at = pl.ds(first_row(0, p), ENERGIES * PIECES[p])
        thickness = own_spec[0] * maps[0, at, :] + own_spec[1] * maps[1, at, :] + own_spec[2] * maps[2, at, :]
        fade = jnp.exp(-thickness)
        for c in range(2):
            model[c, at, :] = unit[c, at, :] * fade

    def arrived(p, pieces):
        block = maps.at[:, pl.ds(0, pieces * PIECES[p]), :]
        remote(block, block, g_send.at[0], g_recv.at[p + 2], (tile, peer(1))).wait_recv()

    wait_link(border_bytes)
    outer_rows(link_side)
    send_pixels(2)
    decompose(0)
    decompose(1)
    ways[0][0].wait_recv()
    ways[0][4].start()
    ways[0][5].start()
    decompose(2)
    ways[0][1].wait_recv()
    ways[0][6].start()
    for p in range(len(PIECES)):
        arrived(p, ENERGIES - 3 if p == 0 else ENERGIES - 1)
        finish(p)

    sent_bytes = block_pair(num.at[:, :, pl.ds(0, 5 * DEPTH // 2), :], b_recv)
    start_link(sent_bytes, "wait_send")
    start_chip(sent_bytes, "wait_send")
    block = att.at[pl.ds(0, (ENERGIES - 1) * sum(PIECES)), :]
    remote(block, block, a_send.at[0], a_recv.at[0], (tile, peer(1))).wait_send()
    block = maps.at[:, pl.ds(0, (ENERGIES - 1) * sum(PIECES)), :]
    remote(block, block, g_send.at[0], g_recv.at[0], (tile, peer(1))).wait_send()


def put_out(maps, model, maps_out, model_out, sems):
    copies = [
        pltpu.make_async_copy(maps, maps_out, sems.at[0]),
        pltpu.make_async_copy(model, model_out.at[0], sems.at[1]),
    ]
    for copy in copies:
        copy.start()
    for copy in copies:
        copy.wait()


def stay(*arrays):
    return [pltpu.with_memory_space_constraint(array, pltpu.HBM) for array in arrays]


def body(object_tiles, probe_field, intensity, row_offsets, col_offsets, tile_counts, material_spectra):
    tables = jnp.asarray(dft_tables())
    anywhere = pl.BlockSpec(memory_space=pl.ANY)
    dma = pltpu.SemaphoreType.DMA
    vmem = pl.BlockSpec(memory_space=pltpu.VMEM)
    maps, model = pl.pallas_call(
        kernel,
        out_shape=(
            jax.ShapeDtypeStruct((MATERIALS, SIDE, SIDE), F32),
            jax.ShapeDtypeStruct((2, SIDE, SIDE), F32),
        ),
        in_specs=[anywhere] * 6 + [pl.BlockSpec(memory_space=pltpu.SMEM), anywhere],
        out_specs=(vmem, vmem),
        scratch_shapes=[
            pltpu.VMEM((2, 2, SIDE + 2 * DEPTH, PROBE), F32),
            pltpu.VMEM((2, PROBE, PROBE), F32),
            pltpu.VMEM((SLOTS, PROBE, PROBE), BF16),
            pltpu.VMEM((4, SIDE, SIDE), BF16),
            pltpu.VMEM((SLOTS // 2, PROBE, SIDE), F32),
            pltpu.VMEM((SLOTS, 2, PROBE + 2 * PAD, PROBE), F32),
            pltpu.VMEM((SLOTS, PROBE + 2 * PAD, PROBE), F32),
            pltpu.VMEM((2, SIDE + 2 * DEPTH, PROBE), F32),
            pltpu.VMEM((2, 2, DEPTH, PROBE), F32),
            pltpu.VMEM((2, 2, SIDE + 2 * DEPTH, PROBE), F32),
            pltpu.VMEM((2, 2, 2, DEPTH, PROBE), F32),
            pltpu.VMEM((2, SIDE, SIDE), F32),
            pltpu.VMEM((SIDE, SIDE), F32),
            pltpu.VMEM((ENERGIES, sum(PIECES), SIDE), F32),
            pltpu.SMEM((1, SLOTS), jnp.int32),
            pltpu.SMEM((1, SLOTS), jnp.int32),
            pltpu.SMEM((MATERIALS, ENERGIES), F32),
            dma((8,)), dma((2,)), dma((2,)), dma((2,)), dma((1,)), dma((len(PIECES),)), dma((1,)), dma((len(PIECES) + 2,)),
        ],
        compiler_params=pltpu.CompilerParams(collective_id=0, has_side_effects=True, vmem_limit_bytes=24 * 2**20),
        name="refine",
    )(*stay(object_tiles, probe_field, intensity, tables, row_offsets, col_offsets), tile_counts, *stay(material_spectra.T))
    return pl.pallas_call(
        put_out,
        out_shape=(
            jax.ShapeDtypeStruct((MATERIALS, SIDE, SIDE), F32),
            jax.ShapeDtypeStruct((1, 2, SIDE, SIDE), F32),
        ),
        in_specs=[vmem, vmem],
        out_specs=(anywhere, anywhere),
        scratch_shapes=[dma((2,))],
        compiler_params=pltpu.CompilerParams(vmem_limit_bytes=8 * 2**20),
        name="put_out",
    )(maps, model)


def solution(mesh):
    placed = (
        P("energy", None, "tile", None),
        P("energy", None, None, None),
        P("energy", "tile", None, None, None),
        P("tile", None),
        P("tile", None),
        P("tile"),
        P(),
    )
    return jax.shard_map(
        body,
        mesh=mesh,
        in_specs=placed,
        out_specs=(P(None, "tile", None), P("energy", None, "tile", None)),
        check_vma=False,
    )
```

```python
import jax
import jax.numpy as jnp
import ml_dtypes
import numpy as np
from jax import lax
from jax.experimental import pallas as pl
from jax.experimental.pallas import tpu as pltpu
from jax.sharding import PartitionSpec as P

PROBE = 128
NN_ITERS = 8
SMOOTH = 0.01
DAMPING = 0.5
SIDE = 256
DEPTH = 64
SLOTS = 8
PAD = 8
ENERGIES = 8
RING = 4
PIECES = (16, 8, 8)
FAR_FIRST = (6, 2, 5, 3, 7, 1, 4)
MATERIALS = 3

F32 = jnp.float32
BF16 = jnp.bfloat16
MESH = pl.DeviceIdType.MESH


def dft_tables():
    k = np.arange(PROBE)
    angles = 2.0 * np.pi / PROBE * (np.outer(k, k) % PROBE)
    cos, sin = np.cos(angles) / np.sqrt(PROBE), np.sin(angles) / np.sqrt(PROBE)
    table = np.block([[cos, -sin], [sin, cos]])
    out = []
    for full in (table, table.T):
        high = full.astype(np.float32).astype(ml_dtypes.bfloat16)
        low = (full - high.astype(np.float64)).astype(np.float32).astype(ml_dtypes.bfloat16)
        out += [high, low]
    return np.stack(out)


def halves(x):
    high = x.astype(BF16)
    return high, (x - high.astype(F32)).astype(BF16)


def mul(a, b):
    return jnp.dot(a, b, preferred_element_type=F32)


def right_apply(x, high, low):
    xh, xl = halves(x)
    return mul(xh, high) + mul(xl, high) + mul(xh, low)


def left_apply(high, low, x):
    xh, xl = halves(x)
    return mul(high, xh) + mul(high, xl) + mul(low, xh)


def swap_blocks(x):
    n = PROBE
    top = jnp.concatenate([x[:n, :n], x[n:, :n]], axis=1)
    bottom = jnp.concatenate([x[:n, n:], x[n:, n:]], axis=1)
    return jnp.concatenate([top, bottom], axis=0)


def kernel(
    obj, probe, inten, tables, rows_in, cols_in, count, spec_in,
    maps, model,
    ext, prb, itn, tab, root, part, pw, wsum, wrecv, num, nrecv, unit, att, gath, rows, cols, spec,
    load_sem, b_send, halo_recv, b_recv, a_send, a_recv, g_send, g_recv,
):
    tile = lax.axis_index("tile")
    me = lax.axis_index("energy")
    tiles = lax.axis_size("tile")
    plane, y = me // RING, lax.rem(me, RING)
    has_up, has_dn = tile > 0, tile < tiles - 1
    up, dn = tile - 1, tile + 1

    def peer(d):
        return lax.rem(me + d, ENERGIES)

    barrier = pltpu.get_barrier_semaphore()

    def greet(where):
        pl.semaphore_signal(barrier, inc=1, device_id=where, device_id_type=MESH)

    @pl.when(has_up)
    def _():
        greet((up, me))

    @pl.when(has_dn)
    def _():
        greet((dn, me))

    for d in range(1, ENERGIES):
        greet((tile, peer(d)))

    loads = [
        pltpu.make_async_copy(
            obj.at[0, :, :, pl.ds(h * PROBE, PROBE)], ext.at[:, h, pl.ds(DEPTH, SIDE), :], load_sem.at[h]
        )
        for h in range(2)
    ] + [
        pltpu.make_async_copy(probe.at[0], prb, load_sem.at[2]),
        pltpu.make_async_copy(inten.at[0, 0], itn, load_sem.at[3]),
        pltpu.make_async_copy(tables, tab, load_sem.at[4]),
    ]
    scalars = [
        pltpu.make_async_copy(rows_in, rows, load_sem.at[5]),
        pltpu.make_async_copy(cols_in, cols, load_sem.at[6]),
        pltpu.make_async_copy(spec_in, spec, load_sem.at[7]),
    ]
    for load in loads[:2] + scalars + loads[2:]:
        load.start()

    greeted = ENERGIES - 1 + has_up.astype(jnp.int32) + has_dn.astype(jnp.int32)
    pl.semaphore_wait(barrier, greeted)

    def remote(src, dst, send, recv, where):
        return pltpu.make_async_remote_copy(
            src_ref=src, dst_ref=dst, send_sem=send, recv_sem=recv, device_id=where, device_id_type=MESH
        )

    def border_pair(src_up, dst_up, src_dn, dst_dn, recv):
        return (
            remote(src_up, dst_up, b_send.at[0], recv.at[0], (up, me)),
            remote(src_dn, dst_dn, b_send.at[1], recv.at[1], (dn, me)),
        )

    def block_pair(block, recv):
        return [border_pair(block, block, block, block, recv)]

    odd = lax.rem(tile, 2) == 1
    even = jnp.logical_not(odd)
    link_up, link_dn = jnp.logical_and(even, has_up), jnp.logical_and(odd, has_dn)
    chip_side = 1 - lax.rem(tile, 2)
    link_side = 1 - chip_side

    def when(condition, action, copies):
        @pl.when(condition)
        def _():
            for copy in copies:
                getattr(copy, action)()

    def start_link(pairs, action="start"):
        when(link_up, action, [to_up for to_up, _ in pairs])
        when(link_dn, action, [to_dn for _, to_dn in pairs])

    def start_chip(pairs, action="start"):
        when(even, action, [to_dn for _, to_dn in pairs])
        when(odd, action, [to_up for to_up, _ in pairs])

    def wait_link(pairs):
        when(link_up, "wait_recv", [to_dn for _, to_dn in pairs])
        when(link_dn, "wait_recv", [to_up for to_up, _ in pairs])

    def wait_chip(pairs):
        when(even, "wait_recv", [to_up for to_up, _ in pairs])
        when(odd, "wait_recv", [to_dn for _, to_dn in pairs])

    last = SIDE + DEPTH
    for load in loads[:2]:
        load.wait()
    halo = [
        border_pair(
            ext.at[:, :, pl.ds(DEPTH, DEPTH), :], ext.at[:, :, pl.ds(last, DEPTH), :],
            ext.at[:, :, pl.ds(SIDE, DEPTH), :], ext.at[:, :, pl.ds(0, DEPTH), :],
            halo_recv,
        )
    ]
    start_link(halo)
    start_chip(halo)

    @pl.when(jnp.logical_not(has_up))
    def _():
        ext[:, :, 0:DEPTH, :] = jnp.zeros((2, 2, DEPTH, PROBE), F32)
        wrecv[0] = jnp.zeros((2, DEPTH, PROBE), F32)
        nrecv[0] = jnp.zeros((2, 2, DEPTH, PROBE), F32)

    @pl.when(jnp.logical_not(has_dn))
    def _():
        ext[:, :, last:, :] = jnp.zeros((2, 2, DEPTH, PROBE), F32)
        wrecv[1] = jnp.zeros((2, DEPTH, PROBE), F32)
        nrecv[1] = jnp.zeros((2, 2, DEPTH, PROBE), F32)

    part[:, :, 0:PAD, :] = jnp.zeros((SLOTS, 2, PAD, PROBE), F32)
    part[:, :, PAD + PROBE :, :] = jnp.zeros((SLOTS, 2, PAD, PROBE), F32)
    pw[:, 0:PAD, :] = jnp.zeros((SLOTS, PAD, PROBE), F32)
    pw[:, PAD + PROBE :, :] = jnp.zeros((SLOTS, PAD, PROBE), F32)

    for load in scalars:
        load.wait()
    live = count[0]
    lefts = [cols[0, j] for j in range(SLOTS)]
    tops = [jnp.where(j < live, rows[0, j] + DEPTH, 8 * SIDE) for j in range(SLOTS)]
    lane8 = lax.broadcasted_iota(jnp.int32, (8, PROBE), 1)

    loads[2].wait()
    probe_re, probe_im = prb[0], prb[1]
    power = probe_re * probe_re + probe_im * probe_im
    for j in range(SLOTS):
        pw[j, PAD : PAD + PROBE, :] = pltpu.roll(power, lax.rem(lefts[j], PROBE), 1)

    def placed(read, group, terms):
        left = [jnp.zeros((8, PROBE), F32) for _ in range(terms)]
        right = [jnp.zeros((8, PROBE), F32) for _ in range(terms)]
        for j in range(SLOTS):
            at = jnp.clip(8 * group - tops[j], -PAD, PROBE) + PAD
            inside = lane8 >= lefts[j]
            for c in range(terms):
                value = read(j, c, pl.ds(at, 8))
                left[c] = left[c] + jnp.where(inside, value, 0.0)
                right[c] = right[c] + jnp.where(inside, 0.0, value)
        return left, right

    def place_weights(group, carry):
        left, right = placed(lambda j, c, where: pw[j, where, :], group, 1)
        at = pl.ds(pl.multiple_of(8 * group, 8), 8)
        wsum[0, at, :] = left[0]
        wsum[1, at, :] = right[0]
        return carry

    edge = DEPTH // 8
    whole = (SIDE + 2 * DEPTH) // 8
    lax.fori_loop(0, edge, place_weights, 0, unroll=4)
    lax.fori_loop(whole - edge, whole, place_weights, 0, unroll=4)
    weights = [
        border_pair(
            wsum.at[:, pl.ds(0, DEPTH), :], wrecv.at[1],
            wsum.at[:, pl.ds(last, DEPTH), :], wrecv.at[0],
            b_recv,
        )
    ]
    lax.fori_loop(edge, whole - edge, place_weights, 0, unroll=4)

    loads[3].wait()

    def take_roots(pair, carry):
        for s in range(2):
            root[pair, :, s * PROBE : (s + 1) * PROBE] = jnp.sqrt(itn[2 * pair + s].astype(F32))
        return carry

    lax.fori_loop(0, SLOTS // 2, take_roots, 0)

    def coef(e, k):
        return spec[k, e]

    gram = [[None] * MATERIALS for _ in range(MATERIALS)]
    for k in range(MATERIALS):
        for l in range(k, MATERIALS):
            total = coef(0, k) * coef(0, l)
            for e in range(1, ENERGIES):
                total = total + coef(e, k) * coef(e, l)
            gram[k][l] = gram[l][k] = total
    squares = gram[0][0] + gram[1][1] + gram[2][2]

    loads[4].wait()
    wait_chip(halo)
    wait_link(halo)
    start_link(weights)
    start_chip(weights)

    lane = lax.broadcasted_iota(jnp.int32, (PROBE, PROBE), 1)

    def cut_windows(pair, state):
        exits = []
        for s in range(2):
            j = 2 * pair + s
            top = pl.ds(rows[0, j] + DEPTH, PROBE)
            inside = lane >= lefts[j]
            turn = lax.rem(PROBE - lefts[j], PROBE)
            view = [
                pltpu.roll(jnp.where(inside, ext[c, 0, top, :], ext[c, 1, top, :]), turn, 1) for c in range(2)
            ]
            pr, pi = prb[0], prb[1]
            exits.append(jnp.concatenate([pr * view[0] - pi * view[1], pr * view[1] + pi * view[0]], axis=1))
        state["exit"] = jnp.concatenate(exits, axis=0)

    def transform_rows(pair, state):
        state["x"] = swap_blocks(right_apply(state["exit"], tab[0], tab[1]))

    def transform_columns(pair, state):
        spectrum = left_apply(tab[2], tab[3], state["x"])
        sr, si = spectrum[:PROBE], spectrum[PROBE:]
        factor = root[pair] * lax.rsqrt(sr * sr + si * si + SMOOTH)
        state["x"] = jnp.concatenate([sr * factor, si * factor], axis=0)

    def restore_columns(pair, state):
        state["x"] = swap_blocks(left_apply(tab[0], tab[1], state["x"]))

    def restore_rows(pair, state):
        change = right_apply(state["x"], tab[2], tab[3]) - state["exit"]
        for s in range(2):
            j = 2 * pair + s
            cr = change[s * PROBE : (s + 1) * PROBE, :PROBE]
            ci = change[s * PROBE : (s + 1) * PROBE, PROBE:]
            pr, pi = prb[0], prb[1]
            turn = lax.rem(lefts[j], PROBE)
            part[j, 0, PAD : PAD + PROBE, :] = pltpu.roll(pr * cr + pi * ci, turn, 1)
            part[j, 1, PAD : PAD + PROBE, :] = pltpu.roll(pr * ci - pi * cr, turn, 1)

    states = [{} for _ in range(SLOTS // 2)]
    for stage in (cut_windows, transform_rows, transform_columns, restore_columns, restore_rows):
        for pair in range(SLOTS // 2):
            stage(pair, states[pair])

    def numerators(group):
        return placed(lambda j, c, where: part[j, c, where, :], group, 2)

    def place_parts(group, carry):
        left, right = numerators(group)
        at = pl.ds(pl.multiple_of(8 * group, 8), 8)
        for c in range(2):
            num[c, 0, at, :] = left[c]
            num[c, 1, at, :] = right[c]
        return carry

    def place_edge(side):
        lax.fori_loop(0, edge, lambda g, carry: place_parts(g + side * (whole - edge), carry), 0, unroll=8)

    def place_next(side):
        lax.fori_loop(0, edge, lambda g, carry: place_parts(g + edge + side * (whole - 3 * edge), carry), 0, unroll=8)

    borders = [
        border_pair(
            num.at[:, :, pl.ds(0, DEPTH), :], nrecv.at[1],
            num.at[:, :, pl.ds(last, DEPTH), :], nrecv.at[0],
            b_recv,
        )
    ]
    place_edge(link_side)
    start_link(borders)
    place_edge(chip_side)
    start_chip(borders)

    def renew(group, h, numerator, weight):
        at = pl.ds(pl.multiple_of(8 * group, 8), 8)
        own = pl.ds(pl.multiple_of(8 * group - DEPTH, 8), 8)
        inverse = 1.0 / (weight + DAMPING)
        new = [ext[c, h, at, :] + numerator[c] * inverse for c in range(2)]
        squared = new[0] * new[0] + new[1] * new[1] + SMOOTH
        scale = lax.rsqrt(squared)
        for c in range(2):
            unit[c, own, h * PROBE : (h + 1) * PROBE] = new[c] * scale
        att[own, h * PROBE : (h + 1) * PROBE] = -0.5 * jnp.log(squared)

    def inner_rows(group, carry):
        at = pl.ds(pl.multiple_of(8 * group, 8), 8)
        for h, sums in enumerate(numerators(group)):
            renew(group, h, sums, wsum[h, at, :])
        return carry

    def first_row(f, p):
        start = (DEPTH, chip_side * (SIDE - DEPTH), link_side * (SIDE - DEPTH))[p]
        return pl.multiple_of(start + PIECES[p] * f, 8)

    spots = [sum(PIECES[:p]) for p in range(len(PIECES))]

    def send_pixels(p):
        spot = pl.ds(spots[p], PIECES[p])
        for d in FAR_FIRST:
            remote(
                att.at[pl.ds(first_row(peer(d), p), PIECES[p]), :], gath.at[me, spot, :],
                a_send.at[0], a_recv.at[p], (tile, peer(d)),
            ).start()
        gath[me, spot, :] = att[pl.ds(first_row(me, p), PIECES[p]), :]

    lax.fori_loop(2 * edge, whole - 2 * edge, inner_rows, 0, unroll=8)
    send_pixels(0)
    place_next(chip_side)

    def device(planes, steps):
        return lax.rem(plane + planes, 2) * RING + lax.rem(y + steps + RING, RING)

    def hop(p, i, owner, to):
        at = pl.ds(first_row(owner, p), PIECES[p])
        return remote(maps.at[:, at, :], maps.at[:, at, :], g_send.at[0], g_recv.at[p + 2 if p > 0 else min(i, 2)], (tile, to))

    steps = ((1, 0), (0, 2), (0, 1), (0, -1), (1, 1), (1, -1), (1, 2))

    def hops(p):
        if p > 0:
            return [hop(p, i, me, device(*step)) for i, step in enumerate(steps)]
        return [hop(p, i, me, device(*step)) for i, step in enumerate(steps[:4])] + [
            hop(p, 4, device(1, 0), device(0, 1)),
            hop(p, 5, device(1, 0), device(0, -1)),
            hop(p, 6, device(0, 2), device(1, 0)),
        ]

    ways = [hops(p) for p in range(len(PIECES))]

    def decompose(p):
        block = att.at[pl.ds(0, (ENERGIES - 1) * PIECES[p]), :]
        remote(block, block, a_send.at[0], a_recv.at[p], (tile, peer(1))).wait_recv()
        spot = pl.ds(spots[p], PIECES[p])
        step = 1.0 / jnp.full((PIECES[p], SIDE), squares, F32)
        pulls = []
        for k in range(MATERIALS):
            total = coef(0, k) * gath[0, spot, :]
            for e in range(1, ENERGIES):
                total = total + coef(e, k) * gath[e, spot, :]
            pulls.append(total)
        levels = [jnp.maximum(step * pull, 0.0) for pull in pulls]
        for _ in range(NN_ITERS - 1):
            levels = [
                jnp.maximum(
                    levels[k]
                    - step
                    * (gram[k][0] * levels[0] + gram[k][1] * levels[1] + gram[k][2] * levels[2] - pulls[k]),
                    0.0,
                )
                for k in range(MATERIALS)
            ]
        for k in range(MATERIALS):
            maps[k, pl.ds(first_row(me, p), PIECES[p]), :] = levels[k]
        for i in (0, 1, 2, 3) if p == 0 else (6, 1, 4, 5, 2, 3, 0):
            ways[p][i].start()

    def outer_rows(side):
        base = edge + side * (whole - 3 * edge)

        def rows_of(group, carry):
            row = pl.ds(pl.multiple_of(8 * group, 8), 8)
            at = pl.ds(pl.multiple_of(8 * (group + base), 8), 8)
            for h in range(2):
                sums = [num[c, h, at, :] + nrecv[side, c, h, row, :] for c in range(2)]
                renew(group + base, h, sums, wsum[h, at, :] + wrecv[side, h, row, :])
            return carry

        lax.fori_loop(0, edge, rows_of, 0, unroll=8)

    border_bytes = block_pair(num.at[:, :, pl.ds(0, 3 * DEPTH // 2), :], b_recv)
    wait_chip(border_bytes)
    outer_rows(chip_side)
    send_pixels(1)
    place_next(link_side)

    own_spec = [spec[k, me] for k in range(MATERIALS)]

    def finish(p):
        at = pl.ds(first_row(0, p), ENERGIES * PIECES[p])
        thickness = own_spec[0] * maps[0, at, :] + own_spec[1] * maps[1, at, :] + own_spec[2] * maps[2, at, :]
        fade = jnp.exp(-thickness)
        for c in range(2):
            model[c, at, :] = unit[c, at, :] * fade

    def arrived(p, pieces):
        block = maps.at[:, pl.ds(0, pieces * PIECES[p]), :]
        remote(block, block, g_send.at[0], g_recv.at[p + 2], (tile, peer(1))).wait_recv()

    wait_link(border_bytes)
    outer_rows(link_side)
    send_pixels(2)
    decompose(0)
    decompose(1)
    ways[0][0].wait_recv()
    ways[0][4].start()
    ways[0][5].start()
    decompose(2)
    ways[0][1].wait_recv()
    ways[0][6].start()
    for p in range(len(PIECES)):
        arrived(p, ENERGIES - 3 if p == 0 else ENERGIES - 1)
        finish(p)

    sent_bytes = block_pair(num.at[:, :, pl.ds(0, 5 * DEPTH // 2), :], b_recv)
    start_link(sent_bytes, "wait_send")
    start_chip(sent_bytes, "wait_send")
    block = att.at[pl.ds(0, (ENERGIES - 1) * sum(PIECES)), :]
    remote(block, block, a_send.at[0], a_recv.at[0], (tile, peer(1))).wait_send()
    block = maps.at[:, pl.ds(0, (ENERGIES - 1) * sum(PIECES)), :]
    remote(block, block, g_send.at[0], g_recv.at[0], (tile, peer(1))).wait_send()


def put_out(maps, model, maps_out, model_out, sems):
    copies = [
        pltpu.make_async_copy(maps, maps_out, sems.at[0]),
        pltpu.make_async_copy(model, model_out.at[0], sems.at[1]),
    ]
    for copy in copies:
        copy.start()
    for copy in copies:
        copy.wait()


def stay(*arrays):
    return [pltpu.with_memory_space_constraint(array, pltpu.HBM) for array in arrays]


def body(object_tiles, probe_field, intensity, row_offsets, col_offsets, tile_counts, material_spectra):
    tables = jnp.asarray(dft_tables())
    anywhere = pl.BlockSpec(memory_space=pl.ANY)
    dma = pltpu.SemaphoreType.DMA
    vmem = pl.BlockSpec(memory_space=pltpu.VMEM)
    maps, model = pl.pallas_call(
        kernel,
        out_shape=(
            jax.ShapeDtypeStruct((MATERIALS, SIDE, SIDE), F32),
            jax.ShapeDtypeStruct((2, SIDE, SIDE), F32),
        ),
        in_specs=[anywhere] * 6 + [pl.BlockSpec(memory_space=pltpu.SMEM), anywhere],
        out_specs=(vmem, vmem),
        scratch_shapes=[
            pltpu.VMEM((2, 2, SIDE + 2 * DEPTH, PROBE), F32),
            pltpu.VMEM((2, PROBE, PROBE), F32),
            pltpu.VMEM((SLOTS, PROBE, PROBE), BF16),
            pltpu.VMEM((4, SIDE, SIDE), BF16),
            pltpu.VMEM((SLOTS // 2, PROBE, SIDE), F32),
            pltpu.VMEM((SLOTS, 2, PROBE + 2 * PAD, PROBE), F32),
            pltpu.VMEM((SLOTS, PROBE + 2 * PAD, PROBE), F32),
            pltpu.VMEM((2, SIDE + 2 * DEPTH, PROBE), F32),
            pltpu.VMEM((2, 2, DEPTH, PROBE), F32),
            pltpu.VMEM((2, 2, SIDE + 2 * DEPTH, PROBE), F32),
            pltpu.VMEM((2, 2, 2, DEPTH, PROBE), F32),
            pltpu.VMEM((2, SIDE, SIDE), F32),
            pltpu.VMEM((SIDE, SIDE), F32),
            pltpu.VMEM((ENERGIES, sum(PIECES), SIDE), F32),
            pltpu.SMEM((1, SLOTS), jnp.int32),
            pltpu.SMEM((1, SLOTS), jnp.int32),
            pltpu.SMEM((MATERIALS, ENERGIES), F32),
            dma((8,)), dma((2,)), dma((2,)), dma((2,)), dma((1,)), dma((len(PIECES),)), dma((1,)), dma((len(PIECES) + 2,)),
        ],
        compiler_params=pltpu.CompilerParams(collective_id=0, has_side_effects=True, vmem_limit_bytes=24 * 2**20),
        name="refine",
    )(*stay(object_tiles, probe_field, intensity, tables, row_offsets, col_offsets), tile_counts, *stay(material_spectra.T))
    return pl.pallas_call(
        put_out,
        out_shape=(
            jax.ShapeDtypeStruct((MATERIALS, SIDE, SIDE), F32),
            jax.ShapeDtypeStruct((1, 2, SIDE, SIDE), F32),
        ),
        in_specs=[vmem, vmem],
        out_specs=(anywhere, anywhere),
        scratch_shapes=[dma((2,))],
        compiler_params=pltpu.CompilerParams(vmem_limit_bytes=8 * 2**20),
        name="put_out",
    )(maps, model)


def solution(mesh):
    placed = (
        P("energy", None, "tile", None),
        P("energy", None, None, None),
        P("energy", "tile", None, None, None),
        P("tile", None),
        P("tile", None),
        P("tile"),
        P(),
    )
    return jax.shard_map(
        body,
        mesh=mesh,
        in_specs=placed,
        out_specs=(P(None, "tile", None), P("energy", None, "tile", None)),
        check_vma=False,
    )
```

```python
import jax
import jax.numpy as jnp
import ml_dtypes
import numpy as np
from jax import lax
from jax.experimental import pallas as pl
from jax.experimental.pallas import tpu as pltpu
from jax.sharding import PartitionSpec as P

PROBE = 128
NN_ITERS = 8
SMOOTH = 0.01
DAMPING = 0.5
SIDE = 256
DEPTH = 64
SLOTS = 8
PAD = 8
ENERGIES = 8
RING = 4
PIECES = (16, 8, 8)
FAR_FIRST = (6, 2, 5, 3, 7, 1, 4)
MATERIALS = 3

F32 = jnp.float32
BF16 = jnp.bfloat16
MESH = pl.DeviceIdType.MESH


def dft_tables():
    k = np.arange(PROBE)
    angles = 2.0 * np.pi / PROBE * (np.outer(k, k) % PROBE)
    cos, sin = np.cos(angles) / np.sqrt(PROBE), np.sin(angles) / np.sqrt(PROBE)
    table = np.block([[cos, -sin], [sin, cos]])
    out = []
    for full in (table, table.T):
        high = full.astype(np.float32).astype(ml_dtypes.bfloat16)
        low = (full - high.astype(np.float64)).astype(np.float32).astype(ml_dtypes.bfloat16)
        out += [high, low]
    return np.stack(out)


def halves(x):
    high = x.astype(BF16)
    return high, (x - high.astype(F32)).astype(BF16)


def mul(a, b):
    return jnp.dot(a, b, preferred_element_type=F32)


def right_apply(x, high, low):
    xh, xl = halves(x)
    return mul(xh, high) + mul(xl, high) + mul(xh, low)


def left_apply(high, low, x):
    xh, xl = halves(x)
    return mul(high, xh) + mul(high, xl) + mul(low, xh)


def swap_blocks(x):
    n = PROBE
    top = jnp.concatenate([x[:n, :n], x[n:, :n]], axis=1)
    bottom = jnp.concatenate([x[:n, n:], x[n:, n:]], axis=1)
    return jnp.concatenate([top, bottom], axis=0)


def kernel(
    obj, probe, inten, tables, rows_in, cols_in, count, spec_in,
    maps, model,
    ext, prb, itn, tab, root, part, pw, wsum, wrecv, num, nrecv, unit, att, gath, rows, cols, spec,
    load_sem, b_send, halo_recv, b_recv, a_send, a_recv, g_send, g_recv,
):
    tile = lax.axis_index("tile")
    me = lax.axis_index("energy")
    tiles = lax.axis_size("tile")
    plane, y = me // RING, lax.rem(me, RING)
    has_up, has_dn = tile > 0, tile < tiles - 1
    up, dn = lax.rem(tile + tiles - 1, tiles), lax.rem(tile + 1, tiles)

    def peer(d):
        return lax.rem(me + d, ENERGIES)

    barrier = pltpu.get_barrier_semaphore()

    def greet(where):
        pl.semaphore_signal(barrier, inc=1, device_id=where, device_id_type=MESH)

    @pl.when(has_up)
    def _():
        greet((up, me))

    @pl.when(has_dn)
    def _():
        greet((dn, me))

    for d in range(1, ENERGIES):
        greet((tile, peer(d)))

    loads = [
        pltpu.make_async_copy(
            obj.at[0, :, :, pl.ds(h * PROBE, PROBE)], ext.at[:, h, pl.ds(DEPTH, SIDE), :], load_sem.at[h]
        )
        for h in range(2)
    ] + [
        pltpu.make_async_copy(probe.at[0], prb, load_sem.at[2]),
        pltpu.make_async_copy(inten.at[0, 0], itn, load_sem.at[3]),
        pltpu.make_async_copy(tables, tab, load_sem.at[4]),
    ]
    scalars = [
        pltpu.make_async_copy(rows_in, rows, load_sem.at[5]),
        pltpu.make_async_copy(cols_in, cols, load_sem.at[6]),
        pltpu.make_async_copy(spec_in, spec, load_sem.at[7]),
    ]
    for load in loads[:2] + scalars + loads[2:]:
        load.start()

    greeted = ENERGIES - 1 + has_up.astype(jnp.int32) + has_dn.astype(jnp.int32)
    pl.semaphore_wait(barrier, greeted)

    def remote(src, dst, send, recv, where):
        return pltpu.make_async_remote_copy(
            src_ref=src, dst_ref=dst, send_sem=send, recv_sem=recv, device_id=where, device_id_type=MESH
        )

    def border_pair(src_up, dst_up, src_dn, dst_dn, recv):
        return (
            remote(src_up, dst_up, b_send.at[0], recv.at[0], (up, me)),
            remote(src_dn, dst_dn, b_send.at[1], recv.at[1], (dn, me)),
        )

    def block_pair(block, recv):
        return [border_pair(block, block, block, block, recv)]

    odd = lax.rem(tile, 2) == 1
    even = jnp.logical_not(odd)
    link_up, link_dn = jnp.logical_and(even, has_up), jnp.logical_and(odd, has_dn)
    chip_side = 1 - lax.rem(tile, 2)
    link_side = 1 - chip_side

    def when(condition, action, copies):
        @pl.when(condition)
        def _():
            for copy in copies:
                getattr(copy, action)()

    def start_link(pairs, action="start"):
        when(link_up, action, [to_up for to_up, _ in pairs])
        when(link_dn, action, [to_dn for _, to_dn in pairs])

    def start_chip(pairs, action="start"):
        when(even, action, [to_dn for _, to_dn in pairs])
        when(odd, action, [to_up for to_up, _ in pairs])

    def wait_link(pairs):
        when(link_up, "wait_recv", [to_dn for _, to_dn in pairs])
        when(link_dn, "wait_recv", [to_up for to_up, _ in pairs])

    def wait_chip(pairs):
        when(even, "wait_recv", [to_up for to_up, _ in pairs])
        when(odd, "wait_recv", [to_dn for _, to_dn in pairs])

    last = SIDE + DEPTH
    for load in loads[:2]:
        load.wait()
    halo = [
        border_pair(
            ext.at[:, :, pl.ds(DEPTH, DEPTH), :], ext.at[:, :, pl.ds(last, DEPTH), :],
            ext.at[:, :, pl.ds(SIDE, DEPTH), :], ext.at[:, :, pl.ds(0, DEPTH), :],
            halo_recv,
        )
    ]
    start_link(halo)
    start_chip(halo)

    @pl.when(jnp.logical_not(has_up))
    def _():
        ext[:, :, 0:DEPTH, :] = jnp.zeros((2, 2, DEPTH, PROBE), F32)
        wrecv[0] = jnp.zeros((2, DEPTH, PROBE), F32)
        nrecv[0] = jnp.zeros((2, 2, DEPTH, PROBE), F32)

    @pl.when(jnp.logical_not(has_dn))
    def _():
        ext[:, :, last:, :] = jnp.zeros((2, 2, DEPTH, PROBE), F32)
        wrecv[1] = jnp.zeros((2, DEPTH, PROBE), F32)
        nrecv[1] = jnp.zeros((2, 2, DEPTH, PROBE), F32)

    part[:, :, 0:PAD, :] = jnp.zeros((SLOTS, 2, PAD, PROBE), F32)
    part[:, :, PAD + PROBE :, :] = jnp.zeros((SLOTS, 2, PAD, PROBE), F32)
    pw[:, 0:PAD, :] = jnp.zeros((SLOTS, PAD, PROBE), F32)
    pw[:, PAD + PROBE :, :] = jnp.zeros((SLOTS, PAD, PROBE), F32)

    for load in scalars:
        load.wait()
    live = count[0]
    lefts = [cols[0, j] for j in range(SLOTS)]
    tops = [jnp.where(j < live, rows[0, j] + DEPTH, 8 * SIDE) for j in range(SLOTS)]
    lane8 = lax.broadcasted_iota(jnp.int32, (8, PROBE), 1)

    loads[2].wait()
    probe_re, probe_im = prb[0], prb[1]
    power = probe_re * probe_re + probe_im * probe_im
    for j in range(SLOTS):
        pw[j, PAD : PAD + PROBE, :] = pltpu.roll(power, lax.rem(lefts[j], PROBE), 1)

    def placed(read, group, terms):
        left = [jnp.zeros((8, PROBE), F32) for _ in range(terms)]
        right = [jnp.zeros((8, PROBE), F32) for _ in range(terms)]
        for j in range(SLOTS):
            at = jnp.clip(8 * group - tops[j], -PAD, PROBE) + PAD
            inside = lane8 >= lefts[j]
            for c in range(terms):
                value = read(j, c, pl.ds(at, 8))
                left[c] = left[c] + jnp.where(inside, value, 0.0)
                right[c] = right[c] + jnp.where(inside, 0.0, value)
        return left, right

    def place_weights(group, carry):
        left, right = placed(lambda j, c, where: pw[j, where, :], group, 1)
        at = pl.ds(pl.multiple_of(8 * group, 8), 8)
        wsum[0, at, :] = left[0]
        wsum[1, at, :] = right[0]
        return carry

    edge = DEPTH // 8
    whole = (SIDE + 2 * DEPTH) // 8
    lax.fori_loop(0, edge, place_weights, 0, unroll=4)
    lax.fori_loop(whole - edge, whole, place_weights, 0, unroll=4)
    weights = [
        border_pair(
            wsum.at[:, pl.ds(0, DEPTH), :], wrecv.at[1],
            wsum.at[:, pl.ds(last, DEPTH), :], wrecv.at[0],
            b_recv,
        )
    ]
    lax.fori_loop(edge, whole - edge, place_weights, 0, unroll=4)

    loads[3].wait()

    def take_roots(pair, carry):
        for s in range(2):
            root[pair, :, s * PROBE : (s + 1) * PROBE] = jnp.sqrt(itn[2 * pair + s].astype(F32))
        return carry

    lax.fori_loop(0, SLOTS // 2, take_roots, 0)

    def coef(e, k):
        return spec[k, e]

    gram = [[None] * MATERIALS for _ in range(MATERIALS)]
    for k in range(MATERIALS):
        for l in range(k, MATERIALS):
            total = coef(0, k) * coef(0, l)
            for e in range(1, ENERGIES):
                total = total + coef(e, k) * coef(e, l)
            gram[k][l] = gram[l][k] = total
    squares = gram[0][0] + gram[1][1] + gram[2][2]

    loads[4].wait()
    wait_chip(halo)
    wait_link(halo)
    start_link(weights)
    start_chip(weights)

    lane = lax.broadcasted_iota(jnp.int32, (PROBE, PROBE), 1)

    def cut_windows(pair, state):
        exits = []
        for s in range(2):
            j = 2 * pair + s
            top = pl.ds(rows[0, j] + DEPTH, PROBE)
            inside = lane >= lefts[j]
            turn = lax.rem(PROBE - lefts[j], PROBE)
            view = [
                pltpu.roll(jnp.where(inside, ext[c, 0, top, :], ext[c, 1, top, :]), turn, 1) for c in range(2)
            ]
            pr, pi = prb[0], prb[1]
            exits.append(jnp.concatenate([pr * view[0] - pi * view[1], pr * view[1] + pi * view[0]], axis=1))
        state["exit"] = jnp.concatenate(exits, axis=0)

    def transform_rows(pair, state):
        state["x"] = swap_blocks(right_apply(state["exit"], tab[0], tab[1]))

    def transform_columns(pair, state):
        spectrum = left_apply(tab[2], tab[3], state["x"])
        sr, si = spectrum[:PROBE], spectrum[PROBE:]
        factor = root[pair] * lax.rsqrt(sr * sr + si * si + SMOOTH)
        state["x"] = jnp.concatenate([sr * factor, si * factor], axis=0)

    def restore_columns(pair, state):
        state["x"] = swap_blocks(left_apply(tab[0], tab[1], state["x"]))

    def restore_rows(pair, state):
        change = right_apply(state["x"], tab[2], tab[3]) - state["exit"]
        for s in range(2):
            j = 2 * pair + s
            cr = change[s * PROBE : (s + 1) * PROBE, :PROBE]
            ci = change[s * PROBE : (s + 1) * PROBE, PROBE:]
            pr, pi = prb[0], prb[1]
            turn = lax.rem(lefts[j], PROBE)
            part[j, 0, PAD : PAD + PROBE, :] = pltpu.roll(pr * cr + pi * ci, turn, 1)
            part[j, 1, PAD : PAD + PROBE, :] = pltpu.roll(pr * ci - pi * cr, turn, 1)

    states = [{} for _ in range(SLOTS // 2)]
    for stage in (cut_windows, transform_rows, transform_columns, restore_columns, restore_rows):
        for pair in range(SLOTS // 2):
            stage(pair, states[pair])

    def numerators(group):
        return placed(lambda j, c, where: part[j, c, where, :], group, 2)

    def place_parts(group, carry):
        left, right = numerators(group)
        at = pl.ds(pl.multiple_of(8 * group, 8), 8)
        for c in range(2):
            num[c, 0, at, :] = left[c]
            num[c, 1, at, :] = right[c]
        return carry

    def place_edge(side):
        lax.fori_loop(0, edge, lambda g, carry: place_parts(g + side * (whole - edge), carry), 0, unroll=8)

    def place_next(side):
        lax.fori_loop(0, edge, lambda g, carry: place_parts(g + edge + side * (whole - 3 * edge), carry), 0, unroll=8)

    borders = [
        border_pair(
            num.at[:, :, pl.ds(0, DEPTH), :], nrecv.at[1],
            num.at[:, :, pl.ds(last, DEPTH), :], nrecv.at[0],
            b_recv,
        )
    ]
    place_edge(link_side)
    start_link(borders)
    place_edge(chip_side)
    start_chip(borders)

    def renew(group, h, numerator, weight):
        at = pl.ds(pl.multiple_of(8 * group, 8), 8)
        own = pl.ds(pl.multiple_of(8 * group - DEPTH, 8), 8)
        inverse = 1.0 / (weight + DAMPING)
        new = [ext[c, h, at, :] + numerator[c] * inverse for c in range(2)]
        squared = new[0] * new[0] + new[1] * new[1] + SMOOTH
        scale = lax.rsqrt(squared)
        for c in range(2):
            unit[c, own, h * PROBE : (h + 1) * PROBE] = new[c] * scale
        att[own, h * PROBE : (h + 1) * PROBE] = -0.5 * jnp.log(squared)

    def inner_rows(group, carry):
        at = pl.ds(pl.multiple_of(8 * group, 8), 8)
        for h, sums in enumerate(numerators(group)):
            renew(group, h, sums, wsum[h, at, :])
        return carry

    def first_row(f, p):
        start = (DEPTH, chip_side * (SIDE - DEPTH), link_side * (SIDE - DEPTH))[p]
        return pl.multiple_of(start + PIECES[p] * f, 8)

    spots = [sum(PIECES[:p]) for p in range(len(PIECES))]

    def send_pixels(p):
        spot = pl.ds(spots[p], PIECES[p])
        for d in FAR_FIRST:
            remote(
                att.at[pl.ds(first_row(peer(d), p), PIECES[p]), :], gath.at[me, spot, :],
                a_send.at[0], a_recv.at[p], (tile, peer(d)),
            ).start()
        gath[me, spot, :] = att[pl.ds(first_row(me, p), PIECES[p]), :]

    lax.fori_loop(2 * edge, whole - 2 * edge, inner_rows, 0, unroll=8)
    send_pixels(0)
    place_next(chip_side)

    def device(planes, steps):
        return lax.rem(plane + planes, 2) * RING + lax.rem(y + steps + RING, RING)

    def hop(p, i, owner, to):
        at = pl.ds(first_row(owner, p), PIECES[p])
        return remote(maps.at[:, at, :], maps.at[:, at, :], g_send.at[0], g_recv.at[p + 2 if p > 0 else min(i, 2)], (tile, to))

    steps = ((1, 0), (0, 2), (0, 1), (0, -1), (1, 1), (1, -1), (1, 2))

    def hops(p):
        if p > 0:
            return [hop(p, i, me, device(*step)) for i, step in enumerate(steps)]
        return [hop(p, i, me, device(*step)) for i, step in enumerate(steps[:4])] + [
            hop(p, 4, device(1, 0), device(0, 1)),
            hop(p, 5, device(1, 0), device(0, -1)),
            hop(p, 6, device(0, 2), device(1, 0)),
        ]

    ways = [hops(p) for p in range(len(PIECES))]

    def decompose(p):
        block = att.at[pl.ds(0, (ENERGIES - 1) * PIECES[p]), :]
        remote(block, block, a_send.at[0], a_recv.at[p], (tile, peer(1))).wait_recv()
        spot = pl.ds(spots[p], PIECES[p])
        step = 1.0 / jnp.full((PIECES[p], SIDE), squares, F32)
        pulls = []
        for k in range(MATERIALS):
            total = coef(0, k) * gath[0, spot, :]
            for e in range(1, ENERGIES):
                total = total + coef(e, k) * gath[e, spot, :]
            pulls.append(total)
        levels = [jnp.maximum(step * pull, 0.0) for pull in pulls]
        for _ in range(NN_ITERS - 1):
            levels = [
                jnp.maximum(
                    levels[k]
                    - step
                    * (gram[k][0] * levels[0] + gram[k][1] * levels[1] + gram[k][2] * levels[2] - pulls[k]),
                    0.0,
                )
                for k in range(MATERIALS)
            ]
        for k in range(MATERIALS):
            maps[k, pl.ds(first_row(me, p), PIECES[p]), :] = levels[k]
        for i in (1, 0, 2, 3) if p == 0 else (6, 1, 4, 5, 2, 3, 0):
            ways[p][i].start()

    def outer_rows(side):
        base = edge + side * (whole - 3 * edge)

        def rows_of(group, carry):
            row = pl.ds(pl.multiple_of(8 * group, 8), 8)
            at = pl.ds(pl.multiple_of(8 * (group + base), 8), 8)
            for h in range(2):
                sums = [num[c, h, at, :] + nrecv[side, c, h, row, :] for c in range(2)]
                renew(group + base, h, sums, wsum[h, at, :] + wrecv[side, h, row, :])
            return carry

        lax.fori_loop(0, edge, rows_of, 0, unroll=8)

    border_bytes = block_pair(num.at[:, :, pl.ds(0, 3 * DEPTH // 2), :], b_recv)
    wait_chip(border_bytes)
    outer_rows(chip_side)
    send_pixels(1)
    place_next(link_side)

    own_spec = [spec[k, me] for k in range(MATERIALS)]

    def finish(p):
        at = pl.ds(first_row(0, p), ENERGIES * PIECES[p])
        thickness = own_spec[0] * maps[0, at, :] + own_spec[1] * maps[1, at, :] + own_spec[2] * maps[2, at, :]
        fade = jnp.exp(-thickness)
        for c in range(2):
            model[c, at, :] = unit[c, at, :] * fade

    def arrived(p, pieces):
        block = maps.at[:, pl.ds(0, pieces * PIECES[p]), :]
        remote(block, block, g_send.at[0], g_recv.at[p + 2], (tile, peer(1))).wait_recv()

    wait_link(border_bytes)
    outer_rows(link_side)
    send_pixels(2)
    decompose(0)
    decompose(1)
    ways[0][0].wait_recv()
    ways[0][4].start()
    ways[0][5].start()
    decompose(2)
    ways[0][1].wait_recv()
    ways[0][6].start()
    for p in range(len(PIECES)):
        arrived(p, ENERGIES - 3 if p == 0 else ENERGIES - 1)
        finish(p)

    sent_bytes = block_pair(num.at[:, :, pl.ds(0, 5 * DEPTH // 2), :], b_recv)
    start_link(sent_bytes, "wait_send")
    start_chip(sent_bytes, "wait_send")
    block = att.at[pl.ds(0, (ENERGIES - 1) * sum(PIECES)), :]
    remote(block, block, a_send.at[0], a_recv.at[0], (tile, peer(1))).wait_send()
    block = maps.at[:, pl.ds(0, (ENERGIES - 1) * sum(PIECES)), :]
    remote(block, block, g_send.at[0], g_recv.at[0], (tile, peer(1))).wait_send()


def put_out(maps, model, maps_out, model_out, sems):
    copies = [
        pltpu.make_async_copy(maps, maps_out, sems.at[0]),
        pltpu.make_async_copy(model, model_out.at[0], sems.at[1]),
    ]
    for copy in copies:
        copy.start()
    for copy in copies:
        copy.wait()


def stay(*arrays):
    return [pltpu.with_memory_space_constraint(array, pltpu.HBM) for array in arrays]


def body(object_tiles, probe_field, intensity, row_offsets, col_offsets, tile_counts, material_spectra):
    tables = jnp.asarray(dft_tables())
    anywhere = pl.BlockSpec(memory_space=pl.ANY)
    dma = pltpu.SemaphoreType.DMA
    vmem = pl.BlockSpec(memory_space=pltpu.VMEM)
    maps, model = pl.pallas_call(
        kernel,
        out_shape=(
            jax.ShapeDtypeStruct((MATERIALS, SIDE, SIDE), F32),
            jax.ShapeDtypeStruct((2, SIDE, SIDE), F32),
        ),
        in_specs=[anywhere] * 6 + [pl.BlockSpec(memory_space=pltpu.SMEM), anywhere],
        out_specs=(vmem, vmem),
        scratch_shapes=[
            pltpu.VMEM((2, 2, SIDE + 2 * DEPTH, PROBE), F32),
            pltpu.VMEM((2, PROBE, PROBE), F32),
            pltpu.VMEM((SLOTS, PROBE, PROBE), BF16),
            pltpu.VMEM((4, SIDE, SIDE), BF16),
            pltpu.VMEM((SLOTS // 2, PROBE, SIDE), F32),
            pltpu.VMEM((SLOTS, 2, PROBE + 2 * PAD, PROBE), F32),
            pltpu.VMEM((SLOTS, PROBE + 2 * PAD, PROBE), F32),
            pltpu.VMEM((2, SIDE + 2 * DEPTH, PROBE), F32),
            pltpu.VMEM((2, 2, DEPTH, PROBE), F32),
            pltpu.VMEM((2, 2, SIDE + 2 * DEPTH, PROBE), F32),
            pltpu.VMEM((2, 2, 2, DEPTH, PROBE), F32),
            pltpu.VMEM((2, SIDE, SIDE), F32),
            pltpu.VMEM((SIDE, SIDE), F32),
            pltpu.VMEM((ENERGIES, sum(PIECES), SIDE), F32),
            pltpu.SMEM((1, SLOTS), jnp.int32),
            pltpu.SMEM((1, SLOTS), jnp.int32),
            pltpu.SMEM((MATERIALS, ENERGIES), F32),
            dma((8,)), dma((2,)), dma((2,)), dma((2,)), dma((1,)), dma((len(PIECES),)), dma((1,)), dma((len(PIECES) + 2,)),
        ],
        compiler_params=pltpu.CompilerParams(collective_id=0, has_side_effects=True, vmem_limit_bytes=24 * 2**20),
        name="refine",
    )(*stay(object_tiles, probe_field, intensity, tables, row_offsets, col_offsets), tile_counts, *stay(material_spectra.T))
    return pl.pallas_call(
        put_out,
        out_shape=(
            jax.ShapeDtypeStruct((MATERIALS, SIDE, SIDE), F32),
            jax.ShapeDtypeStruct((1, 2, SIDE, SIDE), F32),
        ),
        in_specs=[vmem, vmem],
        out_specs=(anywhere, anywhere),
        scratch_shapes=[dma((2,))],
        compiler_params=pltpu.CompilerParams(vmem_limit_bytes=8 * 2**20),
        name="put_out",
    )(maps, model)


def solution(mesh):
    placed = (
        P("energy", None, "tile", None),
        P("energy", None, None, None),
        P("energy", "tile", None, None, None),
        P("tile", None),
        P("tile", None),
        P("tile"),
        P(),
    )
    return jax.shard_map(
        body,
        mesh=mesh,
        in_specs=placed,
        out_specs=(P(None, "tile", None), P("energy", None, "tile", None)),
        check_vma=False,
    )
```

```python
import jax
import jax.numpy as jnp
import ml_dtypes
import numpy as np
from jax import lax
from jax.experimental import pallas as pl
from jax.experimental.pallas import tpu as pltpu
from jax.sharding import PartitionSpec as P

PROBE = 128
NN_ITERS = 8
SMOOTH = 0.01
DAMPING = 0.5
SIDE = 256
DEPTH = 64
SLOTS = 8
PAD = 8
ENERGIES = 8
RING = 4
PIECES = (16, 8, 8)
FAR_FIRST = (6, 2, 5, 3, 7, 1, 4)
MATERIALS = 3

F32 = jnp.float32
BF16 = jnp.bfloat16
MESH = pl.DeviceIdType.MESH


def dft_tables():
    k = np.arange(PROBE)
    angles = 2.0 * np.pi / PROBE * (np.outer(k, k) % PROBE)
    cos, sin = np.cos(angles) / np.sqrt(PROBE), np.sin(angles) / np.sqrt(PROBE)
    table = np.block([[cos, -sin], [sin, cos]])
    out = []
    for full in (table, table.T):
        high = full.astype(np.float32).astype(ml_dtypes.bfloat16)
        low = (full - high.astype(np.float64)).astype(np.float32).astype(ml_dtypes.bfloat16)
        out += [high, low]
    return np.stack(out)


def halves(x):
    high = x.astype(BF16)
    return high, (x - high.astype(F32)).astype(BF16)


def mul(a, b):
    return jnp.dot(a, b, preferred_element_type=F32)


def right_apply(x, high, low):
    xh, xl = halves(x)
    return mul(xh, high) + mul(xl, high) + mul(xh, low)


def left_apply(high, low, x):
    xh, xl = halves(x)
    return mul(high, xh) + mul(high, xl) + mul(low, xh)


def swap_blocks(x):
    n = PROBE
    top = jnp.concatenate([x[:n, :n], x[n:, :n]], axis=1)
    bottom = jnp.concatenate([x[:n, n:], x[n:, n:]], axis=1)
    return jnp.concatenate([top, bottom], axis=0)


def kernel(
    obj, probe, inten, tables, rows_in, cols_in, count, spec_in,
    maps, model,
    ext, prb, itn, tab, root, part, pw, wsum, wrecv, num, nrecv, unit, att, gath, rows, cols, spec,
    load_sem, b_send, halo_recv, b_recv, a_send, a_recv, g_send, g_recv,
):
    tile = lax.axis_index("tile")
    me = lax.axis_index("energy")
    tiles = lax.axis_size("tile")
    plane, y = me // RING, lax.rem(me, RING)
    has_up, has_dn = tile > 0, tile < tiles - 1
    up, dn = lax.rem(tile + tiles - 1, tiles), lax.rem(tile + 1, tiles)

    def peer(d):
        return lax.rem(me + d, ENERGIES)

    barrier = pltpu.get_barrier_semaphore()

    def greet(where):
        pl.semaphore_signal(barrier, inc=1, device_id=where, device_id_type=MESH)

    @pl.when(has_up)
    def _():
        greet((up, me))

    @pl.when(has_dn)
    def _():
        greet((dn, me))

    for d in range(1, ENERGIES):
        greet((tile, peer(d)))

    loads = [
        pltpu.make_async_copy(
            obj.at[0, :, :, pl.ds(h * PROBE, PROBE)], ext.at[:, h, pl.ds(DEPTH, SIDE), :], load_sem.at[h]
        )
        for h in range(2)
    ] + [
        pltpu.make_async_copy(probe.at[0], prb, load_sem.at[2]),
        pltpu.make_async_copy(inten.at[0, 0], itn, load_sem.at[3]),
        pltpu.make_async_copy(tables, tab, load_sem.at[4]),
    ]
    scalars = [
        pltpu.make_async_copy(rows_in, rows, load_sem.at[5]),
        pltpu.make_async_copy(cols_in, cols, load_sem.at[6]),
        pltpu.make_async_copy(spec_in, spec, load_sem.at[7]),
    ]
    for load in loads[:2] + scalars + loads[2:]:
        load.start()

    greeted = ENERGIES - 1 + has_up.astype(jnp.int32) + has_dn.astype(jnp.int32)
    pl.semaphore_wait(barrier, greeted)

    def remote(src, dst, send, recv, where):
        return pltpu.make_async_remote_copy(
            src_ref=src, dst_ref=dst, send_sem=send, recv_sem=recv, device_id=where, device_id_type=MESH
        )

    def border_pair(src_up, dst_up, src_dn, dst_dn, recv):
        return (
            remote(src_up, dst_up, b_send.at[0], recv.at[0], (up, me)),
            remote(src_dn, dst_dn, b_send.at[1], recv.at[1], (dn, me)),
        )

    def block_pair(block, recv):
        return [border_pair(block, block, block, block, recv)]

    odd = lax.rem(tile, 2) == 1
    even = jnp.logical_not(odd)
    link_up, link_dn = jnp.logical_and(even, has_up), jnp.logical_and(odd, has_dn)
    chip_side = 1 - lax.rem(tile, 2)
    link_side = 1 - chip_side

    def when(condition, action, copies):
        @pl.when(condition)
        def _():
            for copy in copies:
                getattr(copy, action)()

    def start_link(pairs, action="start"):
        when(link_up, action, [to_up for to_up, _ in pairs])
        when(link_dn, action, [to_dn for _, to_dn in pairs])

    def start_chip(pairs, action="start"):
        when(even, action, [to_dn for _, to_dn in pairs])
        when(odd, action, [to_up for to_up, _ in pairs])

    def wait_link(pairs):
        when(link_up, "wait_recv", [to_dn for _, to_dn in pairs])
        when(link_dn, "wait_recv", [to_up for to_up, _ in pairs])

    def wait_chip(pairs):
        when(even, "wait_recv", [to_up for to_up, _ in pairs])
        when(odd, "wait_recv", [to_dn for _, to_dn in pairs])

    last = SIDE + DEPTH
    for load in loads[:2]:
        load.wait()
    halo = [
        border_pair(
            ext.at[:, :, pl.ds(DEPTH, DEPTH), :], ext.at[:, :, pl.ds(last, DEPTH), :],
            ext.at[:, :, pl.ds(SIDE, DEPTH), :], ext.at[:, :, pl.ds(0, DEPTH), :],
            halo_recv,
        )
    ]
    start_link(halo)
    start_chip(halo)

    @pl.when(jnp.logical_not(has_up))
    def _():
        ext[:, :, 0:DEPTH, :] = jnp.zeros((2, 2, DEPTH, PROBE), F32)
        wrecv[0] = jnp.zeros((2, DEPTH, PROBE), F32)
        nrecv[0] = jnp.zeros((2, 2, DEPTH, PROBE), F32)

    @pl.when(jnp.logical_not(has_dn))
    def _():
        ext[:, :, last:, :] = jnp.zeros((2, 2, DEPTH, PROBE), F32)
        wrecv[1] = jnp.zeros((2, DEPTH, PROBE), F32)
        nrecv[1] = jnp.zeros((2, 2, DEPTH, PROBE), F32)

    part[:, :, 0:PAD, :] = jnp.zeros((SLOTS, 2, PAD, PROBE), F32)
    part[:, :, PAD + PROBE :, :] = jnp.zeros((SLOTS, 2, PAD, PROBE), F32)
    pw[:, 0:PAD, :] = jnp.zeros((SLOTS, PAD, PROBE), F32)
    pw[:, PAD + PROBE :, :] = jnp.zeros((SLOTS, PAD, PROBE), F32)

    for load in scalars:
        load.wait()
    live = count[0]
    lefts = [cols[0, j] for j in range(SLOTS)]
    tops = [jnp.where(j < live, rows[0, j] + DEPTH, 8 * SIDE) for j in range(SLOTS)]
    lane8 = lax.broadcasted_iota(jnp.int32, (8, PROBE), 1)

    loads[2].wait()
    probe_re, probe_im = prb[0], prb[1]
    power = probe_re * probe_re + probe_im * probe_im
    for j in range(SLOTS):
        pw[j, PAD : PAD + PROBE, :] = pltpu.roll(power, lax.rem(lefts[j], PROBE), 1)

    def placed(read, group, terms):
        left = [jnp.zeros((8, PROBE), F32) for _ in range(terms)]
        right = [jnp.zeros((8, PROBE), F32) for _ in range(terms)]
        for j in range(SLOTS):
            at = jnp.clip(8 * group - tops[j], -PAD, PROBE) + PAD
            inside = lane8 >= lefts[j]
            for c in range(terms):
                value = read(j, c, pl.ds(at, 8))
                left[c] = left[c] + jnp.where(inside, value, 0.0)
                right[c] = right[c] + jnp.where(inside, 0.0, value)
        return left, right

    def place_weights(group, carry):
        left, right = placed(lambda j, c, where: pw[j, where, :], group, 1)
        at = pl.ds(pl.multiple_of(8 * group, 8), 8)
        wsum[0, at, :] = left[0]
        wsum[1, at, :] = right[0]
        return carry

    edge = DEPTH // 8
    whole = (SIDE + 2 * DEPTH) // 8
    lax.fori_loop(0, edge, place_weights, 0, unroll=4)
    lax.fori_loop(whole - edge, whole, place_weights, 0, unroll=4)
    weights = [
        border_pair(
            wsum.at[:, pl.ds(0, DEPTH), :], wrecv.at[1],
            wsum.at[:, pl.ds(last, DEPTH), :], wrecv.at[0],
            b_recv,
        )
    ]
    lax.fori_loop(edge, whole - edge, place_weights, 0, unroll=4)

    loads[3].wait()

    def take_roots(pair, carry):
        for s in range(2):
            root[pair, :, s * PROBE : (s + 1) * PROBE] = jnp.sqrt(itn[2 * pair + s].astype(F32))
        return carry

    lax.fori_loop(0, SLOTS // 2, take_roots, 0)

    def coef(e, k):
        return spec[k, e]

    gram = [[None] * MATERIALS for _ in range(MATERIALS)]
    for k in range(MATERIALS):
        for l in range(k, MATERIALS):
            total = coef(0, k) * coef(0, l)
            for e in range(1, ENERGIES):
                total = total + coef(e, k) * coef(e, l)
            gram[k][l] = gram[l][k] = total
    squares = gram[0][0] + gram[1][1] + gram[2][2]

    loads[4].wait()
    wait_chip(halo)
    wait_link(halo)
    start_link(weights)
    start_chip(weights)

    lane = lax.broadcasted_iota(jnp.int32, (PROBE, PROBE), 1)

    def cut_windows(pair, state):
        exits = []
        for s in range(2):
            j = 2 * pair + s
            top = pl.ds(rows[0, j] + DEPTH, PROBE)
            inside = lane >= lefts[j]
            turn = lax.rem(PROBE - lefts[j], PROBE)
            view = [
                pltpu.roll(jnp.where(inside, ext[c, 0, top, :], ext[c, 1, top, :]), turn, 1) for c in range(2)
            ]
            pr, pi = prb[0], prb[1]
            exits.append(jnp.concatenate([pr * view[0] - pi * view[1], pr * view[1] + pi * view[0]], axis=1))
        state["exit"] = jnp.concatenate(exits, axis=0)

    def transform_rows(pair, state):
        state["x"] = swap_blocks(right_apply(state["exit"], tab[0], tab[1]))

    def transform_columns(pair, state):
        spectrum = left_apply(tab[2], tab[3], state["x"])
        sr, si = spectrum[:PROBE], spectrum[PROBE:]
        factor = root[pair] * lax.rsqrt(sr * sr + si * si + SMOOTH)
        state["x"] = jnp.concatenate([sr * factor, si * factor], axis=0)

    def restore_columns(pair, state):
        state["x"] = swap_blocks(left_apply(tab[0], tab[1], state["x"]))

    def restore_rows(pair, state):
        change = right_apply(state["x"], tab[2], tab[3]) - state["exit"]
        for s in range(2):
            j = 2 * pair + s
            cr = change[s * PROBE : (s + 1) * PROBE, :PROBE]
            ci = change[s * PROBE : (s + 1) * PROBE, PROBE:]
            pr, pi = prb[0], prb[1]
            turn = lax.rem(lefts[j], PROBE)
            part[j, 0, PAD : PAD + PROBE, :] = pltpu.roll(pr * cr + pi * ci, turn, 1)
            part[j, 1, PAD : PAD + PROBE, :] = pltpu.roll(pr * ci - pi * cr, turn, 1)

    states = [{} for _ in range(SLOTS // 2)]
    for stage in (cut_windows, transform_rows, transform_columns, restore_columns, restore_rows):
        for pair in range(SLOTS // 2):
            stage(pair, states[pair])

    def numerators(group):
        return placed(lambda j, c, where: part[j, c, where, :], group, 2)

    def place_parts(group, carry):
        left, right = numerators(group)
        at = pl.ds(pl.multiple_of(8 * group, 8), 8)
        for c in range(2):
            num[c, 0, at, :] = left[c]
            num[c, 1, at, :] = right[c]
        return carry

    def place_edge(side):
        lax.fori_loop(0, edge, lambda g, carry: place_parts(g + side * (whole - edge), carry), 0, unroll=8)

    def place_next(side):
        lax.fori_loop(0, edge, lambda g, carry: place_parts(g + edge + side * (whole - 3 * edge), carry), 0, unroll=8)

    borders = [
        border_pair(
            num.at[:, :, pl.ds(0, DEPTH), :], nrecv.at[1],
            num.at[:, :, pl.ds(last, DEPTH), :], nrecv.at[0],
            b_recv,
        )
    ]
    place_edge(link_side)
    start_link(borders)
    place_edge(chip_side)
    start_chip(borders)

    def renew(group, h, numerator, weight):
        at = pl.ds(pl.multiple_of(8 * group, 8), 8)
        own = pl.ds(pl.multiple_of(8 * group - DEPTH, 8), 8)
        inverse = 1.0 / (weight + DAMPING)
        new = [ext[c, h, at, :] + numerator[c] * inverse for c in range(2)]
        squared = new[0] * new[0] + new[1] * new[1] + SMOOTH
        scale = lax.rsqrt(squared)
        for c in range(2):
            unit[c, own, h * PROBE : (h + 1) * PROBE] = new[c] * scale
        att[own, h * PROBE : (h + 1) * PROBE] = -0.5 * jnp.log(squared)

    def inner_rows(group, carry):
        at = pl.ds(pl.multiple_of(8 * group, 8), 8)
        for h, sums in enumerate(numerators(group)):
            renew(group, h, sums, wsum[h, at, :])
        return carry

    def first_row(f, p):
        start = (DEPTH, chip_side * (SIDE - DEPTH), link_side * (SIDE - DEPTH))[p]
        return pl.multiple_of(start + PIECES[p] * f, 8)

    spots = [sum(PIECES[:p]) for p in range(len(PIECES))]

    def send_pixels(p):
        spot = pl.ds(spots[p], PIECES[p])
        for d in FAR_FIRST:
            remote(
                att.at[pl.ds(first_row(peer(d), p), PIECES[p]), :], gath.at[me, spot, :],
                a_send.at[0], a_recv.at[p], (tile, peer(d)),
            ).start()
        gath[me, spot, :] = att[pl.ds(first_row(me, p), PIECES[p]), :]

    lax.fori_loop(2 * edge, whole - 2 * edge, inner_rows, 0, unroll=8)
    send_pixels(0)
    place_next(chip_side)

    def device(planes, steps):
        return lax.rem(plane + planes, 2) * RING + lax.rem(y + steps + RING, RING)

    def hop(p, i, owner, to):
        at = pl.ds(first_row(owner, p), PIECES[p])
        return remote(maps.at[:, at, :], maps.at[:, at, :], g_send.at[0], g_recv.at[p + 2 if p > 0 else min(i, 2)], (tile, to))

    steps = ((1, 0), (0, 2), (0, 1), (0, -1), (1, 1), (1, -1), (1, 2))

    def hops(p):
        if p > 0:
            return [hop(p, i, me, device(*step)) for i, step in enumerate(steps)]
        return [hop(p, i, me, device(*step)) for i, step in enumerate(steps[:4])] + [
            hop(p, 4, device(1, 0), device(0, 1)),
            hop(p, 5, device(1, 0), device(0, -1)),
            hop(p, 6, device(0, 2), device(1, 0)),
        ]

    ways = [hops(p) for p in range(len(PIECES))]

    def decompose(p):
        block = att.at[pl.ds(0, (ENERGIES - 1) * PIECES[p]), :]
        remote(block, block, a_send.at[0], a_recv.at[p], (tile, peer(1))).wait_recv()
        spot = pl.ds(spots[p], PIECES[p])
        step = 1.0 / jnp.full((PIECES[p], SIDE), squares, F32)
        pulls = []
        for k in range(MATERIALS):
            total = coef(0, k) * gath[0, spot, :]
            for e in range(1, ENERGIES):
                total = total + coef(e, k) * gath[e, spot, :]
            pulls.append(total)
        keep = [[(1.0 if k == l else 0.0) - step * gram[k][l] for l in range(MATERIALS)] for k in range(MATERIALS)]
        gains = [step * pull for pull in pulls]
        levels = [jnp.maximum(gain, 0.0) for gain in gains]
        for _ in range(NN_ITERS - 1):
            levels = [
                jnp.maximum(
                    (keep[k][0] * levels[0] + keep[k][1] * levels[1]) + (keep[k][2] * levels[2] + gains[k]), 0.0
                )
                for k in range(MATERIALS)
            ]
        for k in range(MATERIALS):
            maps[k, pl.ds(first_row(me, p), PIECES[p]), :] = levels[k]
        for i in (1, 0, 2, 3) if p == 0 else (6, 1, 4, 5, 2, 3, 0):
            ways[p][i].start()

    def outer_rows(side):
        base = edge + side * (whole - 3 * edge)

        def rows_of(group, carry):
            row = pl.ds(pl.multiple_of(8 * group, 8), 8)
            at = pl.ds(pl.multiple_of(8 * (group + base), 8), 8)
            for h in range(2):
                sums = [num[c, h, at, :] + nrecv[side, c, h, row, :] for c in range(2)]
                renew(group + base, h, sums, wsum[h, at, :] + wrecv[side, h, row, :])
            return carry

        lax.fori_loop(0, edge, rows_of, 0, unroll=8)

    border_bytes = block_pair(num.at[:, :, pl.ds(0, 3 * DEPTH // 2), :], b_recv)
    wait_chip(border_bytes)
    outer_rows(chip_side)
    send_pixels(1)
    place_next(link_side)

    own_spec = [spec[k, me] for k in range(MATERIALS)]

    def finish(p):
        at = pl.ds(first_row(0, p), ENERGIES * PIECES[p])
        thickness = own_spec[0] * maps[0, at, :] + own_spec[1] * maps[1, at, :] + own_spec[2] * maps[2, at, :]
        fade = jnp.exp(-thickness)
        for c in range(2):
            model[c, at, :] = unit[c, at, :] * fade

    def arrived(p, pieces):
        block = maps.at[:, pl.ds(0, pieces * PIECES[p]), :]
        remote(block, block, g_send.at[0], g_recv.at[p + 2], (tile, peer(1))).wait_recv()

    wait_link(border_bytes)
    outer_rows(link_side)
    send_pixels(2)
    decompose(0)
    decompose(1)
    ways[0][0].wait_recv()
    ways[0][4].start()
    ways[0][5].start()
    decompose(2)
    ways[0][1].wait_recv()
    ways[0][6].start()
    for p in range(len(PIECES)):
        arrived(p, ENERGIES - 3 if p == 0 else ENERGIES - 1)
        finish(p)

    sent_bytes = block_pair(num.at[:, :, pl.ds(0, 5 * DEPTH // 2), :], b_recv)
    start_link(sent_bytes, "wait_send")
    start_chip(sent_bytes, "wait_send")
    block = att.at[pl.ds(0, (ENERGIES - 1) * sum(PIECES)), :]
    remote(block, block, a_send.at[0], a_recv.at[0], (tile, peer(1))).wait_send()
    block = maps.at[:, pl.ds(0, (ENERGIES - 1) * sum(PIECES)), :]
    remote(block, block, g_send.at[0], g_recv.at[0], (tile, peer(1))).wait_send()


def put_out(maps, model, maps_out, model_out, sems):
    copies = [
        pltpu.make_async_copy(maps, maps_out, sems.at[0]),
        pltpu.make_async_copy(model, model_out.at[0], sems.at[1]),
    ]
    for copy in copies:
        copy.start()
    for copy in copies:
        copy.wait()


def stay(*arrays):
    return [pltpu.with_memory_space_constraint(array, pltpu.HBM) for array in arrays]


def body(object_tiles, probe_field, intensity, row_offsets, col_offsets, tile_counts, material_spectra):
    tables = jnp.asarray(dft_tables())
    anywhere = pl.BlockSpec(memory_space=pl.ANY)
    dma = pltpu.SemaphoreType.DMA
    vmem = pl.BlockSpec(memory_space=pltpu.VMEM)
    maps, model = pl.pallas_call(
        kernel,
        out_shape=(
            jax.ShapeDtypeStruct((MATERIALS, SIDE, SIDE), F32),
            jax.ShapeDtypeStruct((2, SIDE, SIDE), F32),
        ),
        in_specs=[anywhere] * 6 + [pl.BlockSpec(memory_space=pltpu.SMEM), anywhere],
        out_specs=(vmem, vmem),
        scratch_shapes=[
            pltpu.VMEM((2, 2, SIDE + 2 * DEPTH, PROBE), F32),
            pltpu.VMEM((2, PROBE, PROBE), F32),
            pltpu.VMEM((SLOTS, PROBE, PROBE), BF16),
            pltpu.VMEM((4, SIDE, SIDE), BF16),
            pltpu.VMEM((SLOTS // 2, PROBE, SIDE), F32),
            pltpu.VMEM((SLOTS, 2, PROBE + 2 * PAD, PROBE), F32),
            pltpu.VMEM((SLOTS, PROBE + 2 * PAD, PROBE), F32),
            pltpu.VMEM((2, SIDE + 2 * DEPTH, PROBE), F32),
            pltpu.VMEM((2, 2, DEPTH, PROBE), F32),
            pltpu.VMEM((2, 2, SIDE + 2 * DEPTH, PROBE), F32),
            pltpu.VMEM((2, 2, 2, DEPTH, PROBE), F32),
            pltpu.VMEM((2, SIDE, SIDE), F32),
            pltpu.VMEM((SIDE, SIDE), F32),
            pltpu.VMEM((ENERGIES, sum(PIECES), SIDE), F32),
            pltpu.SMEM((1, SLOTS), jnp.int32),
            pltpu.SMEM((1, SLOTS), jnp.int32),
            pltpu.SMEM((MATERIALS, ENERGIES), F32),
            dma((8,)), dma((2,)), dma((2,)), dma((2,)), dma((1,)), dma((len(PIECES),)), dma((1,)), dma((len(PIECES) + 2,)),
        ],
        compiler_params=pltpu.CompilerParams(collective_id=0, has_side_effects=True, vmem_limit_bytes=24 * 2**20),
        name="refine",
    )(*stay(object_tiles, probe_field, intensity, tables, row_offsets, col_offsets), tile_counts, *stay(material_spectra.T))
    return pl.pallas_call(
        put_out,
        out_shape=(
            jax.ShapeDtypeStruct((MATERIALS, SIDE, SIDE), F32),
            jax.ShapeDtypeStruct((1, 2, SIDE, SIDE), F32),
        ),
        in_specs=[vmem, vmem],
        out_specs=(anywhere, anywhere),
        scratch_shapes=[dma((2,))],
        compiler_params=pltpu.CompilerParams(vmem_limit_bytes=8 * 2**20),
        name="put_out",
    )(maps, model)


def solution(mesh):
    placed = (
        P("energy", None, "tile", None),
        P("energy", None, None, None),
        P("energy", "tile", None, None, None),
        P("tile", None),
        P("tile", None),
        P("tile"),
        P(),
    )
    return jax.shard_map(
        body,
        mesh=mesh,
        in_specs=placed,
        out_specs=(P(None, "tile", None), P("energy", None, "tile", None)),
        check_vma=False,
    )
```
